32 devices in a mesh: rep: 4 (over y, x), shard: 8 (over z, core).
Axes of the slice: x: 2, y: 2, z: 4, core: 2. Of those that a mesh axis runs over, the one named last changes fastest.
Arguments:
- tokens: bfloat16 [16, 2048, 768], P('shard', 'rep'), may hold values from -6 to 6
- segment_ids: int32 [16, 2048], P('shard'), may hold values from 0 to 7, never falling along the last dimension, each value on 1 to 1024 neighbouring positions
- cotangent: bfloat16 [16, 2048, 768], P('shard', 'rep'), may hold values from -6 to 6
- query_weight: bfloat16 [768, 768], P('shard'), may hold values from -0.3125 to 0.3125
- key_weight: bfloat16 [768, 768], P('shard'), may hold values from -0.3125 to 0.3125
- value_weight: bfloat16 [768, 768], P('shard'), may hold values from -0.21875 to 0.21875
- output_weight: bfloat16 [768, 768], P('shard'), may hold values from -1.5 to 1.5
- expand_weight: bfloat16 [768, 3072], P('shard'), may hold values from -0.21875 to 0.21875
- reduce_weight: bfloat16 [3072, 768], P('shard'), may hold values from -0.109375 to 0.109375
- query_bias: bfloat16 [768], P('shard'), may hold values from -1.5 to 1.5
- value_bias: bfloat16 [768], P('shard'), may hold values from -0.5 to 0.5
- output_bias: bfloat16 [768], P('shard'), may hold values from -1.5 to 1.5
- expand_bias: bfloat16 [3072], P('shard'), may hold values from -1.5 to 1.5
- reduce_bias: bfloat16 [768], P('shard'), may hold values from -1.5 to 1.5
- first_gain: bfloat16 [768], P('shard'), may hold values from 0.099609375 to 1.8984375
- first_shift: bfloat16 [768], P('shard'), may hold values from -1.5 to 1.5
- second_gain: bfloat16 [768], P('shard'), may hold values from 0.099609375 to 1.8984375
- second_shift: bfloat16 [768], P('shard'), may hold values from -1.5 to 1.5
Outputs:
- layer_output: bfloat16 [16, 2048, 768], P('shard', 'rep')
- tokens_gradient: bfloat16 [16, 2048, 768], P('shard', 'rep')
- query_weight_gradient: float32 [768, 768], P('shard')
- key_weight_gradient: float32 [768, 768], P('shard')
- value_weight_gradient: float32 [768, 768], P('shard')
- output_weight_gradient: float32 [768, 768], P('shard')
- expand_weight_gradient: float32 [768, 3072], P('shard')
- reduce_weight_gradient: float32 [3072, 768], P('shard')
- query_bias_gradient: float32 [768], P('shard')
- value_bias_gradient: float32 [768], P('shard')
- output_bias_gradient: float32 [768], P('shard')
- expand_bias_gradient: float32 [3072], P('shard')
- reduce_bias_gradient: float32 [768], P('shard')
- first_gain_gradient: float32 [768], P('shard')
- first_shift_gradient: float32 [768], P('shard')
- second_gain_gradient: float32 [768], P('shard')
- second_shift_gradient: float32 [768], P('shard')
The draws below stay inside these ranges and needn't reach their ends.
Inputs may be any that keep to these rules, and one draw needn't show every extreme that they name: `segment_ids`: within each sequence the ids never fall; each document holds 1 to 1024 positions and some document of each sequence exactly 1024.
All inputs are finite; a program needn't handle non-finite values.
Results may differ from the reference program's by a relative error of at most 0.017.
The reference program's roundings to bfloat16 on the way count: a program that leaves them out, or rounds other values in their place, can miss the bound.
Values may be sent and summed in bfloat16 or wider, within the bound.
A program may use at most 448 MiB of HBM per device.

```python
import math
import jax
import jax.numpy as jnp
import numpy as np
from jax import lax

D = 768
HEADS = 12
HEAD_DIM = 64
FF = 3072
DOCS = 8
SEQ = 2048
SEQS = 16
MOST = 1024


def raised(values, own_key, source, target, shards_of, factor):
    owner, partner = [(jnp.arange(values.shape[dim]) // (values.shape[dim] // shards_of)).reshape([-1 if axis == dim else 1 for axis in range(values.ndim)]) for dim in (source, target)]
    chosen = jax.random.permutation(own_key, shards_of)[partner]
    strong = (owner == chosen) | (owner == (partner + shards_of // 2) % shards_of)
    return jnp.where(strong, factor * values, values)


def shard_levels(stream_key, extent, cuts, least, top_value):
    level, own = 1.0, jax.random.fold_in(stream_key, 6)
    for axis_at, shards_of in cuts:
        draws = jnp.exp(jax.random.uniform(jax.random.fold_in(own, axis_at), (shards_of,), jnp.float32, least / len(cuts), top_value / len(cuts)))
        level = level * jnp.repeat(draws, extent[axis_at] // shards_of).reshape([-1 if axis == axis_at else 1 for axis in range(len(extent))])
    return level


def length_profile(count, total, limit, lean):
    loads = [(1 << 20) // math.isqrt(standing ** lean) + 1 for standing in range(2, count + 1)]
    surplus, given = total - limit - (count - 1), [1] * (count - 1)
    while surplus > 0:
        free = [i for i in range(count - 1) if given[i] < limit]
        whole, budget = sum([loads[i] for i in free]), surplus
        for i in free:
            extra = min(limit - given[i], max(1, budget * loads[i] // whole), surplus)
            given[i] = given[i] + extra
            surplus = surplus - extra
    return np.array([limit] + given)


def ragged(stream_key, count, total, most, skew):
    if count == 2:
        one = jax.random.randint(stream_key, (), max(1, total - most), min(most, total - 1) + 1)
        return jnp.stack([one, total - one])
    lengths = jnp.asarray(length_profile(count, total, most, skew), jnp.int32)
    twos = (count - 1) // 2
    donor, taker = lengths[1:1 + 2 * twos:2], lengths[2:2 + 2 * twos:2]
    margin = jnp.minimum(donor - 1, most - taker)
    passed = jax.random.randint(jax.random.fold_in(stream_key, 1), (twos,), 0, 1 << 20) % (margin + 1)
    lengths = lengths.at[1:1 + 2 * twos:2].set(donor - passed).at[2:2 + 2 * twos:2].set(taker + passed)
    return lengths[jax.random.permutation(jax.random.fold_in(stream_key, 2), count)]


def normal_values(rng, extent, scale, limit, cuts=(), kind=jnp.bfloat16):
    drawn = jax.random.normal(rng, extent, jnp.float32) * scale
    if len(cuts) > 0:
        drawn = shard_levels(rng, extent, cuts, -0.22, 0.18) * drawn
    return jnp.clip(drawn, min=-limit, max=limit).astype(kind)


def heavy_noise(key, extent, scale, bound, shards, heavy, held_as=jnp.bfloat16):
    array = scale * jax.random.normal(key, extent, jnp.float32)
    if shards:
        array = array * shard_levels(key, extent, shards, -0.22, 0.18)
    return jnp.clip(raised(array, jax.random.fold_in(key, 3), *heavy), -bound, bound).astype(held_as)


def setup_inputs(seed: int = 0) -> dict:
    key_of = jax.random.split(jax.random.key(seed), 19)
    return {
        "tokens": heavy_noise(key_of[0], (SEQS, SEQ, D), 1.0, 6.0, ((0, 8), (1, 4)), (0, 2, 8, 2.0)),
        "segment_ids": jax.vmap(lambda own: jnp.searchsorted(jnp.cumsum(ragged(own, DOCS, SEQ, MOST, 1)), jnp.arange(SEQ), side="right"))(jax.random.split(key_of[1], SEQS)).reshape((SEQS, SEQ)).astype(jnp.int32),
        "cotangent": heavy_noise(key_of[2], (SEQS, SEQ, D), 1.0, 6.0, ((0, 8), (1, 4)), (0, 2, 8, 2.0)),
        "query_weight": normal_values(key_of[3], (D, D), (D // 2) ** -0.5, 0.3125, ((0, 8),)),
        "key_weight": normal_values(key_of[4], (D, D), (D // 2) ** -0.5, 0.3125, ((0, 8),)),
        "value_weight": normal_values(key_of[5], (D, D), D ** -0.5, 0.21875, ((0, 8),)),
        "output_weight": normal_values(key_of[6], (D, D), (max(D // 48, 1)) ** -0.5, 1.5, ((0, 8),)),
        "expand_weight": normal_values(key_of[7], (D, FF), D ** -0.5, 0.21875, ((0, 8),)),
        "reduce_weight": normal_values(key_of[8], (FF, D), FF ** -0.5, 0.109375, ((0, 8),)),
        "query_bias": normal_values(key_of[9], (D,), 0.3, 1.5, ((0, 8),)),
        "value_bias": normal_values(key_of[10], (D,), 0.1, 0.5, ((0, 8),)),
        "output_bias": normal_values(key_of[11], (D,), 0.3, 1.5, ((0, 8),)),
        "expand_bias": normal_values(key_of[12], (FF,), 0.3, 1.5, ((0, 8),)),
        "reduce_bias": normal_values(key_of[13], (D,), 0.3, 1.5, ((0, 8),)),
        "first_gain": jnp.clip(1.0 + 0.18 * jax.random.normal(key_of[14], (D,), jnp.float32), 0.099609375, 1.8984375).astype(jnp.bfloat16),
        "first_shift": normal_values(key_of[15], (D,), 0.3, 1.5, ((0, 8),)),
        "second_gain": jnp.clip(1.0 + 0.18 * jax.random.normal(key_of[16], (D,), jnp.float32), 0.099609375, 1.8984375).astype(jnp.bfloat16),
        "second_shift": normal_values(key_of[17], (D,), 0.3, 1.5, ((0, 8),)),
    }


@jax.custom_vjp
def low(v):
    return lax.optimization_barrier(v.astype(jnp.bfloat16)).astype(jnp.float32)

@jax.custom_vjp
def low_back(v):
    return v

def low_keep(v):
    return (low(v), None)

def low_pass(kept, grad):
    return (grad,)

def back_keep(v):
    return (v, None)

def back_low(kept, grad):
    return (low(grad),)
low.defvjp(low_keep, low_pass)
low_back.defvjp(back_keep, back_low)
masked_value = -1e+30
norm_eps = 1e-05
highest = lax.Precision.HIGHEST

def matmul(left, right):
    return jnp.dot(left, right, precision=highest)

def norm_rows(values, gain, shift):
    centre = values - lax.optimization_barrier(jnp.mean(values, axis=-1, keepdims=True))
    spread = lax.optimization_barrier(jnp.mean(centre * centre, axis=-1, keepdims=True))
    return centre * lax.rsqrt(spread + norm_eps) * gain + shift

def forward(inputs, segment_row, params):
    query_weight, key_weight, value_weight, output_weight, expand_weight, reduce_weight, query_bias, value_bias, output_bias, expand_bias, reduce_bias, first_gain, first_shift, second_gain, second_shift = params
    length = inputs.shape[0]
    queries = low_back(low(matmul(inputs, query_weight) + query_bias))
    keys_all = low_back(low(matmul(inputs, key_weight)))
    values_all = low_back(low(matmul(inputs, value_weight) + value_bias))
    query_heads = queries.reshape(length, HEADS, HEAD_DIM)
    key_heads = keys_all.reshape(length, HEADS, HEAD_DIM)
    value_heads = values_all.reshape(length, HEADS, HEAD_DIM)
    block_rows = min(512, length)
    block_count = length // block_rows

    def attend(pieces):
        query_block, segment_block = pieces
        scores = jnp.einsum('qhd,khd->hqk', query_block, key_heads, precision=highest) * HEAD_DIM ** (-0.5)
        scores = low_back(scores)
        allowed = segment_block[:, None] == segment_row[None, :]
        scores = jnp.where(allowed[None, :, :], scores, masked_value)
        largest = lax.optimization_barrier(jnp.max(scores, axis=-1, keepdims=True))
        exponent = jnp.exp(scores - largest)
        chances = exponent / lax.optimization_barrier(jnp.sum(exponent, axis=-1, keepdims=True))
        return jnp.einsum('hqk,khd->qhd', low(chances), value_heads, precision=highest)
    mixture = lax.map(jax.checkpoint(attend), (query_heads.reshape(block_count, block_rows, HEADS, HEAD_DIM), segment_row.reshape(block_count, block_rows)))
    attended = low(low_back(mixture.reshape(length, D)))
    branch = low_back(matmul(attended, output_weight) + output_bias)
    first = norm_rows(inputs + branch, first_gain, first_shift)
    expanded = low_back(matmul(low(first), expand_weight) + expand_bias)
    reduced = low_back(matmul(low(jax.nn.gelu(expanded)), reduce_weight) + reduce_bias)
    return norm_rows(first + reduced, second_gain, second_shift)

def reference(tokens, segment_ids, cotangent, query_weight, key_weight, value_weight, output_weight, expand_weight, reduce_weight, query_bias, value_bias, output_bias, expand_bias, reduce_bias, first_gain, first_shift, second_gain, second_shift):
    params = (query_weight.astype(jnp.float32), key_weight.astype(jnp.float32), value_weight.astype(jnp.float32), output_weight.astype(jnp.float32), expand_weight.astype(jnp.float32), reduce_weight.astype(jnp.float32), query_bias.astype(jnp.float32), value_bias.astype(jnp.float32), output_bias.astype(jnp.float32), expand_bias.astype(jnp.float32), reduce_bias.astype(jnp.float32), first_gain.astype(jnp.float32), first_shift.astype(jnp.float32), second_gain.astype(jnp.float32), second_shift.astype(jnp.float32))

    def step(totals, item):
        inputs, segment_row, incoming = item

        def apply_layer(values_in, params_in):
            return forward(values_in, segment_row, params_in)
        result, backward = jax.vjp(apply_layer, inputs.astype(jnp.float32), params)
        grad_inputs, grad_params = backward(incoming.astype(jnp.float32))
        totals = tuple((total + change for total, change in zip(totals, grad_params)))
        return (totals, (result.astype(jnp.bfloat16), grad_inputs.astype(jnp.bfloat16)))
    zeros = tuple((jnp.zeros(member.shape, jnp.float32) for member in params))
    totals, (outputs, input_grads) = lax.scan(step, zeros, (tokens, segment_ids, cotangent))
    return (outputs, input_grads, totals[0], totals[1], totals[2], totals[3], totals[4], totals[5], totals[6], totals[7], totals[8], totals[9], totals[10], totals[11], totals[12], totals[13], totals[14])
```

```python
import functools
import math

import jax
import jax.numpy as jnp
from jax import lax
from jax.experimental import pallas as pl
from jax.experimental.pallas import tpu as pltpu
from jax.sharding import PartitionSpec as P

HEAD_DIM = 64
BLOCK = 256
ROWS = 256
MASKED = -1e30
EPS = 1e-05
SCALE = HEAD_DIM**-0.5
SCALE2 = SCALE * math.log2(math.e)
GELU_A = math.sqrt(2.0 / math.pi)
GELU_B = 0.044715
F32 = jnp.float32
BF16 = jnp.bfloat16
VMEM_LIMIT = 60 * 1024 * 1024


def dot(left, right):
    return jnp.dot(left, right, preferred_element_type=F32)


def dot_right(left, right):
    return lax.dot_general(left, right, (((1,), (1,)), ((), ())), preferred_element_type=F32)


def dot_left(left, right):
    return lax.dot_general(left, right, (((0,), (0,)), ((), ())), preferred_element_type=F32)


def params(**more):
    return pltpu.CompilerParams(vmem_limit_bytes=VMEM_LIMIT, **more)


def qkv_kernel(core, own, other, wq, wk, wv, bq, bv, q_out, k_out, v_out):
    per_core = pl.num_programs(0) // 2
    mine = pl.program_id(0) // per_core == core[0]
    rows = jnp.where(mine, own[...], other[...])
    q_out[...] = (dot(rows, wq[...]) + bq[...]).astype(BF16)
    k_out[...] = dot(rows, wk[...]).astype(BF16)
    v_out[...] = (dot(rows, wv[...]) + bv[...]).astype(BF16)


def project(core, own, other, wq, wk, wv, bq, bv):
    rows, width = own.shape
    half = width // 2
    steps = rows // ROWS

    def side(flip):
        def index(i, core):
            first = jnp.where(core[0] == flip, 0, steps)
            return (jnp.clip(i - first, 0, steps - 1), 0)

        return index

    weight = pl.BlockSpec((width, half), lambda i, core: (0, core[0]))
    bias = pl.BlockSpec((1, half), lambda i, core: (0, core[0]))
    result = pl.BlockSpec((ROWS, half), lambda i, core: (i, 0))
    return pl.pallas_call(
        qkv_kernel,
        out_shape=[jax.ShapeDtypeStruct((2 * rows, half), BF16)] * 3,
        grid_spec=pltpu.PrefetchScalarGridSpec(
            num_scalar_prefetch=1,
            grid=(2 * steps,),
            in_specs=[
                pl.BlockSpec((ROWS, width), side(0)),
                pl.BlockSpec((ROWS, width), side(1)),
                weight,
                weight,
                weight,
                bias,
                bias,
            ],
            out_specs=[result] * 3,
        ),
        compiler_params=params(),
        cost_estimate=pl.CostEstimate(
            flops=2 * 2 * rows * width * 3 * half, bytes_accessed=10 << 20, transcendentals=0
        ),
        name="project",
    )(core, own, other, wq, wk, wv, bq, bv)


def halves(pair):
    lane = lax.broadcasted_iota(jnp.int32, pair.shape, 1)
    zero = jnp.zeros_like(pair)
    return jnp.where(lane < HEAD_DIM, pair, zero), jnp.where(lane < HEAD_DIM, zero, pair)


def attend_kernel(low, high, q_ref, k_ref, v_ref, seg_row, seg_col, out, lse, v_turned, top, total, mix):
    rows, width = q_ref.shape
    heads = width // HEAD_DIM
    pairs = heads // 2
    v_turned[...] = v_ref[...].T

    @pl.loop(0, rows // BLOCK)
    def _(qb):
        q_rows = pl.ds(pl.multiple_of(qb * BLOCK, BLOCK), BLOCK)
        seg_q = seg_row[:, q_rows]
        top[...] = jnp.full_like(top, MASKED)
        total[...] = jnp.zeros_like(total)
        mix[...] = jnp.zeros_like(mix)

        def step(kb, carry):
            k_rows = pl.ds(pl.multiple_of(kb * BLOCK, BLOCK), BLOCK)
            same = seg_col[k_rows, :] == seg_q
            for pair in range(pairs):
                cols = pl.ds(pair * 2 * HEAD_DIM, 2 * HEAD_DIM)
                keys = k_ref[k_rows, cols]
                for side, queries in enumerate(halves(q_ref[q_rows, cols])):
                    h = 2 * pair + side
                    head = pl.ds(h * HEAD_DIM, HEAD_DIM)
                    scores = jnp.where(same, dot_right(keys, queries) * SCALE2, MASKED)
                    before = top[pl.ds(h, 1), :]
                    now = jnp.maximum(before, jnp.max(scores, axis=0, keepdims=True))
                    weight = jnp.exp2(scores - now)
                    fade = jnp.exp2(before - now)
                    top[pl.ds(h, 1), :] = now
                    total[pl.ds(h, 1), :] = total[pl.ds(h, 1), :] * fade + jnp.sum(
                        weight, axis=0, keepdims=True
                    )
                    mix[head, :] = mix[head, :] * fade + dot(
                        v_turned[head, k_rows], weight.astype(BF16)
                    )
            return carry

        lax.fori_loop(low[qb], high[qb], step, 0)
        lse[:, q_rows] = top[...] + jnp.log2(total[...])
        for h in range(heads):
            head = pl.ds(h * HEAD_DIM, HEAD_DIM)
            mix[head, :] = mix[head, :] / total[pl.ds(h, 1), :]
        out[q_rows, :] = mix[...].T.astype(BF16)


def attend(low, high, q, k, v, seg_row, seg_col):
    rows, width = q.shape
    heads = width // HEAD_DIM
    whole = lambda shape: pl.BlockSpec(shape, lambda i, *_: (0,) * len(shape))
    return pl.pallas_call(
        attend_kernel,
        out_shape=[
            jax.ShapeDtypeStruct((rows, width), BF16),
            jax.ShapeDtypeStruct((heads, rows), F32),
        ],
        grid_spec=pltpu.PrefetchScalarGridSpec(
            num_scalar_prefetch=2,
            grid=(1,),
            in_specs=[whole((rows, width))] * 3 + [whole((1, rows)), whole((rows, 1))],
            out_specs=[whole((rows, width)), whole((heads, rows))],
            scratch_shapes=[
                pltpu.VMEM((width, rows), BF16),
                pltpu.VMEM((heads, BLOCK), F32),
                pltpu.VMEM((heads, BLOCK), F32),
                pltpu.VMEM((width, BLOCK), F32),
            ],
        ),
        compiler_params=params(),
        cost_estimate=pl.CostEstimate(
            flops=4 * rows * rows * width * 2,
            bytes_accessed=8 << 20,
            transcendentals=rows * rows * heads // 2,
        ),
        name="attend",
    )(low, high, q, k, v, seg_row, seg_col)


def attend_back_kernel(
    core, low, high, q_ref, k_ref, v_ref, out_ref, own, other, lse, seg_row, seg_col,
    dq_out, dk_out, dv_out, grad, k_turned, delta, dq, dk, dv,
):
    rows, width = q_ref.shape
    heads = width // HEAD_DIM
    pairs = heads // 2
    per_core = own.shape[0]
    mine = pl.multiple_of(core[0] * per_core, per_core)
    theirs = pl.multiple_of((1 - core[0]) * per_core, per_core)
    grad[pl.ds(mine, per_core), :] = own[...]
    grad[pl.ds(theirs, per_core), :] = other[...]
    k_turned[...] = k_ref[...].T
    picks = (
        lax.broadcasted_iota(jnp.int32, (8, width), 1) // HEAD_DIM
        == lax.broadcasted_iota(jnp.int32, (8, width), 0)
    ).astype(BF16)

    @pl.loop(0, rows // BLOCK)
    def _(qb):
        q_rows = pl.ds(pl.multiple_of(qb * BLOCK, BLOCK), BLOCK)
        both = grad[q_rows, :].astype(F32) * out_ref[q_rows, :].astype(F32)
        coarse = both.astype(BF16)
        fine = (both - coarse.astype(F32)).astype(BF16)
        delta[:, q_rows] = dot_right(picks, coarse) + dot_right(picks, fine)

    dq[...] = jnp.zeros_like(dq)

    @pl.loop(0, rows // BLOCK)
    def _(kb):
        k_rows = pl.ds(pl.multiple_of(kb * BLOCK, BLOCK), BLOCK)
        seg_k = seg_col[k_rows, :]
        dk[...] = jnp.zeros_like(dk)
        dv[...] = jnp.zeros_like(dv)

        def step(qb, carry):
            q_rows = pl.ds(pl.multiple_of(qb * BLOCK, BLOCK), BLOCK)
            same = seg_k == seg_row[:, q_rows]
            for pair in range(pairs):
                cols = pl.ds(pair * 2 * HEAD_DIM, 2 * HEAD_DIM)
                keys, values = k_ref[k_rows, cols], v_ref[k_rows, cols]
                q_sides, grad_sides = halves(q_ref[q_rows, cols]), halves(grad[q_rows, cols])
                lows, slopes = [], []
                for side in range(2):
                    h = 2 * pair + side
                    scores = jnp.where(same, dot_right(keys, q_sides[side]) * SCALE2, MASKED)
                    probs = jnp.exp2(scores - lse[pl.ds(h, 1), q_rows])
                    grad_probs = dot_right(values, grad_sides[side])
                    slope = (probs * (grad_probs - delta[pl.ds(h, 1), q_rows])).astype(BF16)
                    lows.append(probs.astype(BF16))
                    slopes.append(slope)
                    head = pl.ds(h * HEAD_DIM, HEAD_DIM)
                    dq[head, q_rows] += dot(k_turned[head, k_rows], slope)
                dv[:, cols] += dot(jnp.concatenate(lows, 1), jnp.concatenate(grad_sides, 0))
                dk[:, cols] += dot(jnp.concatenate(slopes, 1), jnp.concatenate(q_sides, 0))
            return carry

        lax.fori_loop(low[kb], high[kb], step, 0)
        dk_out[k_rows, :] = (dk[...] * SCALE).astype(BF16)
        dv_out[k_rows, :] = dv[...].astype(BF16)

    @pl.loop(0, rows // BLOCK)
    def _(qb):
        q_rows = pl.ds(pl.multiple_of(qb * BLOCK, BLOCK), BLOCK)
        dq_out[q_rows, :] = (dq[:, q_rows] * SCALE).T.astype(BF16)


def attend_back(core, low, high, q, k, v, out, own, other, lse, seg_row, seg_col):
    rows, width = q.shape
    heads = width // HEAD_DIM
    whole = lambda shape: pl.BlockSpec(shape, lambda i, *_: (0,) * len(shape))
    return pl.pallas_call(
        attend_back_kernel,
        out_shape=[jax.ShapeDtypeStruct((rows, width), BF16)] * 3,
        grid_spec=pltpu.PrefetchScalarGridSpec(
            num_scalar_prefetch=3,
            grid=(1,),
            in_specs=[whole((rows, width))] * 4
            + [whole((rows // 2, width))] * 2
            + [whole((heads, rows)), whole((1, rows)), whole((rows, 1))],
            out_specs=[whole((rows, width))] * 3,
            scratch_shapes=[
                pltpu.VMEM((rows, width), BF16),
                pltpu.VMEM((width, rows), BF16),
                pltpu.VMEM((8, rows), F32),
                pltpu.VMEM((width, rows), F32),
                pltpu.VMEM((BLOCK, width), F32),
                pltpu.VMEM((BLOCK, width), F32),
            ],
        ),
        compiler_params=params(),
        cost_estimate=pl.CostEstimate(
            flops=10 * rows * rows * width * 2,
            bytes_accessed=16 << 20,
            transcendentals=rows * rows * heads // 2,
        ),
        name="attend_back",
    )(core, low, high, q, k, v, out, own, other, lse, seg_row, seg_col)


def row_mean(values):
    return jnp.mean(values, axis=-1, keepdims=True)


def norm(values):
    centre = values - row_mean(values)
    scale = lax.rsqrt(row_mean(centre * centre) + EPS)
    return centre * scale, scale


def norm_back(normed, scale, gain, grad):
    inner = grad * gain
    return scale * (inner - row_mean(inner) - normed * row_mean(inner * normed))


def column_sum(values):
    return jnp.sum(values.astype(F32), axis=0, keepdims=True)


def rows_kernel(
    core, x_ref, mine, theirs, cot, wo, we, wr, vectors, be,
    out, ga_mine, ga_theirs, residual, act, ge, low_out, gr_out, gb_out, sums, sum_e, slope,
):
    width = x_ref.shape[1]
    half = width // 2
    chunks = we.shape[1] // width
    bo, br = vectors[0:1, :], vectors[1:2, :]
    gain1, shift1, gain2, shift2 = [vectors[n : n + 1, :] for n in range(2, 6)]
    at_mine = pl.multiple_of(core[0] * half, half)
    at_theirs = pl.multiple_of((1 - core[0]) * half, half)
    wo_mine, wo_theirs = wo[pl.ds(at_mine, half), :], wo[pl.ds(at_theirs, half), :]

    @pl.when(pl.program_id(0) == 0)
    def _():
        sums[...] = jnp.zeros_like(sums)
        sum_e[...] = jnp.zeros_like(sum_e)

    branch = dot(mine[...], wo_mine) + dot(theirs[...], wo_theirs) + bo
    normed1, scale1 = norm(x_ref[...].astype(F32) + branch)
    first = normed1 * gain1 + shift1
    first_low = first.astype(BF16)
    low_out[...] = first_low
    reduced = jnp.zeros_like(first)
    for j in range(chunks):
        cols = slice(j * width, (j + 1) * width)
        u = dot(first_low, we[:, cols]) + be[:, cols]
        square = u * u
        curve = jnp.tanh(GELU_A * (u + GELU_B * (square * u)))
        cdf = 0.5 * (1.0 + curve)
        slope[:, cols] = cdf + (0.5 * GELU_A) * u * (1.0 - curve * curve) * (
            1.0 + (3.0 * GELU_B) * square
        )
        activated = (u * cdf).astype(BF16)
        act[:, cols] = activated
        reduced += dot(activated, wr[cols, :])
    normed2, scale2 = norm(first + (reduced + br))
    out[...] = (normed2 * gain2 + shift2).astype(BF16)

    incoming = cot[...].astype(F32)
    grad_second = norm_back(normed2, scale2, gain2, incoming)
    grad_reduced = grad_second.astype(BF16)
    gr_out[...] = grad_reduced
    grad_first = grad_second
    for j in range(chunks):
        cols = slice(j * width, (j + 1) * width)
        grad_expanded = (dot_right(grad_reduced, wr[cols, :]) * slope[:, cols]).astype(BF16)
        ge[:, cols] = grad_expanded
        sum_e[:, cols] += column_sum(grad_expanded)
        grad_first += dot_right(grad_expanded, we[:, cols])
    grad_residual = norm_back(normed1, scale1, gain1, grad_first)
    residual[...] = grad_residual
    grad_branch = grad_residual.astype(BF16)
    gb_out[...] = grad_branch
    ga_mine[...] = dot_right(grad_branch, wo_mine).astype(BF16)
    ga_theirs[...] = dot_right(grad_branch, wo_theirs).astype(BF16)
    sums[0:1, :] += column_sum(grad_branch)
    sums[1:2, :] += column_sum(grad_reduced)
    sums[2:3, :] += column_sum(grad_first * normed1)
    sums[3:4, :] += column_sum(grad_first)
    sums[4:5, :] += column_sum(incoming * normed2)
    sums[5:6, :] += column_sum(incoming)


def row_local(core, x, mine, theirs, cot, wo, we, wr, vectors, be):
    rows, width = x.shape
    half, wide = width // 2, we.shape[1]
    block = lambda cols: pl.BlockSpec((ROWS, cols), lambda i, *_: (i, 0))
    fixed = lambda a: pl.BlockSpec(a.shape, lambda i, *_: (0, 0), pipeline_mode=pl.Buffered(1))
    shape = lambda cols, kind: jax.ShapeDtypeStruct((rows, cols), kind)
    resident = lambda r, cols: pl.BlockSpec((r, cols), lambda i, *_: (0, 0))
    return pl.pallas_call(
        rows_kernel,
        out_shape=[
            shape(width, BF16),
            shape(half, BF16),
            shape(half, BF16),
            shape(width, F32),
            shape(wide, BF16),
            shape(wide, BF16),
            shape(width, BF16),
            shape(width, BF16),
            shape(width, BF16),
            jax.ShapeDtypeStruct((8, width), F32),
            jax.ShapeDtypeStruct((1, wide), F32),
        ],
        grid_spec=pltpu.PrefetchScalarGridSpec(
            num_scalar_prefetch=1,
            grid=(rows // ROWS,),
            in_specs=[
                block(width),
                block(half),
                block(half),
                block(width),
                fixed(wo),
                fixed(we),
                fixed(wr),
                fixed(vectors),
                fixed(be),
            ],
            out_specs=[
                block(width),
                block(half),
                block(half),
                block(width),
                block(wide),
                block(wide),
                block(width),
                block(width),
                block(width),
                resident(8, width),
                resident(1, wide),
            ],
            scratch_shapes=[pltpu.VMEM((ROWS, wide), F32)],
        ),
        compiler_params=params(),
        cost_estimate=pl.CostEstimate(
            flops=2 * 2 * rows * width * (width + 2 * wide),
            bytes_accessed=40 << 20,
            transcendentals=rows * wide,
        ),
        name="row_local",
    )(core, x, mine, theirs, cot, wo, we, wr, vectors, be)


def weight_grad_kernel(left, right, out):
    out[...] = dot_left(left[...], right[...]).astype(out.dtype)


def weight_grad(left, right, kind):
    rows, m = left.shape
    n = right.shape[1]
    tm, tn = min(m, 768), min(n, 768)
    return pl.pallas_call(
        weight_grad_kernel,
        out_shape=jax.ShapeDtypeStruct((m, n), kind),
        grid=(m // tm, n // tn),
        in_specs=[
            pl.BlockSpec((rows, tm), lambda i, j: (0, i)),
            pl.BlockSpec((rows, tn), lambda i, j: (0, j)),
        ],
        out_specs=pl.BlockSpec((tm, tn), lambda i, j: (i, j)),
        compiler_params=params(),
        cost_estimate=pl.CostEstimate(
            flops=2 * rows * m * n, bytes_accessed=16 << 20, transcendentals=0
        ),
        name="weight_grad",
    )(left, right)


def input_grad_kernel(core, own, other, d_ref, w_ref, dw, sums, dx_own, dx_other):
    part = pl.program_id(0)
    rows = own.shape[0]
    mine = pl.multiple_of(core[0] * rows, rows)
    theirs = pl.multiple_of((1 - core[0]) * rows, rows)
    d_own, d_other = d_ref[0, pl.ds(mine, rows), :], d_ref[0, pl.ds(theirs, rows), :]
    dw[0] = (dot_left(own[...], d_own) + dot_left(other[...], d_other)).astype(dw.dtype)
    sums[0] = jnp.broadcast_to(column_sum(d_own) + column_sum(d_other), sums.shape[1:])
    to_own, to_other = dot_right(d_own, w_ref[0]), dot_right(d_other, w_ref[0])

    @pl.when(part == 0)
    def _():
        dx_own[...] = to_own
        dx_other[...] = to_other

    @pl.when(part > 0)
    def _():
        dx_own[...] += to_own
        dx_other[...] += to_other


def input_grad(core, own, other, grads, weights, kind):
    rows, width = own.shape
    half = width // 2
    whole = lambda shape: pl.BlockSpec(shape, lambda i, *_: (0,) * len(shape))
    return pl.pallas_call(
        input_grad_kernel,
        out_shape=[
            jax.ShapeDtypeStruct((3, width, half), kind),
            jax.ShapeDtypeStruct((3, 8, half), F32),
            jax.ShapeDtypeStruct((rows, width), F32),
            jax.ShapeDtypeStruct((rows, width), F32),
        ],
        grid_spec=pltpu.PrefetchScalarGridSpec(
            num_scalar_prefetch=1,
            grid=(3,),
            in_specs=[
                whole((rows, width)),
                whole((rows, width)),
                pl.BlockSpec((1, 2 * rows, half), lambda i, core: (i, 0, 0)),
                pl.BlockSpec((1, width, half), lambda i, core: (i, 0, core[0])),
            ],
            out_specs=[
                pl.BlockSpec((1, width, half), lambda i, core: (i, 0, 0)),
                pl.BlockSpec((1, 8, half), lambda i, core: (i, 0, 0)),
                whole((rows, width)),
                whole((rows, width)),
            ],
        ),
        compiler_params=params(),
        cost_estimate=pl.CostEstimate(
            flops=2 * 2 * 2 * rows * width * 3 * half, bytes_accessed=20 << 20, transcendentals=0
        ),
        name="input_grad",
    )(core, own, other, grads, weights)


def local(tokens, segment_ids, cotangent, *shards):
    rep_size, shard_size = lax.axis_size("rep"), lax.axis_size("shard")
    rep, shard = lax.axis_index("rep"), lax.axis_index("shard")
    core = shard % 2
    core_arg = core.reshape(1).astype(jnp.int32)
    width = tokens.shape[2]
    half = width // 2
    both = ("rep", "shard")

    def flat(r, s):
        return r * shard_size + s

    def route(k, back=False):
        pairs = []
        for r in range(rep_size):
            for s in range(shard_size):
                there = (flat(r, s), flat(2 * (s % 2) + (r + k) % 2, s - s % 2 + r // 2))
                pairs.append(there[::-1] if back else there)
        return pairs

    swap_pairs = [(flat(r, s), flat(r, s ^ 1)) for r in range(rep_size) for s in range(shard_size)]

    def swap(array):
        return lax.ppermute(array, both, swap_pairs)

    odd = rep % 2

    def to_sequences(array):
        a, b = array[0], array[1]
        even_part = lax.ppermute(jnp.where(odd == 0, a, b), both, route(0))
        odd_part = lax.ppermute(jnp.where(odd == 0, b, a), both, route(1))
        return jnp.concatenate(
            [jnp.where(odd == 0, even_part, odd_part), jnp.where(odd == 0, odd_part, even_part)]
        )

    def from_sequences(array):
        rows = array.shape[0] // 2
        a, b = array[:rows], array[rows:]
        even_part = lax.ppermute(jnp.where(odd == 0, a, b), both, route(0, True))
        odd_part = lax.ppermute(jnp.where(odd == 0, b, a), both, route(1, True))
        return jnp.stack(
            [jnp.where(odd == 0, even_part, odd_part), jnp.where(odd == 0, odd_part, even_part)]
        )

    matrices = [lax.all_gather(m, "shard", axis=0, tiled=True) for m in shards[:6]]
    wq, wk, wv, wo, we, wr = matrices
    small = jnp.concatenate(shards[6:])
    small = lax.all_gather(small[None], "shard", axis=0, tiled=True)
    vectors, at = [], 0
    for member in shards[6:]:
        n = member.shape[0]
        vectors.append(small[:, at : at + n].reshape(1, n * shard_size).astype(F32))
        at += n
    bq, bv, bo, be, br, gain1, shift1, gain2, shift2 = vectors

    own = to_sequences(tokens)
    cot = to_sequences(cotangent)
    other = swap(own)
    swapped_ids = swap(segment_ids)
    ids = jnp.where(rep // 2 == core, segment_ids, swapped_ids)
    segments = lax.dynamic_index_in_dim(ids, odd, 0, keepdims=False)
    blocks = segments.reshape(-1, BLOCK)
    begin = jnp.sum((segments[None, :] < blocks[:, :1]).astype(jnp.int32), axis=1)
    end = jnp.sum((segments[None, :] <= blocks[:, -1:]).astype(jnp.int32), axis=1)
    low, high = begin // BLOCK, (end + BLOCK - 1) // BLOCK
    seg_row, seg_col = segments[None, :], segments[:, None]

    q, k, v = project(core_arg, own, other, wq, wk, wv, bq, bv)
    attended, lse = attend(low, high, q, k, v, seg_row, seg_col)
    rows = own.shape[0]
    mine = lax.dynamic_slice_in_dim(attended, core * rows, rows)
    theirs = swap(lax.dynamic_slice_in_dim(attended, (1 - core) * rows, rows))
    table = jnp.concatenate([bo, br, gain1, shift1, gain2, shift2, bo, bo])
    out, ga_mine, ga_theirs, residual, act, ge, first_low, gr, gb, sums, sum_e = row_local(
        core_arg, own, mine, theirs, cot, wo, we, wr, table, be
    )
    ga_other = swap(ga_theirs)
    kind = F32
    dwr = weight_grad(act, gr, kind)
    dwe = weight_grad(first_low, ge, kind)
    dwo_mine, dwo_theirs = weight_grad(mine, gb, kind), weight_grad(theirs, gb, kind)
    dq, dk, dv = attend_back(
        core_arg, low, high, q, k, v, attended, ga_mine, ga_other, lse, seg_row, seg_col
    )
    dw, sum_qkv, dx_own, dx_other = input_grad(
        core_arg, own, other, jnp.stack([dq, dk, dv]), jnp.stack([wq, wk, wv]), kind
    )
    dx = (residual + dx_own + swap(dx_other.astype(BF16)).astype(F32)).astype(BF16)

    def place(part, dim):
        zero = jnp.zeros_like(part)
        return jnp.where(
            core == 0,
            jnp.concatenate([part, zero], axis=dim),
            jnp.concatenate([zero, part], axis=dim),
        )

    dwo = jnp.where(
        core == 0,
        jnp.concatenate([dwo_mine, dwo_theirs]),
        jnp.concatenate([dwo_theirs, dwo_mine]),
    )
    totals = (
        place(dw[0], 1),
        place(dw[1], 1),
        place(dw[2], 1),
        dwo,
        dwe,
        dwr,
        place(sum_qkv[0, 0], 0),
        place(sum_qkv[2, 0], 0),
        sums[0],
        sum_e[0],
        sums[1],
        sums[2],
        sums[3],
        sums[4],
        sums[5],
    )
    summed = lax.psum_scatter(totals, "shard", scatter_dimension=0, tiled=True)
    final = [part.astype(F32) for part in lax.psum([p.astype(BF16) for p in summed], "rep")]
    return (from_sequences(out), from_sequences(dx)) + tuple(final)


def solution(mesh):
    row = P("shard", "rep", None)
    in_specs = (row, P("shard", None), row) + (P("shard", None),) * 6 + (P("shard"),) * 9
    out_specs = (row, row) + (P("shard", None),) * 6 + (P("shard"),) * 9
    return jax.shard_map(local, mesh=mesh, in_specs=in_specs, out_specs=out_specs, check_vma=False)
```

```python
import functools
import math

import jax
import jax.numpy as jnp
from jax import lax
from jax.experimental import pallas as pl
from jax.experimental.pallas import tpu as pltpu
from jax.sharding import PartitionSpec as P

HEAD_DIM = 64
BLOCK = 256
KEYS = 512
PREPARE = 512
DOCS = 8
ROWS = 256
MASKED = -1e30
EPS = 1e-05
UNITS = 8
EXTRA = 8
SCALE = HEAD_DIM**-0.5
SCALE2 = SCALE * math.log2(math.e)
GELU_A = math.sqrt(2.0 / math.pi)
GELU_B = 0.044715
F32 = jnp.float32
BF16 = jnp.bfloat16
VMEM_LIMIT = 60 * 1024 * 1024


def dot(left, right):
    return jnp.dot(left, right, preferred_element_type=F32)


def dot_right(left, right):
    return lax.dot_general(left, right, (((1,), (1,)), ((), ())), preferred_element_type=F32)


def dot_left(left, right):
    return lax.dot_general(left, right, (((0,), (0,)), ((), ())), preferred_element_type=F32)


def params(**more):
    return pltpu.CompilerParams(vmem_limit_bytes=VMEM_LIMIT, **more)


def stacked(ref):
    return ref[...].reshape(-1, ref.shape[-1])


def gather_kernel(
    nz, square, wide, square_all, wide_all,
    z_send, z_recv, p_send, p_recv, c_send, c_recv, own_send, own_recv, copied,
):
    r, s = lax.axis_index("rep"), lax.axis_index("shard")
    z = s // 2
    twin = (r, s ^ 1)
    barrier = pltpu.get_barrier_semaphore()

    def greet(device):
        pl.semaphore_signal(barrier, 1, device_id=device, device_id_type=pl.DeviceIdType.MESH)

    greet(twin)
    for k in (1, 2, 3):
        greet((r ^ k, s))
    for step in (1, -1):

        @pl.when((z + step >= 0) & (z + step < nz))
        def _(step=step):
            greet((r, s + 2 * step))

    pl.semaphore_wait(barrier, 4 + jnp.where(z > 0, 1, 0) + jnp.where(z < nz - 1, 1, 0))

    def copy(source, target, sent, got, device):
        return pltpu.make_async_remote_copy(
            source, target, sent, got, device_id=device, device_id_type=pl.DeviceIdType.MESH
        )

    kept = [
        pltpu.make_async_copy(square, square_all.at[s], copied.at[0]),
        pltpu.make_async_copy(wide, wide_all.at[s], copied.at[1]),
    ]
    own = [
        copy(square, square_all.at[s], own_send.at[0], own_recv.at[0], twin),
        copy(wide, wide_all.at[s], own_send.at[1], own_recv.at[1], twin),
    ]

    def onward(n, d, part):
        step = 1 - 2 * n
        at = s - 2 * step * d
        if part == 0:
            source = square if d == 0 else square_all.at[at]
            target = square_all.at[at]
        else:
            source = wide.at[r] if d == 0 else wide_all.at[at, r]
            target = wide_all.at[at, r]
        return copy(source, target, z_send.at[n, d, part], z_recv.at[n, d, part], (r, s + 2 * step))

    def sideways(n, d, k):
        at = s - 2 * (1 - 2 * n) * d
        part = wide_all.at[at, r]
        return copy(part, part, p_send.at[n, d - 1, k - 1], p_recv.at[n, d - 1, k - 1], (r ^ k, s))

    def across(n, d, k):
        at = s - 2 * (1 - 2 * n) * d
        part = square_all.at[at] if k == 4 else wide_all.at[at, r ^ k]
        return copy(part, part, c_send.at[n, d - 1, k], c_recv.at[n, d - 1, k], twin)

    def has(n, d):
        at = z - (1 - 2 * n) * d
        return (at >= 0) & (at < nz)

    def goes(n):
        at = z + 1 - 2 * n
        return (at >= 0) & (at < nz)

    for n in (0, 1):

        @pl.when(goes(n))
        def _(n=n):
            onward(n, 0, 1).start()
            onward(n, 0, 0).start()

    for c in own + kept:
        c.start()
    for d in range(1, nz):
        for n in (0, 1):

            @pl.when(has(n, d))
            def _(n=n, d=d):
                onward(n, d - 1, 1).wait_recv()
                if d < nz - 1:

                    @pl.when(goes(n))
                    def _():
                        onward(n, d, 1).start()

                for k in (1, 2, 3):
                    sideways(n, d, k).start()
                across(n, d, 0).start()
                onward(n, d - 1, 0).wait_recv()
                if d < nz - 1:

                    @pl.when(goes(n))
                    def _():
                        onward(n, d, 0).start()

                across(n, d, 4).start()

    for d in range(1, nz):
        for n in (0, 1):

            @pl.when(has(n, d))
            def _(n=n, d=d):
                for k in (1, 2, 3):
                    sideways(n, d, k).wait_recv()
                    across(n, d, k).start()

    for c in own + kept:
        c.wait()
    for n in (0, 1):

        @pl.when(goes(n))
        def _(n=n):
            onward(n, 0, 1).wait_send()
            onward(n, 0, 0).wait_send()

    for d in range(1, nz):
        for n in (0, 1):

            @pl.when(has(n, d))
            def _(n=n, d=d):
                for k in (1, 2, 3):
                    sideways(n, d, k).wait_send()
                for k in range(5):
                    across(n, d, k).wait()
                if d < nz - 1:

                    @pl.when(goes(n))
                    def _():
                        onward(n, d, 1).wait_send()
                        onward(n, d, 0).wait_send()


def gather_weights(square, wide, nz):
    anywhere = pl.BlockSpec(memory_space=pl.ANY)
    sems = lambda *shape: pltpu.SemaphoreType.DMA(shape)
    return pl.pallas_call(
        functools.partial(gather_kernel, nz),
        out_shape=[
            jax.ShapeDtypeStruct((2 * nz,) + square.shape, BF16),
            jax.ShapeDtypeStruct((2 * nz,) + wide.shape, BF16),
        ],
        in_specs=[anywhere] * 2,
        out_specs=[anywhere] * 2,
        scratch_shapes=[
            sems(2, nz - 1, 2),
            sems(2, nz - 1, 2),
            sems(2, nz - 1, 3),
            sems(2, nz - 1, 3),
            sems(2, nz - 1, 5),
            sems(2, nz - 1, 5),
            sems(2),
            sems(2),
            sems(2),
        ],
        compiler_params=params(collective_id=0, has_side_effects=True),
        cost_estimate=pl.CostEstimate(flops=0, bytes_accessed=150 << 20, transcendentals=0),
        name="gather_weights",
    )(square, wide)


def qkv_kernel(core, own, other, wq, wk, wv, bq, bv, q_out, k_out, v_out):
    per_core = pl.num_programs(0) // 2
    mine = pl.program_id(0) // per_core == core[0]
    rows = jnp.where(mine, own[...], other[...])
    q_out[...] = (dot(rows, stacked(wq)) + bq[...]).astype(BF16)
    k_out[...] = dot(rows, stacked(wk)).astype(BF16)
    v_out[...] = (dot(rows, stacked(wv)) + bv[...]).astype(BF16)


def project(core, own, other, square, bq, bv):
    rows, width = own.shape
    half = width // 2
    steps = rows // ROWS

    def side(flip):
        def index(i, core):
            first = jnp.where(core[0] == flip, 0, steps)
            return (jnp.clip(i - first, 0, steps - 1), 0)

        return index

    weight = lambda m: pl.BlockSpec(
        (UNITS, width // UNITS, half), lambda i, core: (0, m, core[0])
    )
    bias = pl.BlockSpec((1, half), lambda i, core: (0, core[0]))
    result = pl.BlockSpec((ROWS, half), lambda i, core: (i, 0))
    return pl.pallas_call(
        qkv_kernel,
        out_shape=[jax.ShapeDtypeStruct((2 * rows, half), BF16)] * 3,
        grid_spec=pltpu.PrefetchScalarGridSpec(
            num_scalar_prefetch=1,
            grid=(2 * steps,),
            in_specs=[
                pl.BlockSpec((ROWS, width), side(0)),
                pl.BlockSpec((ROWS, width), side(1)),
                weight(0),
                weight(1),
                weight(2),
                bias,
                bias,
            ],
            out_specs=[result] * 3,
        ),
        compiler_params=params(),
        cost_estimate=pl.CostEstimate(
            flops=2 * 2 * rows * width * 3 * half, bytes_accessed=10 << 20, transcendentals=0
        ),
        name="project",
    )(core, own, other, square, square, square, bq, bv)


def halves(pair):
    lane = lax.broadcasted_iota(jnp.int32, pair.shape, 1)
    zero = jnp.zeros_like(pair)
    return jnp.where(lane < HEAD_DIM, pair, zero), jnp.where(lane < HEAD_DIM, zero, pair)


def rows_at(n, size):
    return pl.ds(pl.multiple_of(n * size, size), size)


def widen(pair, extra):
    lane = lax.broadcasted_iota(jnp.int32, pair.shape, 1)
    return jnp.where(lane < HEAD_DIM, pair, extra[0]), jnp.where(lane < HEAD_DIM, extra[1], pair)


def same_document(ids, extra_lanes):
    slot = lax.broadcasted_iota(jnp.int32, (ids.shape[0], 2 * HEAD_DIM), 1) % HEAD_DIM
    hit = slot == ids
    for_keys = jnp.where(
        (slot < DOCS) & ~hit,
        MASKED,
        jnp.where((slot >= DOCS) & (slot < DOCS + extra_lanes), 1.0, 0.0),
    )
    return jnp.where(hit, 1.0, 0.0), for_keys.astype(BF16)


def attend_kernel(low, high, q_ref, k_ref, v_ref, seg_col, out, lse, qx, kx, v_turned, top, mix, kept):
    rows, width = q_ref.shape
    heads = width // HEAD_DIM
    pairs = heads // 2
    for at in range(0, rows, PREPARE):
        part = pl.ds(at, PREPARE)
        for_queries, for_keys = same_document(seg_col[part, :], 0)
        for_queries = for_queries.astype(BF16)
        for pair in range(pairs):
            cols = pl.ds(pair * 2 * HEAD_DIM, 2 * HEAD_DIM)
            both = slice(2 * pair, 2 * pair + 2)
            qx[both, part, :] = jnp.stack(widen(q_ref[part, cols], (for_queries, for_queries)))
            kx[both, part, :] = jnp.stack(widen(k_ref[part, cols], (for_keys, for_keys)))
            v_turned[both, :HEAD_DIM, part] = v_ref[part, cols].T.reshape(2, HEAD_DIM, PREPARE)
    v_turned[:, HEAD_DIM:, :] = jnp.ones_like(v_turned[:, HEAD_DIM:, :])

    @pl.loop(0, rows // BLOCK)
    def _(qb):
        q_rows = rows_at(qb, BLOCK)
        top[...] = jnp.full_like(top, MASKED)
        mix[...] = jnp.zeros_like(mix)

        def score(kb, carry):
            k_rows = rows_at(kb, KEYS)
            for h in range(heads):
                scores = dot_right(kx[h, k_rows, :], qx[h, q_rows, :])
                kept[h, k_rows, :] = scores
                top[h] = jnp.maximum(top[h], jnp.max(scores.reshape(KEYS // 8, 8, BLOCK), axis=0))
            return carry

        lax.fori_loop(low[qb], high[qb], score, 0)
        tops = [jnp.max(top[h], axis=0, keepdims=True) * SCALE2 for h in range(heads)]

        def weigh(kb, carry):
            k_rows = rows_at(kb, KEYS)
            for h in range(heads):
                weight = jnp.exp2(kept[h, k_rows, :] * SCALE2 - tops[h]).astype(BF16)
                mix[h] += dot(v_turned[h, :, k_rows], weight)
            return carry

        lax.fori_loop(low[qb], high[qb], weigh, 0)
        for h in range(heads):
            total = mix[h, HEAD_DIM : HEAD_DIM + 1, :]
            lse[pl.ds(h, 1), q_rows] = tops[h] + jnp.log2(total)
            mix[h, :HEAD_DIM, :] = mix[h, :HEAD_DIM, :] / total
        for pair in range(pairs):
            both = mix[2 * pair : 2 * pair + 2, :HEAD_DIM, :].reshape(2 * HEAD_DIM, BLOCK)
            out[q_rows, pl.ds(pair * 2 * HEAD_DIM, 2 * HEAD_DIM)] = both.T.astype(BF16)


def spans(begin, end, size):
    return begin // size, (end + size - 1) // size


def attend(begin, end, q, k, v, seg_col):
    rows, width = q.shape
    heads = width // HEAD_DIM
    whole = lambda shape: pl.BlockSpec(shape, lambda i, *_: (0,) * len(shape))
    wide = pltpu.VMEM((heads, rows, 2 * HEAD_DIM), BF16)
    return pl.pallas_call(
        attend_kernel,
        out_shape=[
            jax.ShapeDtypeStruct((rows, width), BF16),
            jax.ShapeDtypeStruct((heads, rows), F32),
        ],
        grid_spec=pltpu.PrefetchScalarGridSpec(
            num_scalar_prefetch=2,
            grid=(1,),
            in_specs=[whole((rows, width))] * 3 + [whole((rows, 1))],
            out_specs=[whole((rows, width)), whole((heads, rows))],
            scratch_shapes=[
                wide,
                wide,
                pltpu.VMEM((heads, HEAD_DIM + 16, rows), BF16),
                pltpu.VMEM((heads, 8, BLOCK), F32),
                pltpu.VMEM((heads, HEAD_DIM + 16, BLOCK), F32),
                pltpu.VMEM((heads, rows, BLOCK), F32),
            ],
        ),
        compiler_params=params(),
        cost_estimate=pl.CostEstimate(
            flops=4 * rows * rows * width,
            bytes_accessed=8 << 20,
            transcendentals=rows * rows * heads // 2,
        ),
        name="attend",
    )(*spans(begin, end, KEYS), q, k, v, seg_col)


def three_parts(values):
    first = values.astype(BF16)
    rest = values - first.astype(F32)
    second = rest.astype(BF16)
    return first, second, (rest - second.astype(F32)).astype(BF16)


def attend_back_kernel(
    core, low, high, q_ref, k_ref, v_ref, out_ref, own, other, lse, seg_col,
    dq_out, dk_out, dv_out, grad, qx, kx, vx, gx, dq, dk, dv, weights, slopes,
):
    rows, width = q_ref.shape
    heads = width // HEAD_DIM
    pairs = heads // 2
    lanes = 2 * HEAD_DIM
    per_core = own.shape[0]
    grad[rows_at(core[0], per_core), :] = own[...]
    grad[rows_at(1 - core[0], per_core), :] = other[...]
    source = lax.broadcasted_iota(jnp.int32, (24, heads * lanes), 0)
    lane = lax.broadcasted_iota(jnp.int32, (24, heads * lanes), 1)
    place = jnp.where(
        (source % 8 == lane // lanes)
        & (lane % HEAD_DIM == DOCS + source // 8)
        & ((lane % lanes) // HEAD_DIM != (lane // lanes) % 2),
        1.0,
        0.0,
    ).astype(BF16)
    picks = jnp.where(
        lax.broadcasted_iota(jnp.int32, (width, 8), 0) // HEAD_DIM
        == lax.broadcasted_iota(jnp.int32, (width, 8), 1),
        1.0,
        0.0,
    ).astype(BF16)
    for at in range(0, rows, PREPARE):
        part = pl.ds(at, PREPARE)
        for_queries, for_keys = same_document(seg_col[part, :], 3)
        ones = jnp.where(for_keys == 1.0, for_keys, jnp.zeros_like(for_keys))
        level = jnp.concatenate(
            [lse[:, part] * (-1.0 / SCALE2), jnp.zeros((8 - heads, PREPARE), F32)]
        )
        levels = dot_left(jnp.concatenate(three_parts(level)), place)
        both = grad[part, :].astype(F32) * out_ref[part, :].astype(F32)
        coarse = both.astype(BF16)
        fine = (both - coarse.astype(F32)).astype(BF16)
        delta = dot(coarse, picks) + dot(fine, picks)
        deltas = dot(jnp.concatenate(three_parts(-delta), 1), place).astype(BF16)
        for pair in range(pairs):
            cols = pl.ds(pair * lanes, lanes)
            sides = slice(2 * pair, 2 * pair + 2)
            one, two = [slice((2 * pair + e) * lanes, (2 * pair + e + 1) * lanes) for e in (0, 1)]
            marks = [(for_queries + levels[:, side]).astype(BF16) for side in (one, two)]
            qx[sides, part, :] = jnp.stack(widen(q_ref[part, cols], marks))
            kx[sides, part, :] = jnp.stack(widen(k_ref[part, cols], (for_keys, for_keys)))
            vx[sides, part, :] = jnp.stack(widen(v_ref[part, cols], (ones, ones)))
            gx[sides, part, :] = jnp.stack(widen(grad[part, cols], (deltas[:, one], deltas[:, two])))

    dq[...] = jnp.zeros_like(dq)

    @pl.loop(0, rows // BLOCK)
    def _(kb):
        k_rows = rows_at(kb, BLOCK)
        dk[...] = jnp.zeros_like(dk)
        dv[...] = jnp.zeros_like(dv)

        def step(qb, carry):
            q_rows = rows_at(qb, BLOCK)
            for h in range(heads):
                probs = jnp.exp2(dot_right(kx[h, k_rows, :], qx[h, q_rows, :]) * SCALE2)
                weights[h] = probs.astype(BF16)
                centred = dot_right(vx[h, k_rows, :], gx[h, q_rows, :])
                slopes[h] = (probs * centred).astype(BF16)
            for pair in range(pairs):
                cols = pl.ds(pair * lanes, lanes)
                slope = [slopes[2 * pair], slopes[2 * pair + 1]]
                weight = [weights[2 * pair], weights[2 * pair + 1]]
                dq[q_rows, cols] += dot_left(
                    jnp.concatenate(slope, 0), jnp.concatenate(halves(k_ref[k_rows, cols]), 0)
                )
                dk[:, cols] += dot(
                    jnp.concatenate(slope, 1), jnp.concatenate(halves(q_ref[q_rows, cols]), 0)
                )
                dv[:, cols] += dot(
                    jnp.concatenate(weight, 1), jnp.concatenate(halves(grad[q_rows, cols]), 0)
                )
            return carry

        lax.fori_loop(low[kb], high[kb], step, 0)
        dk_out[k_rows, :] = (dk[...] * SCALE).astype(BF16)
        dv_out[k_rows, :] = dv[...].astype(BF16)

    dq_out[...] = (dq[...] * SCALE).astype(BF16)


def attend_back(core, begin, end, q, k, v, out, own, other, lse, seg_col):
    rows, width = q.shape
    heads = width // HEAD_DIM
    whole = lambda shape: pl.BlockSpec(shape, lambda i, *_: (0,) * len(shape))
    wide = pltpu.VMEM((heads, rows, 2 * HEAD_DIM), BF16)
    return pl.pallas_call(
        attend_back_kernel,
        out_shape=[jax.ShapeDtypeStruct((rows, width), BF16)] * 3,
        grid_spec=pltpu.PrefetchScalarGridSpec(
            num_scalar_prefetch=3,
            grid=(1,),
            in_specs=[whole((rows, width))] * 4
            + [whole((rows // 2, width))] * 2
            + [whole((heads, rows)), whole((rows, 1))],
            out_specs=[whole((rows, width))] * 3,
            scratch_shapes=[
                pltpu.VMEM((rows, width), BF16),
                wide,
                wide,
                wide,
                wide,
                pltpu.VMEM((rows, width), F32),
                pltpu.VMEM((BLOCK, width), F32),
                pltpu.VMEM((BLOCK, width), F32),
                pltpu.VMEM((heads, BLOCK, BLOCK), BF16),
                pltpu.VMEM((heads, BLOCK, BLOCK), BF16),
            ],
        ),
        compiler_params=params(),
        cost_estimate=pl.CostEstimate(
            flops=10 * rows * rows * width,
            bytes_accessed=16 << 20,
            transcendentals=rows * rows * heads // 2,
        ),
        name="attend_back",
    )(core, *spans(begin, end, BLOCK), q, k, v, out, own, other, lse, seg_col)


def row_mean(values):
    return jnp.mean(values, axis=-1, keepdims=True)


def norm(values):
    centre = values - row_mean(values)
    scale = lax.rsqrt(row_mean(centre * centre) + EPS)
    return centre * scale, scale


def norm_back(normed, scale, gain, grad):
    inner = grad * gain
    return scale * (inner - row_mean(inner) - normed * row_mean(inner * normed))


def column_sum(values):
    return jnp.sum(values.astype(F32), axis=0, keepdims=True)


def rows_kernel(
    core, x_ref, mine, theirs, cot, wo_mine_ref, wo_theirs_ref, wide_ref, vectors, be,
    out, ga_mine, ga_theirs, residual, act, ge, low_out, gr_out, gb_out, sums, sum_e, slope,
):
    width = x_ref.shape[1]
    chunks = slope.shape[1] // width
    unit = width // UNITS
    each = UNITS // chunks
    we = lambda j: wide_ref[:, j, :unit, :].reshape(width, width)
    wr = lambda j: wide_ref[each * j : each * (j + 1), :, unit:, :].reshape(width, width)
    bo, br = vectors[0:1, :], vectors[1:2, :]
    gain1, shift1, gain2, shift2 = [vectors[n : n + 1, :] for n in range(2, 6)]
    wo_mine, wo_theirs = stacked(wo_mine_ref), stacked(wo_theirs_ref)

    @pl.when(pl.program_id(0) == 0)
    def _():
        sums[...] = jnp.zeros_like(sums)
        sum_e[...] = jnp.zeros_like(sum_e)

    branch = dot(mine[...], wo_mine) + dot(theirs[...], wo_theirs) + bo
    normed1, scale1 = norm(x_ref[...].astype(F32) + branch)
    first = normed1 * gain1 + shift1
    first_low = first.astype(BF16)
    low_out[...] = first_low
    reduced = jnp.zeros_like(first)
    for j in range(chunks):
        cols = slice(j * width, (j + 1) * width)
        u = dot(first_low, we(j)) + be[:, cols]
        square = u * u
        curve = jnp.tanh(GELU_A * (u + GELU_B * (square * u)))
        cdf = 0.5 * (1.0 + curve)
        slope[:, cols] = cdf + (0.5 * GELU_A) * u * (1.0 - curve * curve) * (
            1.0 + (3.0 * GELU_B) * square
        )
        activated = (u * cdf).astype(BF16)
        act[:, cols] = activated
        reduced += dot(activated, wr(j))
    normed2, scale2 = norm(first + (reduced + br))
    out[...] = (normed2 * gain2 + shift2).astype(BF16)

    incoming = cot[...].astype(F32)
    grad_second = norm_back(normed2, scale2, gain2, incoming)
    grad_reduced = grad_second.astype(BF16)
    gr_out[...] = grad_reduced
    grad_first = grad_second
    for j in range(chunks):
        cols = slice(j * width, (j + 1) * width)
        grad_expanded = (dot_right(grad_reduced, wr(j)) * slope[:, cols]).astype(BF16)
        ge[:, cols] = grad_expanded
        sum_e[:, cols] += column_sum(grad_expanded)
        grad_first += dot_right(grad_expanded, we(j))
    grad_residual = norm_back(normed1, scale1, gain1, grad_first)
    residual[...] = grad_residual
    grad_branch = grad_residual.astype(BF16)
    gb_out[...] = grad_branch
    ga_mine[...] = dot_right(grad_branch, wo_mine).astype(BF16)
    ga_theirs[...] = dot_right(grad_branch, wo_theirs).astype(BF16)
    sums[0:1, :] += column_sum(grad_branch)
    sums[1:2, :] += column_sum(grad_reduced)
    sums[2:3, :] += column_sum(grad_first * normed1)
    sums[3:4, :] += column_sum(grad_first)
    sums[4:5, :] += column_sum(incoming * normed2)
    sums[5:6, :] += column_sum(incoming)


def row_local(core, x, mine, theirs, cot, square, wide_all, vectors, be):
    rows, width = x.shape
    half, wide = width // 2, be.shape[1]
    side = lambda flip: pl.BlockSpec(
        (UNITS // 2, width // UNITS, width),
        lambda i, core: (core[0] ^ flip, 3, 0),
        pipeline_mode=pl.Buffered(1),
    )
    block = lambda cols: pl.BlockSpec((ROWS, cols), lambda i, *_: (i, 0))
    fixed = lambda a: pl.BlockSpec(
        a.shape, lambda i, *_: (0,) * a.ndim, pipeline_mode=pl.Buffered(1)
    )
    shape = lambda cols, kind: jax.ShapeDtypeStruct((rows, cols), kind)
    resident = lambda r, cols: pl.BlockSpec((r, cols), lambda i, *_: (0, 0))
    return pl.pallas_call(
        rows_kernel,
        out_shape=[
            shape(width, BF16),
            shape(half, BF16),
            shape(half, BF16),
            shape(width, F32),
            shape(wide, BF16),
            shape(wide, BF16),
            shape(width, BF16),
            shape(width, BF16),
            shape(width, BF16),
            jax.ShapeDtypeStruct((8, width), F32),
            jax.ShapeDtypeStruct((1, wide), F32),
        ],
        grid_spec=pltpu.PrefetchScalarGridSpec(
            num_scalar_prefetch=1,
            grid=(rows // ROWS,),
            in_specs=[
                block(width),
                block(half),
                block(half),
                block(width),
                side(0),
                side(1),
                fixed(wide_all),
                fixed(vectors),
                fixed(be),
            ],
            out_specs=[
                block(width),
                block(half),
                block(half),
                block(width),
                block(wide),
                block(wide),
                block(width),
                block(width),
                block(width),
                resident(8, width),
                resident(1, wide),
            ],
            scratch_shapes=[pltpu.VMEM((ROWS, wide), F32)],
        ),
        compiler_params=params(),
        cost_estimate=pl.CostEstimate(
            flops=2 * 2 * rows * width * (width + 2 * wide),
            bytes_accessed=40 << 20,
            transcendentals=rows * wide,
        ),
        name="row_local",
    )(core, x, mine, theirs, cot, square, square, wide_all, vectors, be)


def weight_grad_kernel(left, right, out):
    out[...] = dot_left(left[...], right[...]).astype(out.dtype)


def weight_grad(left, right, kind):
    rows, m = left.shape
    n = right.shape[1]
    tm, tn = min(m, 768), min(n, 768)
    return pl.pallas_call(
        weight_grad_kernel,
        out_shape=jax.ShapeDtypeStruct((m, n), kind),
        grid=(m // tm, n // tn),
        in_specs=[
            pl.BlockSpec((rows, tm), lambda i, j: (0, i)),
            pl.BlockSpec((rows, tn), lambda i, j: (0, j)),
        ],
        out_specs=pl.BlockSpec((tm, tn), lambda i, j: (i, j)),
        compiler_params=params(),
        cost_estimate=pl.CostEstimate(
            flops=2 * rows * m * n, bytes_accessed=16 << 20, transcendentals=0
        ),
        name="weight_grad",
    )(left, right)


def split_cores(core, both, axis):
    first, second = jnp.split(both, 2, axis=axis)
    keep = jnp.where(core == 0, first, second)
    send = jnp.where(core == 0, second, first)
    return keep.astype(BF16), send.astype(BF16)


def expand_grad_kernel(core, low, ge, keep, send):
    nz, unit = keep.shape[1], keep.shape[3]
    whole = dot_left(low[...], ge[...]).reshape(nz, 2, unit, -1)
    kept, sent = split_cores(core[0], whole, 1)
    keep[...] = kept.reshape(keep.shape)
    send[...] = sent.reshape(send.shape)


def reduce_grad_kernel(core, act, gr, keep_in, send_in, keep, send):
    unit = keep.shape[3]
    whole = dot_left(act[...], gr[...]).reshape(2, 4, unit, -1)
    kept, sent = split_cores(core[0], whole, 0)
    keep[...] = kept.reshape(keep.shape)
    send[...] = sent.reshape(send.shape)


def feed_grads(core, low, ge, act, gr):
    rows, width = low.shape
    wide = ge.shape[1]
    chunks = wide // width
    unit = width // 8
    shape = jax.ShapeDtypeStruct((4, 4, 2, unit, width), BF16)
    flops = 2 * rows * width * wide
    keep, send = pl.pallas_call(
        expand_grad_kernel,
        out_shape=[shape, shape],
        grid_spec=pltpu.PrefetchScalarGridSpec(
            num_scalar_prefetch=1,
            grid=(chunks,),
            in_specs=[
                pl.BlockSpec((rows, width), lambda i, *_: (0, 0)),
                pl.BlockSpec((rows, width), lambda i, *_: (0, i)),
            ],
            out_specs=[pl.BlockSpec((1, 4, 1, unit, width), lambda i, *_: (i, 0, 0, 0, 0))] * 2,
        ),
        compiler_params=params(),
        cost_estimate=pl.CostEstimate(flops=flops, bytes_accessed=14 << 20, transcendentals=0),
        name="expand_grad",
    )(core, low, ge)
    return pl.pallas_call(
        reduce_grad_kernel,
        out_shape=[shape, shape],
        grid_spec=pltpu.PrefetchScalarGridSpec(
            num_scalar_prefetch=1,
            grid=(chunks,),
            in_specs=[
                pl.BlockSpec((rows, width), lambda i, *_: (0, i)),
                pl.BlockSpec((rows, width), lambda i, *_: (0, 0)),
                pl.BlockSpec(memory_space=pl.ANY),
                pl.BlockSpec(memory_space=pl.ANY),
            ],
            out_specs=[pl.BlockSpec((4, 1, 1, unit, width), lambda i, *_: (0, i, 1, 0, 0))] * 2,
        ),
        input_output_aliases={3: 0, 4: 1},
        compiler_params=params(),
        cost_estimate=pl.CostEstimate(flops=flops, bytes_accessed=14 << 20, transcendentals=0),
        name="reduce_grad",
    )(core, act, gr, keep, send)


def output_grad_kernel(core, mine, theirs, gb, keep, send):
    nz, unit = keep.shape[:2]
    from_mine, from_theirs = dot_left(mine[...], gb[...]), dot_left(theirs[...], gb[...])
    first = jnp.where(core[0] == 0, from_mine, from_theirs)
    second = jnp.where(core[0] == 0, from_theirs, from_mine)
    whole = jnp.concatenate([first, second]).reshape(nz, 2, unit, -1)
    kept, sent = split_cores(core[0], whole, 1)
    keep[...] = kept.reshape(keep.shape)
    send[...] = sent.reshape(send.shape)


def output_grad(core, mine, theirs, gb):
    rows = mine.shape[0]
    width = gb.shape[1]
    shape = jax.ShapeDtypeStruct((4, width // 8, width), BF16)
    whole = lambda a: pl.BlockSpec(a.shape, lambda i, *_: (0,) * a.ndim)
    return pl.pallas_call(
        output_grad_kernel,
        out_shape=[shape, shape],
        grid_spec=pltpu.PrefetchScalarGridSpec(
            num_scalar_prefetch=1,
            grid=(1,),
            in_specs=[whole(mine), whole(theirs), whole(gb)],
            out_specs=[whole(shape)] * 2,
        ),
        compiler_params=params(),
        cost_estimate=pl.CostEstimate(
            flops=2 * rows * width * width, bytes_accessed=5 << 20, transcendentals=0
        ),
        name="output_grad",
    )(core, mine, theirs, gb)


def packed_input_grad_kernel(
    core, own, other, d_ref, w_ref, keep, send, sums, dx_own, dx_other
):
    part = pl.program_id(0)
    rows = own.shape[0]
    nz, unit = keep.shape[1], keep.shape[2]
    mine = pl.multiple_of(core[0] * rows, rows)
    theirs = pl.multiple_of((1 - core[0]) * rows, rows)
    d_own, d_other = d_ref[0, pl.ds(mine, rows), :], d_ref[0, pl.ds(theirs, rows), :]
    whole = (dot_left(own[...], d_own) + dot_left(other[...], d_other)).reshape(nz, 2, unit, -1)
    kept, sent = split_cores(core[0], whole, 1)
    keep[...] = kept.reshape(keep.shape)
    send[...] = sent.reshape(send.shape)
    sums[0] = jnp.broadcast_to(column_sum(d_own) + column_sum(d_other), sums.shape[1:])
    to_own, to_other = dot_right(d_own, stacked(w_ref)), dot_right(d_other, stacked(w_ref))

    @pl.when(part == 0)
    def _():
        dx_own[...] = to_own
        dx_other[...] = to_other

    @pl.when(part > 0)
    def _():
        dx_own[...] += to_own
        dx_other[...] += to_other


def packed_input_grad(core, own, other, grads, weights):
    rows, width = own.shape
    half = width // 2
    unit = width // 8
    shape = jax.ShapeDtypeStruct((3, 4, unit, half), BF16)
    whole = lambda shape: pl.BlockSpec(shape, lambda i, *_: (0,) * len(shape))
    packed = pl.BlockSpec((1, 4, unit, half), lambda i, core: (i, 0, 0, 0))
    return pl.pallas_call(
        packed_input_grad_kernel,
        out_shape=[
            shape,
            shape,
            jax.ShapeDtypeStruct((3, 8, half), F32),
            jax.ShapeDtypeStruct((rows, width), F32),
            jax.ShapeDtypeStruct((rows, width), F32),
        ],
        grid_spec=pltpu.PrefetchScalarGridSpec(
            num_scalar_prefetch=1,
            grid=(3,),
            in_specs=[
                whole((rows, width)),
                whole((rows, width)),
                pl.BlockSpec((1, 2 * rows, half), lambda i, core: (i, 0, 0)),
                pl.BlockSpec((UNITS, width // UNITS, half), lambda i, core: (0, i, core[0])),
            ],
            out_specs=[
                packed,
                packed,
                pl.BlockSpec((1, 8, half), lambda i, core: (i, 0, 0)),
                whole((rows, width)),
                whole((rows, width)),
            ],
        ),
        compiler_params=params(),
        cost_estimate=pl.CostEstimate(
            flops=2 * 2 * 2 * rows * width * 3 * half, bytes_accessed=20 << 20, transcendentals=0
        ),
        name="input_grad",
    )(core, own, other, grads, weights)


def input_grad_kernel(core, own, other, d_ref, w_ref, dw, sums, dx_own, dx_other):
    part = pl.program_id(0)
    rows = own.shape[0]
    mine = pl.multiple_of(core[0] * rows, rows)
    theirs = pl.multiple_of((1 - core[0]) * rows, rows)
    d_own, d_other = d_ref[0, pl.ds(mine, rows), :], d_ref[0, pl.ds(theirs, rows), :]
    dw[0] = (dot_left(own[...], d_own) + dot_left(other[...], d_other)).astype(dw.dtype)
    sums[0] = jnp.broadcast_to(column_sum(d_own) + column_sum(d_other), sums.shape[1:])
    to_own, to_other = dot_right(d_own, stacked(w_ref)), dot_right(d_other, stacked(w_ref))

    @pl.when(part == 0)
    def _():
        dx_own[...] = to_own
        dx_other[...] = to_other

    @pl.when(part > 0)
    def _():
        dx_own[...] += to_own
        dx_other[...] += to_other


def input_grad(core, own, other, grads, weights, kind):
    rows, width = own.shape
    half = width // 2
    whole = lambda shape: pl.BlockSpec(shape, lambda i, *_: (0,) * len(shape))
    return pl.pallas_call(
        input_grad_kernel,
        out_shape=[
            jax.ShapeDtypeStruct((3, width, half), kind),
            jax.ShapeDtypeStruct((3, 8, half), F32),
            jax.ShapeDtypeStruct((rows, width), F32),
            jax.ShapeDtypeStruct((rows, width), F32),
        ],
        grid_spec=pltpu.PrefetchScalarGridSpec(
            num_scalar_prefetch=1,
            grid=(3,),
            in_specs=[
                whole((rows, width)),
                whole((rows, width)),
                pl.BlockSpec((1, 2 * rows, half), lambda i, core: (i, 0, 0)),
                pl.BlockSpec((UNITS, width // UNITS, half), lambda i, core: (0, i, core[0])),
            ],
            out_specs=[
                pl.BlockSpec((1, width, half), lambda i, core: (i, 0, 0)),
                pl.BlockSpec((1, 8, half), lambda i, core: (i, 0, 0)),
                whole((rows, width)),
                whole((rows, width)),
            ],
        ),
        compiler_params=params(),
        cost_estimate=pl.CostEstimate(
            flops=2 * 2 * 2 * rows * width * 3 * half, bytes_accessed=20 << 20, transcendentals=0
        ),
        name="input_grad",
    )(core, own, other, grads, weights)


def local(tokens, segment_ids, cotangent, *shards):
    rep_size, shard_size = lax.axis_size("rep"), lax.axis_size("shard")
    rep, shard = lax.axis_index("rep"), lax.axis_index("shard")
    core = shard % 2
    core_arg = core.reshape(1).astype(jnp.int32)
    width = tokens.shape[2]
    half = width // 2
    both = ("rep", "shard")

    def flat(r, s):
        return r * shard_size + s

    def route(k, back=False):
        pairs = []
        for r in range(rep_size):
            for s in range(shard_size):
                there = (flat(r, s), flat(2 * (s % 2) + (r + k) % 2, s - s % 2 + r // 2))
                pairs.append(there[::-1] if back else there)
        return pairs

    swap_pairs = [(flat(r, s), flat(r, s ^ 1)) for r in range(rep_size) for s in range(shard_size)]

    def swap(array):
        return lax.ppermute(array, both, swap_pairs)

    odd = rep % 2

    def to_sequences(array):
        a, b = array[0], array[1]
        even_part = lax.ppermute(jnp.where(odd == 0, a, b), both, route(0))
        odd_part = lax.ppermute(jnp.where(odd == 0, b, a), both, route(1))
        return jnp.concatenate(
            [jnp.where(odd == 0, even_part, odd_part), jnp.where(odd == 0, odd_part, even_part)]
        )

    def from_sequences(array):
        rows = array.shape[0] // 2
        a, b = array[:rows], array[rows:]
        even_part = lax.ppermute(jnp.where(odd == 0, a, b), both, route(0, True))
        odd_part = lax.ppermute(jnp.where(odd == 0, b, a), both, route(1, True))
        return jnp.stack(
            [jnp.where(odd == 0, even_part, odd_part), jnp.where(odd == 0, odd_part, even_part)]
        )

    tuned = rep_size == 4 and shard_size == UNITS
    rows_at = width // UNITS
    chunks = shards[4].shape[1] // width
    small = jnp.concatenate(shards[6:])
    if tuned:
        small_rows = jnp.concatenate([small, jnp.zeros((EXTRA * width - small.shape[0],), BF16)])
        square_own = jnp.concatenate(list(shards[:4]) + [small_rows.reshape(EXTRA, width)])
        wide_own = jnp.concatenate(
            [
                shards[4].reshape(rows_at, chunks, width).transpose(1, 0, 2),
                shards[5].reshape(chunks, rows_at, width),
            ],
            axis=1,
        )
        square, wide_all = gather_weights(square_own, wide_own, shard_size // 2)
        small = square[:, 4 * rows_at :, :].reshape(shard_size, EXTRA * width)
    else:
        wq, wk, wv, wo, we, wr = [lax.all_gather(m, "shard", axis=0, tiled=True) for m in shards[:6]]
        square = jnp.concatenate(
            [m.reshape(UNITS, rows_at, width) for m in (wq, wk, wv, wo)]
            + [jnp.zeros((UNITS, EXTRA, width), BF16)],
            axis=1,
        )
        wide_all = jnp.concatenate(
            [
                we.reshape(UNITS, rows_at, chunks, width).transpose(0, 2, 1, 3),
                wr.reshape(UNITS, chunks, rows_at, width),
            ],
            axis=2,
        )
        small = lax.all_gather(small[None], "shard", axis=0, tiled=True)
    vectors, at = [], 0
    for member in shards[6:]:
        n = member.shape[0]
        vectors.append(small[:, at : at + n].reshape(1, n * shard_size).astype(F32))
        at += n
    bq, bv, bo, be, br, gain1, shift1, gain2, shift2 = vectors

    own = to_sequences(tokens)
    cot = to_sequences(cotangent)
    other = swap(own)
    swapped_ids = swap(segment_ids)
    ids = jnp.where(rep // 2 == core, segment_ids, swapped_ids)
    segments = lax.dynamic_index_in_dim(ids, odd, 0, keepdims=False)
    blocks = segments.reshape(-1, BLOCK)
    begin = jnp.sum((segments[None, :] < blocks[:, :1]).astype(jnp.int32), axis=1)
    end = jnp.sum((segments[None, :] <= blocks[:, -1:]).astype(jnp.int32), axis=1)
    seg_col = segments[:, None]

    q, k, v = project(core_arg, own, other, square, bq, bv)
    attended, lse = attend(begin, end, q, k, v, seg_col)
    rows = own.shape[0]
    mine = lax.dynamic_slice_in_dim(attended, core * rows, rows)
    theirs = swap(lax.dynamic_slice_in_dim(attended, (1 - core) * rows, rows))
    table = jnp.concatenate([bo, br, gain1, shift1, gain2, shift2, bo, bo])
    out, ga_mine, ga_theirs, residual, act, ge, first_low, gr, gb, sums, sum_e = row_local(
        core_arg, own, mine, theirs, cot, square, wide_all, table, be
    )
    ga_other = swap(ga_theirs)
    if not tuned:
        dwr = weight_grad(act, gr, F32)
        dwe = weight_grad(first_low, ge, F32)
        dwo_mine, dwo_theirs = weight_grad(mine, gb, F32), weight_grad(theirs, gb, F32)
        dq, dk, dv = attend_back(
            core_arg, begin, end, q, k, v, attended, ga_mine, ga_other, lse, seg_col
        )
        dw, sum_qkv, dx_own, dx_other = input_grad(
            core_arg, own, other, jnp.stack([dq, dk, dv]), square, F32
        )
        dx = (residual + dx_own + swap(dx_other.astype(BF16)).astype(F32)).astype(BF16)

        def place(part, dim):
            zero = jnp.zeros_like(part)
            return jnp.where(
                core == 0,
                jnp.concatenate([part, zero], axis=dim),
                jnp.concatenate([zero, part], axis=dim),
            )

        dwo = jnp.where(
            core == 0,
            jnp.concatenate([dwo_mine, dwo_theirs]),
            jnp.concatenate([dwo_theirs, dwo_mine]),
        )
        totals = (
            place(dw[0], 1),
            place(dw[1], 1),
            place(dw[2], 1),
            dwo,
            dwe,
            dwr,
            place(sum_qkv[0, 0], 0),
            place(sum_qkv[2, 0], 0),
            sums[0],
            sum_e[0],
            sums[1],
            sums[2],
            sums[3],
            sums[4],
            sums[5],
        )
        summed = lax.psum_scatter(totals, "shard", scatter_dimension=0, tiled=True)
        final = [part.astype(F32) for part in lax.psum([p.astype(BF16) for p in summed], "rep")]
        return (from_sequences(out), from_sequences(dx)) + tuple(final)

    z = shard // 2
    nz = shard_size // 2

    def plane_send(array, k):
        pairs = [(flat(r, s), flat(r ^ k, s)) for r in range(4) for s in range(shard_size)]
        return lax.ppermute(array, both, pairs)

    def line_send(array, k):
        pairs = [(flat(r, s), flat(r, s ^ (2 * k))) for r in range(4) for s in range(shard_size)]
        return lax.ppermute(array, both, pairs)

    def pick(array, n):
        return lax.dynamic_index_in_dim(array, n, 0, keepdims=False)

    def scatter_plane(pieces):
        got = [plane_send(pieces(rep ^ k).astype(BF16), k) for k in (1, 2, 3)]
        total = pieces(rep)
        for part in got:
            total = total + part.astype(F32)
        return total

    def scatter_line(array):
        got = [line_send(pick(array, z ^ k).astype(BF16), k) for k in range(1, nz)]
        total = pick(array, z)
        for part in got:
            total = total + part.astype(F32)
        return total

    def gather_plane(part):
        got = [part] + [plane_send(part, k) for k in (1, 2, 3)]
        result = jnp.zeros((4,) + part.shape, part.dtype)
        for k in range(4):
            result = lax.dynamic_update_index_in_dim(result, got[k], rep ^ k, 0)
        return result.astype(F32)

    feed_keep, feed_send = feed_grads(core_arg, first_low, ge, act, gr)
    wo_keep, wo_send = output_grad(core_arg, mine, theirs, gb)
    feed_got = swap(feed_send)
    wo_got = swap(wo_send)
    feed_parts = [
        pick(feed_keep, rep ^ hop).astype(F32) + pick(feed_got, rep ^ hop).astype(F32)
        for hop in range(4)
    ]
    feed_sent = [part.astype(BF16) for part in feed_parts[1:]]
    feed_sent, ga_other = lax.optimization_barrier((feed_sent, ga_other))
    feed = feed_parts[0]
    for hop in (1, 2, 3):
        feed = feed + plane_send(feed_sent[hop - 1], hop).astype(F32)
    dq, dk, dv = attend_back(
        core_arg, begin, end, q, k, v, attended, ga_mine, ga_other, lse, seg_col
    )
    line_sent = [pick(feed, z ^ hop).astype(BF16) for hop in range(1, nz)]
    line_sent, dq = lax.optimization_barrier((line_sent, dq))
    feed = pick(feed, z)
    for hop in range(1, nz):
        feed = feed + line_send(line_sent[hop - 1], hop).astype(F32)
    feed = feed.astype(BF16)
    qkv_keep, qkv_send, sum_qkv, dx_own, dx_other = packed_input_grad(
        core_arg, own, other, jnp.stack([dq, dk, dv]), square
    )
    dx = (residual + dx_own + swap(dx_other.astype(BF16)).astype(F32)).astype(BF16)
    qkv_got = swap(qkv_send)
    qkv = jnp.where(
        core == 0,
        jnp.concatenate([qkv_keep, qkv_got], axis=3),
        jnp.concatenate([qkv_got, qkv_keep], axis=3),
    )
    unit = width // shard_size
    wide_unit = sum_e.shape[1] // shard_size

    def place(part):
        zero = jnp.zeros_like(part)
        return jnp.where(
            core == 0, jnp.concatenate([part, zero]), jnp.concatenate([zero, part])
        )

    rows_of = [place(sum_qkv[0, 0]), place(sum_qkv[2, 0])] + [sums[n] for n in range(6)]
    table = jnp.concatenate(
        [vector.reshape(shard_size, unit) for vector in rows_of]
        + [
            sum_e.reshape(shard_size, wide_unit),
            jnp.zeros((shard_size, 2 * width - 8 * unit - wide_unit), F32),
        ],
        axis=1,
    ).reshape(nz, 2, 2, width)
    mine_table = lax.dynamic_index_in_dim(table, core, 1, keepdims=False)
    other_table = lax.dynamic_index_in_dim(table, 1 - core, 1, keepdims=False)
    mine_table = mine_table + swap(other_table)
    wo_sum = wo_keep.astype(F32) + wo_got.astype(F32)
    fourth = jnp.concatenate([wo_sum, mine_table, jnp.zeros((nz, 6, width), F32)], axis=1)
    rest = jnp.concatenate(
        [
            jnp.concatenate([qkv, jnp.zeros((3, nz, 8, width), BF16)], axis=2),
            fourth.astype(BF16)[None],
        ]
    )
    rest = scatter_line(scatter_plane(lambda n: pick(rest, n).astype(F32))).astype(BF16)
    result = gather_plane(jnp.concatenate([feed.reshape(2 * unit, width), rest]))
    dwe = result[:, :unit].transpose(1, 0, 2).reshape(unit, 4 * width)
    dwr = result[:, unit : 2 * unit].reshape(4 * unit, width)
    dwq, dwk, dwv, dwo = [result[n, 2 * unit : 3 * unit] for n in range(4)]
    small = result[3, 3 * unit : 3 * unit + 2].reshape(-1)
    dbq, dbv, dbo, dbr, dg1, ds1, dg2, ds2 = [small[n * unit : (n + 1) * unit] for n in range(8)]
    dbe = small[8 * unit : 8 * unit + wide_unit]
    return (
        from_sequences(out),
        from_sequences(dx),
        dwq,
        dwk,
        dwv,
        dwo,
        dwe,
        dwr,
        dbq,
        dbv,
        dbo,
        dbe,
        dbr,
        dg1,
        ds1,
        dg2,
        ds2,
    )


def solution(mesh):
    row = P("shard", "rep", None)
    in_specs = (row, P("shard", None), row) + (P("shard", None),) * 6 + (P("shard"),) * 9
    out_specs = (row, row) + (P("shard", None),) * 6 + (P("shard"),) * 9
    return jax.shard_map(local, mesh=mesh, in_specs=in_specs, out_specs=out_specs, check_vma=False)
```

```python
import functools
import math

import jax
import jax.numpy as jnp
from jax import lax
from jax.experimental import pallas as pl
from jax.experimental.pallas import tpu as pltpu
from jax.sharding import PartitionSpec as P

HEAD_DIM = 64
BLOCK = 256
KEYS = 512
PREPARE = 512
DOCS = 8
ROWS = 256
MASKED = -1e30
EPS = 1e-05
UNITS = 8
EXTRA = 8
SCALE = HEAD_DIM**-0.5
SCALE2 = SCALE * math.log2(math.e)
GELU_A = math.sqrt(2.0 / math.pi)
GELU_B = 0.044715
F32 = jnp.float32
BF16 = jnp.bfloat16
VMEM_LIMIT = 60 * 1024 * 1024


def dot(left, right):
    return jnp.dot(left, right, preferred_element_type=F32)


def dot_right(left, right):
    return lax.dot_general(left, right, (((1,), (1,)), ((), ())), preferred_element_type=F32)


def dot_left(left, right):
    return lax.dot_general(left, right, (((0,), (0,)), ((), ())), preferred_element_type=F32)


def params(**more):
    return pltpu.CompilerParams(vmem_limit_bytes=VMEM_LIMIT, **more)


def stacked(ref):
    return ref[...].reshape(-1, ref.shape[-1])


def gather_kernel(
    nz, square, wide, square_all, wide_all,
    z_send, z_recv, p_send, p_recv, c_send, c_recv, own_send, own_recv, copied,
):
    r, s = lax.axis_index("rep"), lax.axis_index("shard")
    z = s // 2
    twin = (r, s ^ 1)
    barrier = pltpu.get_barrier_semaphore()

    def greet(device):
        pl.semaphore_signal(barrier, 1, device_id=device, device_id_type=pl.DeviceIdType.MESH)

    greet(twin)
    for k in (1, 2, 3):
        greet((r ^ k, s))
    for step in (1, -1):

        @pl.when((z + step >= 0) & (z + step < nz))
        def _(step=step):
            greet((r, s + 2 * step))

    pl.semaphore_wait(barrier, 4 + jnp.where(z > 0, 1, 0) + jnp.where(z < nz - 1, 1, 0))

    def copy(source, target, sent, got, device):
        return pltpu.make_async_remote_copy(
            source, target, sent, got, device_id=device, device_id_type=pl.DeviceIdType.MESH
        )

    kept = [
        pltpu.make_async_copy(square, square_all.at[s], copied.at[0]),
        pltpu.make_async_copy(wide, wide_all.at[s], copied.at[1]),
    ]
    own = [
        copy(square, square_all.at[s], own_send.at[0], own_recv.at[0], twin),
        copy(wide, wide_all.at[s], own_send.at[1], own_recv.at[1], twin),
    ]

    def onward(n, d, part):
        step = 1 - 2 * n
        at = s - 2 * step * d
        if part == 0:
            source = square if d == 0 else square_all.at[at]
            target = square_all.at[at]
        else:
            source = wide.at[r] if d == 0 else wide_all.at[at, r]
            target = wide_all.at[at, r]
        return copy(source, target, z_send.at[n, d, part], z_recv.at[n, d, part], (r, s + 2 * step))

    def sideways(n, d, k):
        at = s - 2 * (1 - 2 * n) * d
        part = wide_all.at[at, r]
        return copy(part, part, p_send.at[n, d - 1, k - 1], p_recv.at[n, d - 1, k - 1], (r ^ k, s))

    def across(n, d, k):
        at = s - 2 * (1 - 2 * n) * d
        part = square_all.at[at] if k == 4 else wide_all.at[at, r ^ k]
        return copy(part, part, c_send.at[n, d - 1, k], c_recv.at[n, d - 1, k], twin)

    def has(n, d):
        at = z - (1 - 2 * n) * d
        return (at >= 0) & (at < nz)

    def goes(n):
        at = z + 1 - 2 * n
        return (at >= 0) & (at < nz)

    for n in (0, 1):

        @pl.when(goes(n))
        def _(n=n):
            onward(n, 0, 1).start()
            onward(n, 0, 0).start()

    for c in own + kept:
        c.start()
    for d in range(1, nz):
        for n in (0, 1):

            @pl.when(has(n, d))
            def _(n=n, d=d):
                onward(n, d - 1, 1).wait_recv()
                if d < nz - 1:

                    @pl.when(goes(n))
                    def _():
                        onward(n, d, 1).start()

                for k in (1, 2, 3):
                    sideways(n, d, k).start()
                across(n, d, 0).start()
                onward(n, d - 1, 0).wait_recv()
                if d < nz - 1:

                    @pl.when(goes(n))
                    def _():
                        onward(n, d, 0).start()

                across(n, d, 4).start()

    for d in range(1, nz):
        for n in (0, 1):

            @pl.when(has(n, d))
            def _(n=n, d=d):
                for k in (1, 2, 3):
                    sideways(n, d, k).wait_recv()
                    across(n, d, k).start()

    for c in own + kept:
        c.wait()
    for n in (0, 1):

        @pl.when(goes(n))
        def _(n=n):
            onward(n, 0, 1).wait_send()
            onward(n, 0, 0).wait_send()

    for d in range(1, nz):
        for n in (0, 1):

            @pl.when(has(n, d))
            def _(n=n, d=d):
                for k in (1, 2, 3):
                    sideways(n, d, k).wait_send()
                for k in range(5):
                    across(n, d, k).wait()
                if d < nz - 1:

                    @pl.when(goes(n))
                    def _():
                        onward(n, d, 1).wait_send()
                        onward(n, d, 0).wait_send()


def gather_weights(square, wide, nz):
    anywhere = pl.BlockSpec(memory_space=pl.ANY)
    sems = lambda *shape: pltpu.SemaphoreType.DMA(shape)
    return pl.pallas_call(
        functools.partial(gather_kernel, nz),
        out_shape=[
            jax.ShapeDtypeStruct((2 * nz,) + square.shape, BF16),
            jax.ShapeDtypeStruct((2 * nz,) + wide.shape, BF16),
        ],
        in_specs=[anywhere] * 2,
        out_specs=[anywhere] * 2,
        scratch_shapes=[
            sems(2, nz - 1, 2),
            sems(2, nz - 1, 2),
            sems(2, nz - 1, 3),
            sems(2, nz - 1, 3),
            sems(2, nz - 1, 5),
            sems(2, nz - 1, 5),
            sems(2),
            sems(2),
            sems(2),
        ],
        compiler_params=params(collective_id=0, has_side_effects=True),
        cost_estimate=pl.CostEstimate(flops=0, bytes_accessed=150 << 20, transcendentals=0),
        name="gather_weights",
    )(square, wide)


def qkv_kernel(core, own, other, wq, wk, wv, bq, bv, q_out, k_out, v_out):
    per_core = pl.num_programs(0) // 2
    mine = pl.program_id(0) // per_core == core[0]
    rows = jnp.where(mine, own[...], other[...])
    q_out[...] = (dot(rows, stacked(wq)) + bq[...]).astype(BF16)
    k_out[...] = dot(rows, stacked(wk)).astype(BF16)
    v_out[...] = (dot(rows, stacked(wv)) + bv[...]).astype(BF16)


def project(core, own, other, square, bq, bv):
    rows, width = own.shape
    half = width // 2
    steps = rows // ROWS

    def side(flip):
        def index(i, core):
            first = jnp.where(core[0] == flip, 0, steps)
            return (jnp.clip(i - first, 0, steps - 1), 0)

        return index

    weight = lambda m: pl.BlockSpec(
        (UNITS, width // UNITS, half), lambda i, core: (0, m, core[0])
    )
    bias = pl.BlockSpec((1, half), lambda i, core: (0, core[0]))
    result = pl.BlockSpec((ROWS, half), lambda i, core: (i, 0))
    return pl.pallas_call(
        qkv_kernel,
        out_shape=[jax.ShapeDtypeStruct((2 * rows, half), BF16)] * 3,
        grid_spec=pltpu.PrefetchScalarGridSpec(
            num_scalar_prefetch=1,
            grid=(2 * steps,),
            in_specs=[
                pl.BlockSpec((ROWS, width), side(0)),
                pl.BlockSpec((ROWS, width), side(1)),
                weight(0),
                weight(1),
                weight(2),
                bias,
                bias,
            ],
            out_specs=[result] * 3,
        ),
        compiler_params=params(),
        cost_estimate=pl.CostEstimate(
            flops=2 * 2 * rows * width * 3 * half, bytes_accessed=10 << 20, transcendentals=0
        ),
        name="project",
    )(core, own, other, square, square, square, bq, bv)


def halves(pair):
    lane = lax.broadcasted_iota(jnp.int32, pair.shape, 1)
    zero = jnp.zeros_like(pair)
    return jnp.where(lane < HEAD_DIM, pair, zero), jnp.where(lane < HEAD_DIM, zero, pair)


def rows_at(n, size):
    return pl.ds(pl.multiple_of(n * size, size), size)


def widen(pair, extra):
    lane = lax.broadcasted_iota(jnp.int32, pair.shape, 1)
    return jnp.where(lane < HEAD_DIM, pair, extra[0]), jnp.where(lane < HEAD_DIM, extra[1], pair)


def same_document(ids, extra_lanes):
    slot = lax.broadcasted_iota(jnp.int32, (ids.shape[0], 2 * HEAD_DIM), 1) % HEAD_DIM
    hit = slot == ids
    for_keys = jnp.where(
        (slot < DOCS) & ~hit,
        MASKED,
        jnp.where((slot >= DOCS) & (slot < DOCS + extra_lanes), 1.0, 0.0),
    )
    return jnp.where(hit, 1.0, 0.0), for_keys.astype(BF16)


def attend_kernel(low, high, q_ref, k_ref, v_ref, seg_col, out, lse, qx, kx, v_turned, top, mix, kept):
    rows, width = q_ref.shape
    heads = width // HEAD_DIM
    pairs = heads // 2
    for at in range(0, rows, PREPARE):
        part = pl.ds(at, PREPARE)
        for_queries, for_keys = same_document(seg_col[part, :], 0)
        for_queries = for_queries.astype(BF16)
        for pair in range(pairs):
            cols = pl.ds(pair * 2 * HEAD_DIM, 2 * HEAD_DIM)
            both = slice(2 * pair, 2 * pair + 2)
            qx[both, part, :] = jnp.stack(widen(q_ref[part, cols], (for_queries, for_queries)))
            kx[both, part, :] = jnp.stack(widen(k_ref[part, cols], (for_keys, for_keys)))
            v_turned[both, :HEAD_DIM, part] = v_ref[part, cols].T.reshape(2, HEAD_DIM, PREPARE)
    v_turned[:, HEAD_DIM:, :] = jnp.ones_like(v_turned[:, HEAD_DIM:, :])

    @pl.loop(0, rows // BLOCK)
    def _(qb):
        q_rows = rows_at(qb, BLOCK)
        top[...] = jnp.full_like(top, MASKED)
        mix[...] = jnp.zeros_like(mix)

        def score(kb, carry):
            k_rows = rows_at(kb, KEYS)
            for h in range(heads):
                scores = dot_right(kx[h, k_rows, :], qx[h, q_rows, :])
                kept[h, k_rows, :] = scores
                top[h] = jnp.maximum(top[h], jnp.max(scores.reshape(KEYS // 8, 8, BLOCK), axis=0))
            return carry

        lax.fori_loop(low[qb], high[qb], score, 0)
        tops = [jnp.max(top[h], axis=0, keepdims=True) * SCALE2 for h in range(heads)]

        def weigh(kb, carry):
            k_rows = rows_at(kb, KEYS)
            for h in range(heads):
                weight = jnp.exp2(kept[h, k_rows, :] * SCALE2 - tops[h]).astype(BF16)
                mix[h] += dot(v_turned[h, :, k_rows], weight)
            return carry

        lax.fori_loop(low[qb], high[qb], weigh, 0)
        for h in range(heads):
            total = mix[h, HEAD_DIM : HEAD_DIM + 1, :]
            lse[pl.ds(h, 1), q_rows] = tops[h] + jnp.log2(total)
            mix[h, :HEAD_DIM, :] = mix[h, :HEAD_DIM, :] / total
        for pair in range(pairs):
            both = mix[2 * pair : 2 * pair + 2, :HEAD_DIM, :].reshape(2 * HEAD_DIM, BLOCK)
            out[q_rows, pl.ds(pair * 2 * HEAD_DIM, 2 * HEAD_DIM)] = both.T.astype(BF16)


def spans(begin, end, size):
    return begin // size, (end + size - 1) // size


def attend(begin, end, q, k, v, seg_col):
    rows, width = q.shape
    heads = width // HEAD_DIM
    whole = lambda shape: pl.BlockSpec(shape, lambda i, *_: (0,) * len(shape))
    wide = pltpu.VMEM((heads, rows, 2 * HEAD_DIM), BF16)
    return pl.pallas_call(
        attend_kernel,
        out_shape=[
            jax.ShapeDtypeStruct((rows, width), BF16),
            jax.ShapeDtypeStruct((heads, rows), F32),
        ],
        grid_spec=pltpu.PrefetchScalarGridSpec(
            num_scalar_prefetch=2,
            grid=(1,),
            in_specs=[whole((rows, width))] * 3 + [whole((rows, 1))],
            out_specs=[whole((rows, width)), whole((heads, rows))],
            scratch_shapes=[
                wide,
                wide,
                pltpu.VMEM((heads, HEAD_DIM + 16, rows), BF16),
                pltpu.VMEM((heads, 8, BLOCK), F32),
                pltpu.VMEM((heads, HEAD_DIM + 16, BLOCK), F32),
                pltpu.VMEM((heads, rows, BLOCK), F32),
            ],
        ),
        compiler_params=params(),
        cost_estimate=pl.CostEstimate(
            flops=4 * rows * rows * width,
            bytes_accessed=8 << 20,
            transcendentals=rows * rows * heads // 2,
        ),
        name="attend",
    )(*spans(begin, end, KEYS), q, k, v, seg_col)


def three_parts(values):
    first = values.astype(BF16)
    rest = values - first.astype(F32)
    second = rest.astype(BF16)
    return first, second, (rest - second.astype(F32)).astype(BF16)


def attend_back_kernel(
    core, low, high, q_ref, k_ref, v_ref, out_ref, own, other, lse, seg_col,
    dq_out, dk_out, dv_out, sums, grad, qx, kx, vx, gx, dq, dk, dv, weights, slopes,
):
    rows, width = q_ref.shape
    heads = width // HEAD_DIM
    pairs = heads // 2
    lanes = 2 * HEAD_DIM
    per_core = own.shape[0]
    grad[rows_at(core[0], per_core), :] = own[...]
    grad[rows_at(1 - core[0], per_core), :] = other[...]
    source = lax.broadcasted_iota(jnp.int32, (24, heads * lanes), 0)
    lane = lax.broadcasted_iota(jnp.int32, (24, heads * lanes), 1)
    place = jnp.where(
        (source % 8 == lane // lanes)
        & (lane % HEAD_DIM == DOCS + source // 8)
        & ((lane % lanes) // HEAD_DIM != (lane // lanes) % 2),
        1.0,
        0.0,
    ).astype(BF16)
    picks = jnp.where(
        lax.broadcasted_iota(jnp.int32, (width, 8), 0) // HEAD_DIM
        == lax.broadcasted_iota(jnp.int32, (width, 8), 1),
        1.0,
        0.0,
    ).astype(BF16)
    for at in range(0, rows, PREPARE):
        part = pl.ds(at, PREPARE)
        for_queries, for_keys = same_document(seg_col[part, :], 3)
        ones = jnp.where(for_keys == 1.0, for_keys, jnp.zeros_like(for_keys))
        level = jnp.concatenate(
            [lse[:, part] * (-1.0 / SCALE2), jnp.zeros((8 - heads, PREPARE), F32)]
        )
        levels = dot_left(jnp.concatenate(three_parts(level)), place)
        both = grad[part, :].astype(F32) * out_ref[part, :].astype(F32)
        coarse = both.astype(BF16)
        fine = (both - coarse.astype(F32)).astype(BF16)
        delta = dot(coarse, picks) + dot(fine, picks)
        deltas = dot(jnp.concatenate(three_parts(-delta), 1), place).astype(BF16)
        for pair in range(pairs):
            cols = pl.ds(pair * lanes, lanes)
            sides = slice(2 * pair, 2 * pair + 2)
            one, two = [slice((2 * pair + e) * lanes, (2 * pair + e + 1) * lanes) for e in (0, 1)]
            marks = [(for_queries + levels[:, side]).astype(BF16) for side in (one, two)]
            qx[sides, part, :] = jnp.stack(widen(q_ref[part, cols], marks))
            kx[sides, part, :] = jnp.stack(widen(k_ref[part, cols], (for_keys, for_keys)))
            vx[sides, part, :] = jnp.stack(widen(v_ref[part, cols], (ones, ones)))
            gx[sides, part, :] = jnp.stack(widen(grad[part, cols], (deltas[:, one], deltas[:, two])))

    dq[...] = jnp.zeros_like(dq)

    @pl.loop(0, rows // BLOCK)
    def _(kb):
        k_rows = rows_at(kb, BLOCK)
        dk[...] = jnp.zeros_like(dk)
        dv[...] = jnp.zeros_like(dv)

        def step(qb, carry):
            q_rows = rows_at(qb, BLOCK)
            for h in range(heads):
                probs = jnp.exp2(dot_right(kx[h, k_rows, :], qx[h, q_rows, :]) * SCALE2)
                weights[h] = probs.astype(BF16)
                centred = dot_right(vx[h, k_rows, :], gx[h, q_rows, :])
                slopes[h] = (probs * centred).astype(BF16)
            for pair in range(pairs):
                cols = pl.ds(pair * lanes, lanes)
                slope = [slopes[2 * pair], slopes[2 * pair + 1]]
                weight = [weights[2 * pair], weights[2 * pair + 1]]
                dq[q_rows, cols] += dot_left(
                    jnp.concatenate(slope, 0), jnp.concatenate(halves(k_ref[k_rows, cols]), 0)
                )
                dk[:, cols] += dot(
                    jnp.concatenate(slope, 1), jnp.concatenate(halves(q_ref[q_rows, cols]), 0)
                )
                dv[:, cols] += dot(
                    jnp.concatenate(weight, 1), jnp.concatenate(halves(grad[q_rows, cols]), 0)
                )
            return carry

        lax.fori_loop(low[kb], high[kb], step, 0)
        dk_out[k_rows, :] = (dk[...] * SCALE).astype(BF16)
        dv_out[k_rows, :] = dv[...].astype(BF16)

    dq_out[...] = (dq[...] * SCALE).astype(BF16)
    ones = jnp.ones((8, rows), BF16)
    sums[0] = dot(ones, dq_out[...])
    sums[1] = dot(ones, dv_out[...])


def attend_back(core, begin, end, q, k, v, out, own, other, lse, seg_col):
    rows, width = q.shape
    heads = width // HEAD_DIM
    whole = lambda shape: pl.BlockSpec(shape, lambda i, *_: (0,) * len(shape))
    wide = pltpu.VMEM((heads, rows, 2 * HEAD_DIM), BF16)
    return pl.pallas_call(
        attend_back_kernel,
        out_shape=[jax.ShapeDtypeStruct((rows, width), BF16)] * 3
        + [jax.ShapeDtypeStruct((2, 8, width), F32)],
        grid_spec=pltpu.PrefetchScalarGridSpec(
            num_scalar_prefetch=3,
            grid=(1,),
            in_specs=[whole((rows, width))] * 4
            + [whole((rows // 2, width))] * 2
            + [whole((heads, rows)), whole((rows, 1))],
            out_specs=[whole((rows, width))] * 3 + [whole((2, 8, width))],
            scratch_shapes=[
                pltpu.VMEM((rows, width), BF16),
                wide,
                wide,
                wide,
                wide,
                pltpu.VMEM((rows, width), F32),
                pltpu.VMEM((BLOCK, width), F32),
                pltpu.VMEM((BLOCK, width), F32),
                pltpu.VMEM((heads, BLOCK, BLOCK), BF16),
                pltpu.VMEM((heads, BLOCK, BLOCK), BF16),
            ],
        ),
        compiler_params=params(),
        cost_estimate=pl.CostEstimate(
            flops=10 * rows * rows * width,
            bytes_accessed=16 << 20,
            transcendentals=rows * rows * heads // 2,
        ),
        name="attend_back",
    )(core, *spans(begin, end, BLOCK), q, k, v, out, own, other, lse, seg_col)


def row_mean(values):
    return jnp.mean(values, axis=-1, keepdims=True)


def norm(values):
    centre = values - row_mean(values)
    scale = lax.rsqrt(row_mean(centre * centre) + EPS)
    return centre * scale, scale


def norm_back(normed, scale, gain, grad):
    inner = grad * gain
    return scale * (inner - row_mean(inner) - normed * row_mean(inner * normed))


def column_sum(values):
    return jnp.sum(values.astype(F32), axis=0, keepdims=True)


def rows_kernel(
    core, x_ref, mine, theirs, cot, wo_mine_ref, wo_theirs_ref, wide_ref, vectors, be,
    out, ga_mine, ga_theirs, residual, act, ge, low_out, gr_out, gb_out, sums, sum_e, slope,
):
    width = x_ref.shape[1]
    chunks = slope.shape[1] // width
    unit = width // UNITS
    each = UNITS // chunks
    we = lambda j: wide_ref[:, j, :unit, :].reshape(width, width)
    wr = lambda j: wide_ref[each * j : each * (j + 1), :, unit:, :].reshape(width, width)
    bo, br = vectors[0:1, :], vectors[1:2, :]
    gain1, shift1, gain2, shift2 = [vectors[n : n + 1, :] for n in range(2, 6)]
    wo_mine, wo_theirs = stacked(wo_mine_ref), stacked(wo_theirs_ref)

    @pl.when(pl.program_id(0) == 0)
    def _():
        sums[...] = jnp.zeros_like(sums)
        sum_e[...] = jnp.zeros_like(sum_e)

    branch = dot(mine[...], wo_mine) + dot(theirs[...], wo_theirs) + bo
    normed1, scale1 = norm(x_ref[...].astype(F32) + branch)
    first = normed1 * gain1 + shift1
    first_low = first.astype(BF16)
    low_out[...] = first_low
    reduced = jnp.zeros_like(first)
    for j in range(chunks):
        cols = slice(j * width, (j + 1) * width)
        u = dot(first_low, we(j)) + be[:, cols]
        square = u * u
        curve = jnp.tanh(GELU_A * (u + GELU_B * (square * u)))
        cdf = 0.5 * (1.0 + curve)
        slope[:, cols] = cdf + (0.5 * GELU_A) * u * (1.0 - curve * curve) * (
            1.0 + (3.0 * GELU_B) * square
        )
        activated = (u * cdf).astype(BF16)
        act[:, cols] = activated
        reduced += dot(activated, wr(j))
    normed2, scale2 = norm(first + (reduced + br))
    out[...] = (normed2 * gain2 + shift2).astype(BF16)

    incoming = cot[...].astype(F32)
    grad_second = norm_back(normed2, scale2, gain2, incoming)
    grad_reduced = grad_second.astype(BF16)
    gr_out[...] = grad_reduced
    grad_first = grad_second
    for j in range(chunks):
        cols = slice(j * width, (j + 1) * width)
        grad_expanded = (dot_right(grad_reduced, wr(j)) * slope[:, cols]).astype(BF16)
        ge[:, cols] = grad_expanded
        sum_e[:, cols] += column_sum(grad_expanded)
        grad_first += dot_right(grad_expanded, we(j))
    grad_residual = norm_back(normed1, scale1, gain1, grad_first)
    residual[...] = grad_residual
    grad_branch = grad_residual.astype(BF16)
    gb_out[...] = grad_branch
    ga_mine[...] = dot_right(grad_branch, wo_mine).astype(BF16)
    ga_theirs[...] = dot_right(grad_branch, wo_theirs).astype(BF16)
    sums[0:1, :] += column_sum(grad_branch)
    sums[1:2, :] += column_sum(grad_reduced)
    sums[2:3, :] += column_sum(grad_first * normed1)
    sums[3:4, :] += column_sum(grad_first)
    sums[4:5, :] += column_sum(incoming * normed2)
    sums[5:6, :] += column_sum(incoming)


def row_local(core, x, mine, theirs, cot, square, wide_all, vectors, be):
    rows, width = x.shape
    half, wide = width // 2, be.shape[1]
    side = lambda flip: pl.BlockSpec(
        (UNITS // 2, width // UNITS, width),
        lambda i, core: (core[0] ^ flip, 3, 0),
        pipeline_mode=pl.Buffered(1),
    )
    block = lambda cols: pl.BlockSpec((ROWS, cols), lambda i, *_: (i, 0))
    fixed = lambda a: pl.BlockSpec(
        a.shape, lambda i, *_: (0,) * a.ndim, pipeline_mode=pl.Buffered(1)
    )
    shape = lambda cols, kind: jax.ShapeDtypeStruct((rows, cols), kind)
    resident = lambda r, cols: pl.BlockSpec((r, cols), lambda i, *_: (0, 0))
    return pl.pallas_call(
        rows_kernel,
        out_shape=[
            shape(width, BF16),
            shape(half, BF16),
            shape(half, BF16),
            shape(width, F32),
            shape(wide, BF16),
            shape(wide, BF16),
            shape(width, BF16),
            shape(width, BF16),
            shape(width, BF16),
            jax.ShapeDtypeStruct((8, width), F32),
            jax.ShapeDtypeStruct((1, wide), F32),
        ],
        grid_spec=pltpu.PrefetchScalarGridSpec(
            num_scalar_prefetch=1,
            grid=(rows // ROWS,),
            in_specs=[
                block(width),
                block(half),
                block(half),
                block(width),
                side(0),
                side(1),
                fixed(wide_all),
                fixed(vectors),
                fixed(be),
            ],
            out_specs=[
                block(width),
                block(half),
                block(half),
                block(width),
                block(wide),
                block(wide),
                block(width),
                block(width),
                block(width),
                resident(8, width),
                resident(1, wide),
            ],
            scratch_shapes=[pltpu.VMEM((ROWS, wide), F32)],
        ),
        compiler_params=params(),
        cost_estimate=pl.CostEstimate(
            flops=2 * 2 * rows * width * (width + 2 * wide),
            bytes_accessed=40 << 20,
            transcendentals=rows * wide,
        ),
        name="row_local",
    )(core, x, mine, theirs, cot, square, square, wide_all, vectors, be)


def weight_grad_kernel(left, right, out):
    out[...] = dot_left(left[...], right[...]).astype(out.dtype)


def weight_grad(left, right, kind):
    rows, m = left.shape
    n = right.shape[1]
    tm, tn = min(m, 768), min(n, 768)
    return pl.pallas_call(
        weight_grad_kernel,
        out_shape=jax.ShapeDtypeStruct((m, n), kind),
        grid=(m // tm, n // tn),
        in_specs=[
            pl.BlockSpec((rows, tm), lambda i, j: (0, i)),
            pl.BlockSpec((rows, tn), lambda i, j: (0, j)),
        ],
        out_specs=pl.BlockSpec((tm, tn), lambda i, j: (i, j)),
        compiler_params=params(),
        cost_estimate=pl.CostEstimate(
            flops=2 * rows * m * n, bytes_accessed=16 << 20, transcendentals=0
        ),
        name="weight_grad",
    )(left, right)


def split_cores(core, both, axis):
    first, second = jnp.split(both, 2, axis=axis)
    keep = jnp.where(core == 0, first, second)
    send = jnp.where(core == 0, second, first)
    return keep.astype(BF16), send.astype(BF16)


def expand_grad_kernel(core, low, ge, keep, send):
    nz, unit = keep.shape[1], keep.shape[2]
    whole = dot_left(low[...], ge[...]).reshape(nz, 2, unit, -1)
    kept, sent = split_cores(core[0], whole, 1)
    keep[...] = kept.reshape(keep.shape)
    send[...] = sent.reshape(send.shape)


def reduce_grad_kernel(core, act, gr, keep_in, send_in, keep, send):
    unit = keep.shape[2]
    whole = dot_left(act[...], gr[...]).reshape(2, 4, unit, -1)
    kept, sent = split_cores(core[0], whole, 0)
    keep[...] = kept.reshape(keep.shape)
    send[...] = sent.reshape(send.shape)


def output_grad_kernel(core, mine, theirs, gb, keep_in, send_in, keep, send):
    quarter = keep.shape[2]
    from_mine, from_theirs = dot_left(mine[...], gb[...]), dot_left(theirs[...], gb[...])
    first = jnp.where(core[0] == 0, from_mine, from_theirs)
    second = jnp.where(core[0] == 0, from_theirs, from_mine)
    whole = jnp.concatenate([first, second]).reshape(keep.shape[1], 2, 4, quarter, -1)
    kept, sent = split_cores(core[0], whole, 1)
    for part in range(4):
        keep[part] = kept[:, 0, part]
        send[part] = sent[:, 0, part]


def feed_grads(core, low, ge, act, gr, mine, theirs, gb):
    rows, width = low.shape
    wide = ge.shape[1]
    chunks = wide // width
    unit = width // UNITS
    quarter = unit // 4
    nz = UNITS // 2
    shape = jax.ShapeDtypeStruct((4, nz, 2 * unit + quarter, width), BF16)
    anywhere = pl.BlockSpec(memory_space=pl.ANY)
    whole = lambda a: pl.BlockSpec(a.shape, lambda i, *_: (0,) * a.ndim)
    chunk = pl.BlockSpec((rows, width), lambda i, *_: (0, i))
    flops = 2 * rows * width * wide

    def call(kernel, grid, in_specs, out_spec, name, flops, *operands, aliases={}):
        return pl.pallas_call(
            kernel,
            out_shape=[shape, shape],
            grid_spec=pltpu.PrefetchScalarGridSpec(
                num_scalar_prefetch=1, grid=(grid,), in_specs=in_specs, out_specs=[out_spec] * 2
            ),
            input_output_aliases=aliases,
            compiler_params=params(),
            cost_estimate=pl.CostEstimate(flops=flops, bytes_accessed=14 << 20, transcendentals=0),
            name=name,
        )(core, *operands)

    keep, send = call(
        expand_grad_kernel,
        chunks,
        [whole(low), chunk],
        pl.BlockSpec((1, nz, unit, width), lambda i, *_: (i, 0, 0, 0)),
        "expand_grad",
        flops,
        low,
        ge,
    )
    keep, send = call(
        reduce_grad_kernel,
        chunks,
        [chunk, whole(gr), anywhere, anywhere],
        pl.BlockSpec((4, 1, unit, width), lambda i, *_: (0, i, 1, 0)),
        "reduce_grad",
        flops,
        act,
        gr,
        keep,
        send,
        aliases={3: 0, 4: 1},
    )
    return call(
        output_grad_kernel,
        1,
        [whole(mine), whole(theirs), whole(gb), anywhere, anywhere],
        pl.BlockSpec((4, nz, quarter, width), lambda i, *_: (0, 0, UNITS, 0)),
        "output_grad",
        flops // chunks,
        mine,
        theirs,
        gb,
        keep,
        send,
        aliases={4: 0, 5: 1},
    )


def finish_kernel(
    own, other, dq, dk, dv, square, residual, feed, small_keep, small_send,
    dx_out, qkv_out, expand_out, reduce_out, output_out, small_out,
    x, d, w, res, keep, send, twin_part, plane_got, line_part, line_got, around,
    feed_mine, feed_got, feed_around, to_twin, from_twin, ready,
    small_got, small_plane, small_line,
    loads, core_s, core_r, dx_s, dx_r, move_s, move_r, moved, plane_s, plane_r, line_s, line_r, ring_s, ring_r,
    feed_s, feed_r, feed_ring_s, feed_ring_r, small_s, small_r,
):
    r, s = lax.axis_index("rep"), lax.axis_index("shard")
    z, core = s // 2, s % 2
    half = dq.shape[1]
    rows = own.shape[0]
    block = rows // 2
    unit = qkv_out.shape[1]
    quarter = unit // 4
    nz = feed.shape[0]
    odd = r % 2
    home = r // 2 == core
    twin = (r, s ^ 1)
    plane = lambda k: (r ^ k, s)
    line = lambda k: (r, s ^ (2 * k))
    barrier = pltpu.get_barrier_semaphore()
    mesh_id = pl.DeviceIdType.MESH
    friends = [twin, (r ^ 2, s ^ 1), (r ^ 3, s ^ 1)] + [plane(k) for k in (1, 2, 3)]
    friends += [line(k) for k in range(1, nz)]
    for device in friends:
        pl.semaphore_signal(barrier, 1, device_id=device, device_id_type=mesh_id)
    pl.semaphore_wait(barrier, len(friends))

    def copy(source, target, sent, got, device):
        return pltpu.make_async_remote_copy(
            source, target, sent, got, device_id=device, device_id_type=mesh_id
        )

    local = [
        pltpu.make_async_copy(own, x.at[0], loads.at[0]),
        pltpu.make_async_copy(other, x.at[1], loads.at[1]),
        pltpu.make_async_copy(dq, d.at[0], loads.at[2]),
        pltpu.make_async_copy(dk, d.at[1], loads.at[3]),
        pltpu.make_async_copy(dv, d.at[2], loads.at[4]),
        pltpu.make_async_copy(residual, res, loads.at[5]),
        pltpu.make_async_copy(feed.at[z], feed_mine, loads.at[6]),
    ] + [
        pltpu.make_async_copy(
            square.at[:, pl.ds(m * unit, unit), pl.ds(pl.multiple_of(core * half, half), half)],
            w.at[m],
            loads.at[7 + m],
        )
        for m in range(3)
    ]
    for c in local:
        c.start()
    feed_line = [
        copy(feed.at[z ^ k], feed_got.at[k - 1], feed_s.at[k - 1], feed_r.at[k - 1], line(k))
        for k in range(1, nz)
    ]
    small_core = copy(small_send, small_got, small_s.at[0], small_r.at[0], twin)
    for c in feed_line + [small_core]:
        c.start()
    for c in local[:5]:
        c.wait()

    def cross(m):
        return copy(send.at[m], twin_part.at[m], core_s.at[m], core_r.at[m], twin)

    def spread(m, side, k):
        source = keep if side == 0 else twin_part
        return copy(
            source.at[m, r ^ k],
            plane_got.at[k - 1, m, side],
            plane_s.at[k - 1, m, side],
            plane_r.at[k - 1, m, side],
            plane(k),
        )

    mine, theirs = rows_at(core, rows), rows_at(1 - core, rows)

    def weight(m, carry):
        whole = dot_left(x[0], d[m, mine, :]) + dot_left(x[1], d[m, theirs, :])
        kept, sent = split_cores(core, whole.reshape(nz, 2, 4, quarter, half), 1)
        for part in range(4):
            keep[m, part] = kept[:, 0, part]
            send[m, part] = sent[:, 0, part]
        cross(m).start()
        for k in (1, 2, 3):
            spread(m, 0, k).start()
        return carry

    lax.fori_loop(0, 3, weight, 0)
    for c in local[7:]:
        c.wait()

    def share(at):
        total = dot_right(d[0, at, :], w[0].reshape(-1, half))
        for m in (1, 2):
            total = total + dot_right(d[m, at, :], w[m].reshape(-1, half))
        return total

    def give(t):
        return copy(to_twin.at[t], from_twin.at[t], dx_s.at[t], dx_r.at[t], twin)

    def away(t, carry):
        at = pl.ds(pl.multiple_of((1 - core) * rows + t * block, block), block)
        to_twin[t] = share(at).astype(BF16)
        give(t).start()
        return carry

    lax.fori_loop(0, 2, away, 0)

    def take(m, carry):
        cross(m).wait_recv()
        for k in (1, 2, 3):
            spread(m, 1, k).start()
        return carry

    lax.fori_loop(0, 3, take, 0)
    local[5].wait()

    def stay(turn):
        return pltpu.make_async_copy(ready.at[odd ^ turn], dx_out.at[odd], moved.at[turn])

    def leave(turn, device):
        return copy(ready.at[odd ^ turn], dx_out.at[odd], move_s.at[turn], move_r.at[turn], device)

    for turn in (0, 1):
        t = odd ^ turn
        at = pl.ds(pl.multiple_of(core * rows + t * block, block), block)
        total = share(at) + res[rows_at(t, block), :]
        give(t).wait_recv()
        ready[t] = (total + from_twin[t].astype(F32)).astype(BF16)
        if turn == 0:

            @pl.when(home)
            def _():
                stay(0).start()

            @pl.when(jnp.logical_not(home))
            def _():
                leave(0, (r ^ 2, s ^ 1)).start()

        else:

            @pl.when(home)
            def _():
                leave(1, (r ^ 1, s)).start()

            @pl.when(jnp.logical_not(home))
            def _():
                leave(1, (r ^ 3, s ^ 1)).start()

    small_core.wait()
    small_mine = small_keep[...] + small_got[...]
    small_got[...] = small_mine
    small_around = [
        copy(small_got, small_plane.at[k - 1], small_s.at[k], small_r.at[k], plane(k))
        for k in (1, 2, 3)
    ]
    for c in small_around:
        c.start()
    local[6].wait()
    total = feed_mine[...].astype(F32)
    for n, c in enumerate(feed_line):
        c.wait_recv()
        total = total + feed_got[n].astype(F32)
    feed_around[0] = total.astype(BF16)
    feed_ring = [
        copy(
            feed_around.at[0], feed_around.at[k], feed_ring_s.at[k - 1], feed_ring_r.at[k - 1], plane(k)
        )
        for k in (1, 2, 3)
    ]
    for c in feed_ring:
        c.start()
    small_total = small_mine
    for n, c in enumerate(small_around):
        c.wait()
        small_total = small_total + small_plane[n]
    small_got[...] = small_total
    small_along = [
        copy(small_got.at[z ^ k], small_line.at[k - 1], small_s.at[3 + k], small_r.at[3 + k], line(k))
        for k in range(1, nz)
    ]
    for c in small_along:
        c.start()
    for m in range(3):
        for side in (0, 1):
            source = keep if side == 0 else twin_part
            total = source[m, r].astype(F32)
            for k in (1, 2, 3):
                spread(m, side, k).wait_recv()
                total = total + plane_got[k - 1, m, side].astype(F32)
            for n in range(nz):
                line_part[n, m, side] = total[n].astype(BF16)
    qkv_line = [
        copy(line_part.at[z ^ k], line_got.at[k - 1], line_s.at[k - 1], line_r.at[k - 1], line(k))
        for k in range(1, nz)
    ]
    for c in qkv_line:
        c.start()
    total = line_part[z].astype(F32)
    for n, c in enumerate(qkv_line):
        c.wait_recv()
        total = total + line_got[n].astype(F32)
    around[0] = total.astype(BF16)
    qkv_ring = [
        copy(around.at[0], around.at[k], ring_s.at[k - 1], ring_r.at[k - 1], plane(k)) for k in (1, 2, 3)
    ]
    for c in qkv_ring:
        c.start()
    total = small_got[z]
    for n, c in enumerate(small_along):
        c.wait()
        total = total + small_line[n]
    small_out[...] = total
    width = qkv_out.shape[2]
    for k in range(4):
        if k > 0:
            feed_ring[k - 1].wait()
        part = r ^ k
        expand_out[:, rows_at(part, width)] = feed_around[k, :unit, :].astype(F32)
        reduce_out[rows_at(part, unit), :] = feed_around[k, unit : 2 * unit, :].astype(F32)
        output_out[rows_at(part, quarter), :] = feed_around[k, 2 * unit :, :].astype(F32)
    for k in range(4):
        if k > 0:
            qkv_ring[k - 1].wait()
        at = rows_at(r ^ k, quarter)
        qkv_out[:, at, rows_at(core, half)] = around[k, :, 0].astype(F32)
        qkv_out[:, at, rows_at(1 - core, half)] = around[k, :, 1].astype(F32)

    @pl.when(home)
    def _():
        stay(0).wait()
        leave(1, (r ^ 1, s)).wait()

    @pl.when(jnp.logical_not(home))
    def _():
        leave(0, (r ^ 2, s ^ 1)).wait()
        leave(1, (r ^ 3, s ^ 1)).wait()

    for c in feed_line + qkv_line:
        c.wait_send()
    for m in range(3):
        cross(m).wait_send()
        for side in (0, 1):
            for k in (1, 2, 3):
                spread(m, side, k).wait_send()
    for t in (0, 1):
        give(t).wait_send()


def finish(own, other, dq, dk, dv, square, residual, feed, small_keep, small_send, wide):
    rows, width = own.shape
    half = width // 2
    nz = feed.shape[0]
    unit = width // UNITS
    quarter = unit // 4
    block = rows // 2
    anywhere = pl.BlockSpec(memory_space=pl.ANY)
    vmem = pl.BlockSpec(memory_space=pltpu.VMEM)
    sems = lambda *shape: pltpu.SemaphoreType.DMA(shape)
    low = lambda *shape: pltpu.VMEM(shape, BF16)
    high = lambda *shape: pltpu.VMEM(shape, F32)
    part = (quarter, half)
    return pl.pallas_call(
        finish_kernel,
        out_shape=[
            jax.ShapeDtypeStruct((2, block, width), BF16),
            jax.ShapeDtypeStruct((3, unit, width), F32),
            jax.ShapeDtypeStruct((unit, wide), F32),
            jax.ShapeDtypeStruct((4 * unit, width), F32),
            jax.ShapeDtypeStruct((unit, width), F32),
            jax.ShapeDtypeStruct(small_keep.shape[1:], F32),
        ],
        in_specs=[anywhere] * 8 + [vmem] * 2,
        out_specs=[anywhere] + [vmem] * 5,
        scratch_shapes=[
            low(2, rows, width),
            low(3, 2 * rows, half),
            low(3, UNITS, unit, half),
            high(rows, width),
            low(3, 4, nz, *part),
            low(3, 4, nz, *part),
            low(3, 4, nz, *part),
            low(3, 3, 2, nz, *part),
            low(nz, 3, 2, *part),
            low(nz - 1, 3, 2, *part),
            low(4, 3, 2, *part),
            low(*feed.shape[1:]),
            low(nz - 1, *feed.shape[1:]),
            low(4, *feed.shape[1:]),
            low(2, block, width),
            low(2, block, width),
            low(2, block, width),
            high(*small_keep.shape),
            high(3, *small_keep.shape),
            high(nz - 1, *small_keep.shape[1:]),
            sems(10),
            sems(3),
            sems(3),
            sems(2),
            sems(2),
            sems(2),
            sems(2),
            sems(2),
            sems(3, 3, 2),
            sems(3, 3, 2),
            sems(nz - 1),
            sems(nz - 1),
            sems(3),
            sems(3),
            sems(nz - 1),
            sems(nz - 1),
            sems(3),
            sems(3),
            sems(3 + nz),
            sems(3 + nz),
        ],
        compiler_params=params(collective_id=1, has_side_effects=True),
        cost_estimate=pl.CostEstimate(
            flops=2 * 2 * 2 * rows * width * 3 * half, bytes_accessed=150 << 20, transcendentals=0
        ),
        name="finish",
    )(own, other, dq, dk, dv, square, residual, feed, small_keep, small_send)


def input_grad_kernel(core, own, other, d_ref, w_ref, dw, sums, dx_own, dx_other):
    part = pl.program_id(0)
    rows = own.shape[0]
    mine = pl.multiple_of(core[0] * rows, rows)
    theirs = pl.multiple_of((1 - core[0]) * rows, rows)
    d_own, d_other = d_ref[0, pl.ds(mine, rows), :], d_ref[0, pl.ds(theirs, rows), :]
    dw[0] = (dot_left(own[...], d_own) + dot_left(other[...], d_other)).astype(dw.dtype)
    sums[0] = jnp.broadcast_to(column_sum(d_own) + column_sum(d_other), sums.shape[1:])
    to_own, to_other = dot_right(d_own, stacked(w_ref)), dot_right(d_other, stacked(w_ref))

    @pl.when(part == 0)
    def _():
        dx_own[...] = to_own
        dx_other[...] = to_other

    @pl.when(part > 0)
    def _():
        dx_own[...] += to_own
        dx_other[...] += to_other


def input_grad(core, own, other, grads, weights, kind):
    rows, width = own.shape
    half = width // 2
    whole = lambda shape: pl.BlockSpec(shape, lambda i, *_: (0,) * len(shape))
    return pl.pallas_call(
        input_grad_kernel,
        out_shape=[
            jax.ShapeDtypeStruct((3, width, half), kind),
            jax.ShapeDtypeStruct((3, 8, half), F32),
            jax.ShapeDtypeStruct((rows, width), F32),
            jax.ShapeDtypeStruct((rows, width), F32),
        ],
        grid_spec=pltpu.PrefetchScalarGridSpec(
            num_scalar_prefetch=1,
            grid=(3,),
            in_specs=[
                whole((rows, width)),
                whole((rows, width)),
                pl.BlockSpec((1, 2 * rows, half), lambda i, core: (i, 0, 0)),
                pl.BlockSpec((UNITS, width // UNITS, half), lambda i, core: (0, i, core[0])),
            ],
            out_specs=[
                pl.BlockSpec((1, width, half), lambda i, core: (i, 0, 0)),
                pl.BlockSpec((1, 8, half), lambda i, core: (i, 0, 0)),
                whole((rows, width)),
                whole((rows, width)),
            ],
        ),
        compiler_params=params(),
        cost_estimate=pl.CostEstimate(
            flops=2 * 2 * 2 * rows * width * 3 * half, bytes_accessed=20 << 20, transcendentals=0
        ),
        name="input_grad",
    )(core, own, other, grads, weights)


def local(tokens, segment_ids, cotangent, *shards):
    rep_size, shard_size = lax.axis_size("rep"), lax.axis_size("shard")
    rep, shard = lax.axis_index("rep"), lax.axis_index("shard")
    core = shard % 2
    core_arg = core.reshape(1).astype(jnp.int32)
    width = tokens.shape[2]
    half = width // 2
    both = ("rep", "shard")

    def flat(r, s):
        return r * shard_size + s

    def route(k, back=False):
        pairs = []
        for r in range(rep_size):
            for s in range(shard_size):
                there = (flat(r, s), flat(2 * (s % 2) + (r + k) % 2, s - s % 2 + r // 2))
                pairs.append(there[::-1] if back else there)
        return pairs

    swap_pairs = [(flat(r, s), flat(r, s ^ 1)) for r in range(rep_size) for s in range(shard_size)]

    def swap(array):
        return lax.ppermute(array, both, swap_pairs)

    odd = rep % 2

    def to_sequences(array):
        a, b = array[0], array[1]
        even_part = lax.ppermute(jnp.where(odd == 0, a, b), both, route(0))
        odd_part = lax.ppermute(jnp.where(odd == 0, b, a), both, route(1))
        return jnp.concatenate(
            [jnp.where(odd == 0, even_part, odd_part), jnp.where(odd == 0, odd_part, even_part)]
        )

    def from_sequences(array):
        rows = array.shape[0] // 2
        a, b = array[:rows], array[rows:]
        even_part = lax.ppermute(jnp.where(odd == 0, a, b), both, route(0, True))
        odd_part = lax.ppermute(jnp.where(odd == 0, b, a), both, route(1, True))
        return jnp.stack(
            [jnp.where(odd == 0, even_part, odd_part), jnp.where(odd == 0, odd_part, even_part)]
        )

    tuned = rep_size == 4 and shard_size == UNITS
    rows_at = width // UNITS
    chunks = shards[4].shape[1] // width
    small = jnp.concatenate(shards[6:])
    if tuned:
        small_rows = jnp.concatenate([small, jnp.zeros((EXTRA * width - small.shape[0],), BF16)])
        square_own = jnp.concatenate(list(shards[:4]) + [small_rows.reshape(EXTRA, width)])
        wide_own = jnp.concatenate(
            [
                shards[4].reshape(rows_at, chunks, width).transpose(1, 0, 2),
                shards[5].reshape(chunks, rows_at, width),
            ],
            axis=1,
        )
        square, wide_all = gather_weights(square_own, wide_own, shard_size // 2)
        small = square[:, 4 * rows_at :, :].reshape(shard_size, EXTRA * width)
    else:
        wq, wk, wv, wo, we, wr = [lax.all_gather(m, "shard", axis=0, tiled=True) for m in shards[:6]]
        square = jnp.concatenate(
            [m.reshape(UNITS, rows_at, width) for m in (wq, wk, wv, wo)]
            + [jnp.zeros((UNITS, EXTRA, width), BF16)],
            axis=1,
        )
        wide_all = jnp.concatenate(
            [
                we.reshape(UNITS, rows_at, chunks, width).transpose(0, 2, 1, 3),
                wr.reshape(UNITS, chunks, rows_at, width),
            ],
            axis=2,
        )
        small = lax.all_gather(small[None], "shard", axis=0, tiled=True)
    vectors, at = [], 0
    for member in shards[6:]:
        n = member.shape[0]
        vectors.append(small[:, at : at + n].reshape(1, n * shard_size).astype(F32))
        at += n
    bq, bv, bo, be, br, gain1, shift1, gain2, shift2 = vectors

    own = to_sequences(tokens)
    cot = to_sequences(cotangent)
    other = swap(own)
    swapped_ids = swap(segment_ids)
    ids = jnp.where(rep // 2 == core, segment_ids, swapped_ids)
    segments = lax.dynamic_index_in_dim(ids, odd, 0, keepdims=False)
    blocks = segments.reshape(-1, BLOCK)
    begin = jnp.sum((segments[None, :] < blocks[:, :1]).astype(jnp.int32), axis=1)
    end = jnp.sum((segments[None, :] <= blocks[:, -1:]).astype(jnp.int32), axis=1)
    seg_col = segments[:, None]

    q, k, v = project(core_arg, own, other, square, bq, bv)
    attended, lse = attend(begin, end, q, k, v, seg_col)
    rows = own.shape[0]
    mine = lax.dynamic_slice_in_dim(attended, core * rows, rows)
    theirs = swap(lax.dynamic_slice_in_dim(attended, (1 - core) * rows, rows))
    table = jnp.concatenate([bo, br, gain1, shift1, gain2, shift2, bo, bo])
    out, ga_mine, ga_theirs, residual, act, ge, first_low, gr, gb, sums, sum_e = row_local(
        core_arg, own, mine, theirs, cot, square, wide_all, table, be
    )
    ga_other = swap(ga_theirs)
    if not tuned:
        dwr = weight_grad(act, gr, F32)
        dwe = weight_grad(first_low, ge, F32)
        dwo_mine, dwo_theirs = weight_grad(mine, gb, F32), weight_grad(theirs, gb, F32)
        dq, dk, dv, sum_qv = attend_back(
            core_arg, begin, end, q, k, v, attended, ga_mine, ga_other, lse, seg_col
        )
        dw, sum_qkv, dx_own, dx_other = input_grad(
            core_arg, own, other, jnp.stack([dq, dk, dv]), square, F32
        )
        dx = (residual + dx_own + swap(dx_other.astype(BF16)).astype(F32)).astype(BF16)

        def place(part, dim):
            zero = jnp.zeros_like(part)
            return jnp.where(
                core == 0,
                jnp.concatenate([part, zero], axis=dim),
                jnp.concatenate([zero, part], axis=dim),
            )

        dwo = jnp.where(
            core == 0,
            jnp.concatenate([dwo_mine, dwo_theirs]),
            jnp.concatenate([dwo_theirs, dwo_mine]),
        )
        totals = (
            place(dw[0], 1),
            place(dw[1], 1),
            place(dw[2], 1),
            dwo,
            dwe,
            dwr,
            place(sum_qkv[0, 0], 0),
            place(sum_qkv[2, 0], 0),
            sums[0],
            sum_e[0],
            sums[1],
            sums[2],
            sums[3],
            sums[4],
            sums[5],
        )
        summed = lax.psum_scatter(totals, "shard", scatter_dimension=0, tiled=True)
        final = [part.astype(F32) for part in lax.psum([p.astype(BF16) for p in summed], "rep")]
        return (from_sequences(out), from_sequences(dx)) + tuple(final)

    nz = shard_size // 2

    def plane_send(array, hop):
        pairs = [(flat(r, s), flat(r ^ hop, s)) for r in range(4) for s in range(shard_size)]
        return lax.ppermute(array, both, pairs)

    def pick(array, n):
        return lax.dynamic_index_in_dim(array, n, 0, keepdims=False)

    feed_keep, feed_send = feed_grads(core_arg, first_low, ge, act, gr, mine, theirs, gb)
    feed_got = swap(feed_send)
    feed_parts = [
        pick(feed_keep, rep ^ hop).astype(F32) + pick(feed_got, rep ^ hop).astype(F32)
        for hop in range(4)
    ]
    feed_sent = [part.astype(BF16) for part in feed_parts[1:]]
    feed_sent, ga_other = lax.optimization_barrier((feed_sent, ga_other))
    feed = feed_parts[0]
    for hop in (1, 2, 3):
        feed = feed + plane_send(feed_sent[hop - 1], hop).astype(F32)
    feed = feed.astype(BF16)
    dq, dk, dv, sum_qv = attend_back(
        core_arg, begin, end, q, k, v, attended, ga_mine, ga_other, lse, seg_col
    )
    unit = width // shard_size
    wide_unit = sum_e.shape[1] // shard_size

    def place(part):
        zero = jnp.zeros_like(part)
        return jnp.where(
            core == 0, jnp.concatenate([part, zero]), jnp.concatenate([zero, part])
        )

    rows_of = [place(sum_qv[0, 0]), place(sum_qv[1, 0])] + [sums[n] for n in range(6)]
    table = jnp.concatenate(
        [vector.reshape(shard_size, unit) for vector in rows_of]
        + [
            sum_e.reshape(shard_size, wide_unit),
            jnp.zeros((shard_size, 8 * 256 - 8 * unit - wide_unit), F32),
        ],
        axis=1,
    ).reshape(nz, 2, 8, 256)
    small_keep = lax.dynamic_index_in_dim(table, core, 1, keepdims=False)
    small_send = lax.dynamic_index_in_dim(table, 1 - core, 1, keepdims=False)
    dx, dqkv, dwe, dwr, dwo, small = finish(
        own, other, dq, dk, dv, square, residual, feed, small_keep, small_send, be.shape[1]
    )
    small = small.reshape(-1)
    dbq, dbv, dbo, dbr, dg1, ds1, dg2, ds2 = [small[n * unit : (n + 1) * unit] for n in range(8)]
    dbe = small[8 * unit : 8 * unit + wide_unit]
    return (
        from_sequences(out),
        dx,
        dqkv[0],
        dqkv[1],
        dqkv[2],
        dwo,
        dwe,
        dwr,
        dbq,
        dbv,
        dbo,
        dbe,
        dbr,
        dg1,
        ds1,
        dg2,
        ds2,
    )


def solution(mesh):
    row = P("shard", "rep", None)
    in_specs = (row, P("shard", None), row) + (P("shard", None),) * 6 + (P("shard"),) * 9
    out_specs = (row, row) + (P("shard", None),) * 6 + (P("shard"),) * 9
    return jax.shard_map(local, mesh=mesh, in_specs=in_specs, out_specs=out_specs, check_vma=False)
```

```python
import functools
import math

import jax
import jax.numpy as jnp
from jax import lax
from jax.experimental import pallas as pl
from jax.experimental.pallas import tpu as pltpu
from jax.sharding import PartitionSpec as P

HEAD_DIM = 64
BLOCK = 256
KEYS = 512
PREPARE = 512
DOCS = 8
ROWS = 256
WIDE_ROWS = 512
MASKED = -1e30
EPS = 1e-05
UNITS = 8
EXTRA = 8
SCALE = HEAD_DIM**-0.5
SCALE2 = SCALE * math.log2(math.e)
GELU_A = math.sqrt(2.0 / math.pi)
GELU_B = 0.044715
F32 = jnp.float32
BF16 = jnp.bfloat16
VMEM_LIMIT = 60 * 1024 * 1024


def dot(left, right):
    return jnp.dot(left, right, preferred_element_type=F32)


def dot_right(left, right):
    return lax.dot_general(left, right, (((1,), (1,)), ((), ())), preferred_element_type=F32)


def dot_left(left, right):
    return lax.dot_general(left, right, (((0,), (0,)), ((), ())), preferred_element_type=F32)


def params(**more):
    return pltpu.CompilerParams(vmem_limit_bytes=VMEM_LIMIT, **more)


def stacked(ref):
    return ref[...].reshape(-1, ref.shape[-1])


def gather_kernel(
    nz, wq, wk, wv, wo, expand, reduce, small, tokens, cotangent, ids,
    square_all, wide_all, own, other, cot, segments,
    z_send, z_recv, p_send, p_recv, c_send, c_recv, own_send, own_recv, copied,
    row_send, row_recv, row_kept, twin_send, twin_recv, id_sems,
    square_here, wide_here, rows_here, ids_here, brought,
):
    r, s = lax.axis_index("rep"), lax.axis_index("shard")
    z, core = s // 2, s % 2
    odd = r % 2
    home = r // 2 == core
    twin = (r, s ^ 1)
    barrier = pltpu.get_barrier_semaphore()
    mesh_id = pl.DeviceIdType.MESH

    def greet(device):
        pl.semaphore_signal(barrier, 1, device_id=device, device_id_type=mesh_id)

    for device in [twin, (r ^ 2, s ^ 1), (r ^ 3, s ^ 1)] + [(r ^ k, s) for k in (1, 2, 3)]:
        greet(device)
    for step in (1, -1):

        @pl.when((z + step >= 0) & (z + step < nz))
        def _(step=step):
            greet((r, s + 2 * step))

    pl.semaphore_wait(barrier, 6 + jnp.where(z > 0, 1, 0) + jnp.where(z < nz - 1, 1, 0))

    def copy(source, target, sent, got, device):
        return pltpu.make_async_remote_copy(
            source, target, sent, got, device_id=device, device_id_type=mesh_id
        )

    block = tokens.shape[1]
    unit, width = wq.shape
    square, wide = square_here, wide_here
    pairs = [(small, square.at[pl.ds(4 * unit, EXTRA)])]
    pairs += [(m, square.at[pl.ds(n * unit, unit)]) for n, m in enumerate((wq, wk, wv, wo))]
    for n in range(wide.shape[0]):
        pairs.append((expand.at[:, pl.ds(n * width, width)], wide.at[n, pl.ds(0, unit)]))
        pairs.append((reduce.at[pl.ds(n * unit, unit)], wide.at[n, pl.ds(unit, unit)]))
    weights = len(pairs)
    pairs.append((tokens.at[odd], rows_here.at[0]))
    pairs.append((cotangent.at[odd], rows_here.at[1]))
    pairs.append((ids.at[odd], ids_here))
    fetched = [
        pltpu.make_async_copy(source, target, brought.at[n])
        for n, (source, target) in enumerate(pairs)
    ]
    kept = [
        pltpu.make_async_copy(square_here, square_all.at[s], copied.at[0]),
        pltpu.make_async_copy(wide_here, wide_all.at[s], copied.at[1]),
    ]
    mine = [
        copy(square, square_all.at[s], own_send.at[0], own_recv.at[0], twin),
        copy(wide, wide_all.at[s], own_send.at[1], own_recv.at[1], twin),
    ]

    def onward(n, d, part):
        step = 1 - 2 * n
        at = s - 2 * step * d
        if part == 0:
            source = square if d == 0 else square_all.at[at]
            target = square_all.at[at]
        else:
            source = wide.at[r] if d == 0 else wide_all.at[at, r]
            target = wide_all.at[at, r]
        return copy(source, target, z_send.at[n, d, part], z_recv.at[n, d, part], (r, s + 2 * step))

    turns = [(0, 0, 1), (0, 0, 2), (0, 1, 2), (1, 0, 2), (1, 0, 1), (1, 2, 1)]

    def sideways(n, d, which):
        at = s - 2 * (1 - 2 * n) * d
        half, whose, to = turns[which]
        part = wide_all.at[at, r ^ whose, pl.ds(half * unit, unit)]
        return copy(
            part, part, p_send.at[n, d - 1, which], p_recv.at[n, d - 1, which], (r ^ to, s)
        )

    def across(n, d, k):
        at = s - 2 * (1 - 2 * n) * d
        part = square_all.at[at] if k == 4 else wide_all.at[at, r ^ k]
        return copy(part, part, c_send.at[n, d - 1, k], c_recv.at[n, d - 1, k], twin)

    def has(n, d):
        at = z - (1 - 2 * n) * d
        return (at >= 0) & (at < nz)

    def goes(n):
        at = z + 1 - 2 * n
        return (at >= 0) & (at < nz)

    def stay(target, which):
        at = pl.ds(pl.multiple_of(odd * block, block), block)
        return pltpu.make_async_copy(rows_here.at[which], target.at[at], row_kept.at[which])

    def move(source, target, which, turn, device):
        at = pl.ds(pl.multiple_of(odd * block, block), block)
        return copy(
            source.at[odd ^ turn],
            target.at[at],
            row_send.at[which, turn],
            row_recv.at[which, turn],
            device,
        )

    def rows_act(source, target, which, act_kept, act_moved):
        @pl.when(home)
        def _():
            if act_kept:
                act_kept(stay(target, which))
            act_moved(move(source, target, which, 1, (r ^ 1, s)))

        @pl.when(jnp.logical_not(home))
        def _():
            act_moved(move(source, target, which, 0, (r ^ 2, s ^ 1)))
            act_moved(move(source, target, which, 1, (r ^ 3, s ^ 1)))

    begin = lambda c: c.start()
    for c in fetched:
        c.start()
    rows_act(tokens, own, 0, None, begin)
    for c in fetched[:weights]:
        c.wait()
    for n in (0, 1):

        @pl.when(goes(n))
        def _(n=n):
            onward(n, 0, 1).start()
            onward(n, 0, 0).start()

    id_kept = pltpu.make_async_copy(ids_here, segments, id_sems.at[0])
    id_sent = copy(ids.at[odd], segments, id_sems.at[1], id_sems.at[2], twin)

    @pl.when(home)
    def _():
        id_sent.start()

    for c in mine + kept:
        c.start()
    for c in fetched[weights:]:
        c.wait()

    @pl.when(home)
    def _():
        id_kept.start()
        stay(own, 0).start()
        stay(cot, 1).start()

    def arrivals(d):
        for n in (0, 1):

            @pl.when(has(n, d))
            def _(n=n):
                onward(n, d - 1, 1).wait_recv()
                if d < nz - 1:

                    @pl.when(goes(n))
                    def _():
                        onward(n, d, 1).start()

                for which in (0, 3, 1, 4):
                    sideways(n, d, which).start()
                across(n, d, 0).start()
                onward(n, d - 1, 0).wait_recv()
                if d < nz - 1:

                    @pl.when(goes(n))
                    def _():
                        onward(n, d, 0).start()

                across(n, d, 4).start()

    def hand_on(turn):
        at = pl.ds(pl.multiple_of((odd ^ turn) * block, block), block)
        return copy(own.at[at], other.at[at], twin_send.at[turn], twin_recv.at[turn], twin)

    def relays(d):
        for n in (0, 1):

            @pl.when(has(n, d))
            def _(n=n):
                sideways(n, d, 0).wait_recv()
                sideways(n, d, 2).start()
                sideways(n, d, 3).wait_recv()
                sideways(n, d, 5).start()
                sideways(n, d, 4).wait_recv()
                across(n, d, 1).start()
                sideways(n, d, 1).wait_recv()
                across(n, d, 2).start()

    arrivals(1)

    @pl.when(home)
    def _():
        stay(own, 0).wait()

    @pl.when(jnp.logical_not(home))
    def _():
        move(tokens, own, 0, 0, (r ^ 2, s ^ 1)).wait_recv()

    hand_on(0).start()
    move(tokens, own, 0, 1, (r ^ 1, s)).wait_recv()
    hand_on(1).start()
    relays(1)
    rows_act(cotangent, cot, 1, None, begin)
    for d in range(2, nz):
        arrivals(d)
        relays(d)
    for d in range(1, nz):
        for n in (0, 1):

            @pl.when(has(n, d))
            def _(n=n, d=d):
                sideways(n, d, 2).wait_recv()
                sideways(n, d, 5).wait_recv()
                across(n, d, 3).start()

    def sent(c):
        c.wait_send()

    rows_act(tokens, own, 0, None, sent)
    rows_act(cotangent, cot, 1, lambda c: c.wait(), lambda c: c.wait())
    for c in mine + kept + [hand_on(0), hand_on(1)]:
        c.wait()

    @pl.when(home)
    def _():
        id_kept.wait()
        id_sent.wait_send()

    @pl.when(jnp.logical_not(home))
    def _():
        id_sent.wait_recv()

    for n in (0, 1):

        @pl.when(goes(n))
        def _(n=n):
            onward(n, 0, 1).wait_send()
            onward(n, 0, 0).wait_send()

    for d in range(1, nz):
        for n in (0, 1):

            @pl.when(has(n, d))
            def _(n=n, d=d):
                for which in range(6):
                    sideways(n, d, which).wait_send()
                for k in range(5):
                    across(n, d, k).wait()
                if d < nz - 1:

                    @pl.when(goes(n))
                    def _():
                        onward(n, d, 1).wait_send()
                        onward(n, d, 0).wait_send()


def gather(matrices, small, tokens, cotangent, ids, nz):
    anywhere = pl.BlockSpec(memory_space=pl.ANY)
    sems = lambda *shape: pltpu.SemaphoreType.DMA(shape)
    unit, width = matrices[0].shape
    chunks = matrices[4].shape[1] // width
    square, wide = (4 * unit + EXTRA, width), (chunks, 2 * unit, width)
    rows = jax.ShapeDtypeStruct((2 * tokens.shape[1], tokens.shape[2]), BF16)
    return pl.pallas_call(
        functools.partial(gather_kernel, nz),
        out_shape=[
            jax.ShapeDtypeStruct((2 * nz,) + square, BF16),
            jax.ShapeDtypeStruct((2 * nz,) + wide, BF16),
            rows,
            rows,
            rows,
            jax.ShapeDtypeStruct(ids.shape[1:], jnp.int32),
        ],
        in_specs=[anywhere] * 10,
        out_specs=[anywhere] * 6,
        scratch_shapes=[
            sems(2, nz - 1, 2),
            sems(2, nz - 1, 2),
            sems(2, nz - 1, 6),
            sems(2, nz - 1, 6),
            sems(2, nz - 1, 5),
            sems(2, nz - 1, 5),
            sems(2),
            sems(2),
            sems(2),
            sems(2, 2),
            sems(2, 2),
            sems(2),
            sems(2),
            sems(2),
            sems(3),
            pltpu.VMEM(square, BF16),
            pltpu.VMEM(wide, BF16),
            pltpu.VMEM((2,) + tokens.shape[1:], BF16),
            pltpu.VMEM(ids.shape[1:], jnp.int32),
            sems(8 + 2 * chunks),
        ],
        compiler_params=params(collective_id=0, has_side_effects=True),
        cost_estimate=pl.CostEstimate(flops=0, bytes_accessed=150 << 20, transcendentals=0),
        name="gather",
    )(*matrices, small, tokens, cotangent, ids)


def qkv_kernel(core, own, other, wq, wk, wv, vectors, q_out, k_out, v_out):
    per_core = pl.num_programs(0) // 2
    mine = pl.program_id(0) // per_core == core[0]
    rows = jnp.where(mine, own[...], other[...])
    q_out[...] = (dot(rows, stacked(wq)) + vectors[0:1, :]).astype(BF16)
    k_out[...] = dot(rows, stacked(wk)).astype(BF16)
    v_out[...] = (dot(rows, stacked(wv)) + vectors[1:2, :]).astype(BF16)


def project(core, own, other, square, vectors):
    rows, width = own.shape
    half = width // 2
    steps = rows // WIDE_ROWS

    def side(flip):
        def index(i, core):
            first = jnp.where(core[0] == flip, 0, steps)
            return (jnp.clip(i - first, 0, steps - 1), 0)

        return index

    weight = lambda m: pl.BlockSpec(
        (UNITS, width // UNITS, half), lambda i, core: (0, m, core[0])
    )
    bias = pl.BlockSpec((8, half), lambda i, core: (0, core[0]))
    result = pl.BlockSpec((WIDE_ROWS, half), lambda i, core: (i, 0))
    return pl.pallas_call(
        qkv_kernel,
        out_shape=[jax.ShapeDtypeStruct((2 * rows, half), BF16)] * 3,
        grid_spec=pltpu.PrefetchScalarGridSpec(
            num_scalar_prefetch=1,
            grid=(2 * steps,),
            in_specs=[
                pl.BlockSpec((WIDE_ROWS, width), side(0)),
                pl.BlockSpec((WIDE_ROWS, width), side(1)),
                weight(0),
                weight(1),
                weight(2),
                bias,
            ],
            out_specs=[result] * 3,
        ),
        compiler_params=params(),
        cost_estimate=pl.CostEstimate(
            flops=2 * 2 * rows * width * 3 * half, bytes_accessed=10 << 20, transcendentals=0
        ),
        name="project",
    )(core, own, other, square, square, square, vectors)


def halves(pair):
    lane = lax.broadcasted_iota(jnp.int32, pair.shape, 1)
    zero = jnp.zeros_like(pair)
    return jnp.where(lane < HEAD_DIM, pair, zero), jnp.where(lane < HEAD_DIM, zero, pair)


def rows_at(n, size):
    return pl.ds(pl.multiple_of(n * size, size), size)


def widen(pair, extra):
    lane = lax.broadcasted_iota(jnp.int32, pair.shape, 1)
    return jnp.where(lane < HEAD_DIM, pair, extra[0]), jnp.where(lane < HEAD_DIM, extra[1], pair)


def same_document(ids, extra_lanes):
    size = ids.shape[1]
    number = lax.broadcasted_iota(jnp.int32, (2 * DOCS, size), 0)
    hit = jnp.where(number == ids, 1.0, 0.0).astype(BF16)
    lane = lax.broadcasted_iota(jnp.int32, (2 * DOCS, 2 * HEAD_DIM), 1) % HEAD_DIM
    spread = lane == lax.broadcasted_iota(jnp.int32, (2 * DOCS, 2 * HEAD_DIM), 0)
    for_queries = dot_left(hit, jnp.where(spread, 1.0, 0.0).astype(BF16))
    slot = lax.broadcasted_iota(jnp.int32, (size, 2 * HEAD_DIM), 1) % HEAD_DIM
    for_keys = jnp.where(
        (slot < DOCS) & (for_queries == 0.0),
        MASKED,
        jnp.where((slot >= DOCS) & (slot < DOCS + extra_lanes), 1.0, 0.0),
    )
    return for_queries, for_keys.astype(BF16)


def attend_kernel(low, high, q_ref, k_ref, v_ref, segments, out, lse, qx, kx, v_turned, top, mix, kept):
    rows, width = q_ref.shape
    heads = width // HEAD_DIM
    pairs = heads // 2
    for at in range(0, rows, PREPARE):
        part = pl.ds(at, PREPARE)
        for_queries, for_keys = same_document(segments[:, part], 0)
        for_queries = for_queries.astype(BF16)
        for pair in range(pairs):
            cols = pl.ds(pair * 2 * HEAD_DIM, 2 * HEAD_DIM)
            both = slice(2 * pair, 2 * pair + 2)
            qx[both, part, :] = jnp.stack(widen(q_ref[part, cols], (for_queries, for_queries)))
            kx[both, part, :] = jnp.stack(widen(k_ref[part, cols], (for_keys, for_keys)))
            v_turned[both, :HEAD_DIM, part] = v_ref[part, cols].T.reshape(2, HEAD_DIM, PREPARE)
    v_turned[:, HEAD_DIM:, :] = jnp.ones_like(v_turned[:, HEAD_DIM:, :])

    @pl.loop(0, rows // BLOCK)
    def _(qb):
        q_rows = rows_at(qb, BLOCK)
        top[...] = jnp.full_like(top, MASKED)
        mix[...] = jnp.zeros_like(mix)

        def score(kb, carry):
            k_rows = rows_at(kb, KEYS)
            for h in range(heads):
                scores = dot_right(kx[h, k_rows, :], qx[h, q_rows, :])
                kept[h, k_rows, :] = scores
                top[h] = jnp.maximum(top[h], jnp.max(scores.reshape(KEYS // 8, 8, BLOCK), axis=0))
            return carry

        lax.fori_loop(low[qb], high[qb], score, 0)
        tops = [jnp.max(top[h], axis=0, keepdims=True) * SCALE2 for h in range(heads)]

        def weigh(kb, carry):
            k_rows = rows_at(kb, KEYS)
            for h in range(heads):
                weight = jnp.exp2(kept[h, k_rows, :] * SCALE2 - tops[h]).astype(BF16)
                mix[h] += dot(v_turned[h, :, k_rows], weight)
            return carry

        lax.fori_loop(low[qb], high[qb], weigh, 0)
        for h in range(heads):
            total = mix[h, HEAD_DIM : HEAD_DIM + 1, :]
            lse[pl.ds(h, 1), q_rows] = tops[h] + jnp.log2(total)
            mix[h, :HEAD_DIM, :] = mix[h, :HEAD_DIM, :] / total
        for pair in range(pairs):
            both = mix[2 * pair : 2 * pair + 2, :HEAD_DIM, :].reshape(2 * HEAD_DIM, BLOCK)
            out[q_rows, pl.ds(pair * 2 * HEAD_DIM, 2 * HEAD_DIM)] = both.T.astype(BF16)


def spans(begin, end, size):
    return begin // size, (end + size - 1) // size


def attend(begin, end, q, k, v, segments):
    rows, width = q.shape
    heads = width // HEAD_DIM
    whole = lambda shape: pl.BlockSpec(shape, lambda i, *_: (0,) * len(shape))
    wide = pltpu.VMEM((heads, rows, 2 * HEAD_DIM), BF16)
    return pl.pallas_call(
        attend_kernel,
        out_shape=[
            jax.ShapeDtypeStruct((rows, width), BF16),
            jax.ShapeDtypeStruct((heads, rows), F32),
        ],
        grid_spec=pltpu.PrefetchScalarGridSpec(
            num_scalar_prefetch=2,
            grid=(1,),
            in_specs=[whole((rows, width))] * 3 + [whole((1, rows))],
            out_specs=[whole((rows, width)), whole((heads, rows))],
            scratch_shapes=[
                wide,
                wide,
                pltpu.VMEM((heads, HEAD_DIM + 16, rows), BF16),
                pltpu.VMEM((heads, 8, BLOCK), F32),
                pltpu.VMEM((heads, HEAD_DIM + 16, BLOCK), F32),
                pltpu.VMEM((heads, rows, BLOCK), F32),
            ],
        ),
        compiler_params=params(),
        cost_estimate=pl.CostEstimate(
            flops=4 * rows * rows * width,
            bytes_accessed=8 << 20,
            transcendentals=rows * rows * heads // 2,
        ),
        name="attend",
    )(*spans(begin, end, KEYS), q, k, v, segments)


def three_parts(values):
    first = values.astype(BF16)
    rest = values - first.astype(F32)
    second = rest.astype(BF16)
    return first, second, (rest - second.astype(F32)).astype(BF16)


def attend_back_kernel(
    core, low, high, q_ref, k_ref, v_ref, out_ref, own, other, lse, segments,
    dq_out, dk_out, dv_out, sums, grad, qx, kx, vx, gx, dq, dk, dv, weights, slopes,
):
    rows, width = q_ref.shape
    heads = width // HEAD_DIM
    pairs = heads // 2
    lanes = 2 * HEAD_DIM
    per_core = own.shape[0]
    grad[rows_at(core[0], per_core), :] = own[...]
    grad[rows_at(1 - core[0], per_core), :] = other[...]
    source = lax.broadcasted_iota(jnp.int32, (24, heads * lanes), 0)
    lane = lax.broadcasted_iota(jnp.int32, (24, heads * lanes), 1)
    place = jnp.where(
        (source % 8 == lane // lanes)
        & (lane % HEAD_DIM == DOCS + source // 8)
        & ((lane % lanes) // HEAD_DIM != (lane // lanes) % 2),
        1.0,
        0.0,
    ).astype(BF16)
    picks = jnp.where(
        lax.broadcasted_iota(jnp.int32, (width, 8), 0) // HEAD_DIM
        == lax.broadcasted_iota(jnp.int32, (width, 8), 1),
        1.0,
        0.0,
    ).astype(BF16)
    for at in range(0, rows, PREPARE):
        part = pl.ds(at, PREPARE)
        for_queries, for_keys = same_document(segments[:, part], 3)
        ones = jnp.where(for_keys == 1.0, for_keys, jnp.zeros_like(for_keys))
        level = jnp.concatenate(
            [lse[:, part] * (-1.0 / SCALE2), jnp.zeros((8 - heads, PREPARE), F32)]
        )
        levels = dot_left(jnp.concatenate(three_parts(level)), place)
        both = grad[part, :].astype(F32) * out_ref[part, :].astype(F32)
        coarse = both.astype(BF16)
        fine = (both - coarse.astype(F32)).astype(BF16)
        delta = dot(coarse, picks) + dot(fine, picks)
        deltas = dot(jnp.concatenate(three_parts(-delta), 1), place).astype(BF16)
        for pair in range(pairs):
            cols = pl.ds(pair * lanes, lanes)
            sides = slice(2 * pair, 2 * pair + 2)
            one, two = [slice((2 * pair + e) * lanes, (2 * pair + e + 1) * lanes) for e in (0, 1)]
            marks = [(for_queries + levels[:, side]).astype(BF16) for side in (one, two)]
            qx[sides, part, :] = jnp.stack(widen(q_ref[part, cols], marks))
            kx[sides, part, :] = jnp.stack(widen(k_ref[part, cols], (for_keys, for_keys)))
            vx[sides, part, :] = jnp.stack(widen(v_ref[part, cols], (ones, ones)))
            gx[sides, part, :] = jnp.stack(widen(grad[part, cols], (deltas[:, one], deltas[:, two])))

    dq[...] = jnp.zeros_like(dq)

    @pl.loop(0, rows // BLOCK)
    def _(kb):
        k_rows = rows_at(kb, BLOCK)
        dk[...] = jnp.zeros_like(dk)
        dv[...] = jnp.zeros_like(dv)

        def step(qb, carry):
            q_rows = rows_at(qb, BLOCK)
            for h in range(heads):
                probs = jnp.exp2(dot_right(kx[h, k_rows, :], qx[h, q_rows, :]) * SCALE2)
                weights[h] = probs.astype(BF16)
                centred = dot_right(vx[h, k_rows, :], gx[h, q_rows, :])
                slopes[h] = (probs * centred).astype(BF16)
            for pair in range(pairs):
                cols = pl.ds(pair * lanes, lanes)
                slope = [slopes[2 * pair], slopes[2 * pair + 1]]
                weight = [weights[2 * pair], weights[2 * pair + 1]]
                dq[q_rows, cols] += dot_left(
                    jnp.concatenate(slope, 0), jnp.concatenate(halves(k_ref[k_rows, cols]), 0)
                )
                dk[:, cols] += dot(
                    jnp.concatenate(slope, 1), jnp.concatenate(halves(q_ref[q_rows, cols]), 0)
                )
                dv[:, cols] += dot(
                    jnp.concatenate(weight, 1), jnp.concatenate(halves(grad[q_rows, cols]), 0)
                )
            return carry

        lax.fori_loop(low[kb], high[kb], step, 0)
        dk_out[k_rows, :] = (dk[...] * SCALE).astype(BF16)
        dv_out[k_rows, :] = dv[...].astype(BF16)

    dq_out[...] = (dq[...] * SCALE).astype(BF16)
    ones = jnp.ones((8, rows), BF16)
    sums[0] = dot(ones, dq_out[...])
    sums[1] = dot(ones, dv_out[...])


def attend_back(core, begin, end, q, k, v, out, own, other, lse, segments):
    rows, width = q.shape
    heads = width // HEAD_DIM
    whole = lambda shape: pl.BlockSpec(shape, lambda i, *_: (0,) * len(shape))
    wide = pltpu.VMEM((heads, rows, 2 * HEAD_DIM), BF16)
    return pl.pallas_call(
        attend_back_kernel,
        out_shape=[jax.ShapeDtypeStruct((rows, width), BF16)] * 3
        + [jax.ShapeDtypeStruct((2, 8, width), F32)],
        grid_spec=pltpu.PrefetchScalarGridSpec(
            num_scalar_prefetch=3,
            grid=(1,),
            in_specs=[whole((rows, width))] * 4
            + [whole((rows // 2, width))] * 2
            + [whole((heads, rows)), whole((1, rows))],
            out_specs=[whole((rows, width))] * 3 + [whole((2, 8, width))],
            scratch_shapes=[
                pltpu.VMEM((rows, width), BF16),
                wide,
                wide,
                wide,
                wide,
                pltpu.VMEM((rows, width), F32),
                pltpu.VMEM((BLOCK, width), F32),
                pltpu.VMEM((BLOCK, width), F32),
                pltpu.VMEM((heads, BLOCK, BLOCK), BF16),
                pltpu.VMEM((heads, BLOCK, BLOCK), BF16),
            ],
        ),
        compiler_params=params(),
        cost_estimate=pl.CostEstimate(
            flops=10 * rows * rows * width,
            bytes_accessed=16 << 20,
            transcendentals=rows * rows * heads // 2,
        ),
        name="attend_back",
    )(core, *spans(begin, end, BLOCK), q, k, v, out, own, other, lse, segments)


def row_mean(values):
    return jnp.mean(values, axis=-1, keepdims=True)


def norm(values):
    centre = values - row_mean(values)
    scale = lax.rsqrt(row_mean(centre * centre) + EPS)
    return centre * scale, scale


def norm_back(normed, scale, gain, grad):
    inner = grad * gain
    return scale * (inner - row_mean(inner) - normed * row_mean(inner * normed))


def column_sum(values):
    return jnp.sum(values.astype(F32), axis=0, keepdims=True)


def rows_kernel(
    core, x_ref, mine, theirs, cot, wo_mine_ref, wo_theirs_ref, wide_ref, vectors, be,
    out, ga_mine, ga_theirs, residual, act, ge, low_out, gr_out, gb_out, sums, sum_e, slope,
):
    width = x_ref.shape[1]
    chunks = slope.shape[1] // width
    unit = width // UNITS
    each = UNITS // chunks
    we = lambda j: wide_ref[:, j, :unit, :].reshape(width, width)
    wr = lambda j: wide_ref[each * j : each * (j + 1), :, unit:, :].reshape(width, width)
    bo, br = vectors[2:3, :], vectors[3:4, :]
    gain1, shift1, gain2, shift2 = [vectors[n : n + 1, :] for n in range(4, 8)]
    wo_mine, wo_theirs = stacked(wo_mine_ref), stacked(wo_theirs_ref)

    @pl.when(pl.program_id(0) == 0)
    def _():
        sums[...] = jnp.zeros_like(sums)
        sum_e[...] = jnp.zeros_like(sum_e)

    branch = dot(mine[...], wo_mine) + dot(theirs[...], wo_theirs) + bo
    normed1, scale1 = norm(x_ref[...].astype(F32) + branch)
    first = normed1 * gain1 + shift1
    first_low = first.astype(BF16)
    low_out[...] = first_low
    reduced = jnp.zeros_like(first)
    for j in range(chunks):
        cols = slice(j * width, (j + 1) * width)
        u = dot(first_low, we(j)) + be[:, cols]
        square = u * u
        curve = jnp.tanh(GELU_A * (u + GELU_B * (square * u)))
        cdf = 0.5 * (1.0 + curve)
        slope[:, cols] = cdf + (0.5 * GELU_A) * u * (1.0 - curve * curve) * (
            1.0 + (3.0 * GELU_B) * square
        )
        activated = (u * cdf).astype(BF16)
        act[:, cols] = activated
        reduced += dot(activated, wr(j))
    normed2, scale2 = norm(first + (reduced + br))
    out[...] = (normed2 * gain2 + shift2).astype(BF16)

    incoming = cot[...].astype(F32)
    grad_second = norm_back(normed2, scale2, gain2, incoming)
    grad_reduced = grad_second.astype(BF16)
    gr_out[...] = grad_reduced
    grad_first = grad_second
    for j in range(chunks):
        cols = slice(j * width, (j + 1) * width)
        grad_expanded = (dot_right(grad_reduced, wr(j)) * slope[:, cols]).astype(BF16)
        ge[:, cols] = grad_expanded
        sum_e[:, cols] += column_sum(grad_expanded)
        grad_first += dot_right(grad_expanded, we(j))
    grad_residual = norm_back(normed1, scale1, gain1, grad_first)
    residual[...] = grad_residual
    grad_branch = grad_residual.astype(BF16)
    gb_out[...] = grad_branch
    ga_mine[...] = dot_right(grad_branch, wo_mine).astype(BF16)
    ga_theirs[...] = dot_right(grad_branch, wo_theirs).astype(BF16)
    sums[0:1, :] += column_sum(grad_branch)
    sums[1:2, :] += column_sum(grad_reduced)
    sums[2:3, :] += column_sum(grad_first * normed1)
    sums[3:4, :] += column_sum(grad_first)
    sums[4:5, :] += column_sum(incoming * normed2)
    sums[5:6, :] += column_sum(incoming)


def row_local(core, x, mine, theirs, cot, square, wide_all, vectors, be):
    rows, width = x.shape
    half, wide = width // 2, be.shape[1]
    side = lambda flip: pl.BlockSpec(
        (UNITS // 2, width // UNITS, width),
        lambda i, core: (core[0] ^ flip, 3, 0),
        pipeline_mode=pl.Buffered(1),
    )
    block = lambda cols: pl.BlockSpec((ROWS, cols), lambda i, *_: (i, 0))
    fixed = lambda a: pl.BlockSpec(
        a.shape, lambda i, *_: (0,) * a.ndim, pipeline_mode=pl.Buffered(1)
    )
    shape = lambda cols, kind: jax.ShapeDtypeStruct((rows, cols), kind)
    resident = lambda r, cols: pl.BlockSpec((r, cols), lambda i, *_: (0, 0))
    return pl.pallas_call(
        rows_kernel,
        out_shape=[
            shape(width, BF16),
            shape(half, BF16),
            shape(half, BF16),
            shape(width, F32),
            shape(wide, BF16),
            shape(wide, BF16),
            shape(width, BF16),
            shape(width, BF16),
            shape(width, BF16),
            jax.ShapeDtypeStruct((8, width), F32),
            jax.ShapeDtypeStruct((1, wide), F32),
        ],
        grid_spec=pltpu.PrefetchScalarGridSpec(
            num_scalar_prefetch=1,
            grid=(rows // ROWS,),
            in_specs=[
                block(width),
                block(half),
                block(half),
                block(width),
                side(0),
                side(1),
                fixed(wide_all),
                fixed(vectors),
                fixed(be),
            ],
            out_specs=[
                block(width),
                block(half),
                block(half),
                block(width),
                block(wide),
                block(wide),
                block(width),
                block(width),
                block(width),
                resident(8, width),
                resident(1, wide),
            ],
            scratch_shapes=[pltpu.VMEM((ROWS, wide), F32)],
        ),
        compiler_params=params(),
        cost_estimate=pl.CostEstimate(
            flops=2 * 2 * rows * width * (width + 2 * wide),
            bytes_accessed=40 << 20,
            transcendentals=rows * wide,
        ),
        name="row_local",
    )(core, x, mine, theirs, cot, square, square, wide_all, vectors, be)


def weight_grad_kernel(left, right, out):
    out[...] = dot_left(left[...], right[...]).astype(out.dtype)


def weight_grad(left, right, kind):
    rows, m = left.shape
    n = right.shape[1]
    tm, tn = min(m, 768), min(n, 768)
    return pl.pallas_call(
        weight_grad_kernel,
        out_shape=jax.ShapeDtypeStruct((m, n), kind),
        grid=(m // tm, n // tn),
        in_specs=[
            pl.BlockSpec((rows, tm), lambda i, j: (0, i)),
            pl.BlockSpec((rows, tn), lambda i, j: (0, j)),
        ],
        out_specs=pl.BlockSpec((tm, tn), lambda i, j: (i, j)),
        compiler_params=params(),
        cost_estimate=pl.CostEstimate(
            flops=2 * rows * m * n, bytes_accessed=16 << 20, transcendentals=0
        ),
        name="weight_grad",
    )(left, right)


def split_cores(core, both, axis):
    first, second = jnp.split(both, 2, axis=axis)
    keep = jnp.where(core == 0, first, second)
    send = jnp.where(core == 0, second, first)
    return keep.astype(BF16), send.astype(BF16)


def feed_kernel(
    low, ge, act, gr, mine, theirs, gb, part0, part1, part2, part3,
    left, wide_left, wide_right, right, narrow, keep, send, got, keep_o, send_o, got_o,
    loads, core_s, core_r,
):
    r, s = lax.axis_index("rep"), lax.axis_index("shard")
    core = s % 2
    twin = (r, s ^ 1)
    rows, width = low.shape
    chunks = wide_left.shape[0]
    nz, unit, quarter = keep.shape[1], keep.shape[2] // 2, keep_o.shape[2]
    half = width // 2
    load = lambda source, target, n: pltpu.make_async_copy(source, target, loads.at[n])
    chunk = lambda ref, u: ref.at[:, pl.ds(pl.multiple_of(u * width, width), width)]
    act_load = lambda u: load(chunk(act, u), wide_left.at[u], u)
    ge_load = lambda u: load(chunk(ge, u), wide_right.at[u], chunks + u)
    others = [
        load(gr, right.at[0], 2 * chunks),
        load(low, left, 2 * chunks + 1),
        load(mine, narrow.at[0], 2 * chunks + 2),
        load(theirs, narrow.at[1], 2 * chunks + 3),
        load(gb, right.at[1], 2 * chunks + 4),
    ]
    others[0].start()
    for u in range(chunks):
        act_load(u).start()
    others[1].start()
    for u in range(chunks):
        ge_load(u).start()
    for c in others[2:]:
        c.start()
    barrier = pltpu.get_barrier_semaphore()
    pl.semaphore_signal(barrier, 1, device_id=twin, device_id_type=pl.DeviceIdType.MESH)
    pl.semaphore_wait(barrier, 1)

    def swap(source, target, n):
        return pltpu.make_async_remote_copy(
            source,
            target,
            core_s.at[n],
            core_r.at[n],
            device_id=twin,
            device_id_type=pl.DeviceIdType.MESH,
        )

    lower, upper = pl.ds(0, unit), pl.ds(unit, unit)
    reduce_swap = lambda u: swap(send.at[:, u, upper], got.at[:, u, upper], u)
    expand_swap = lambda u: swap(send.at[u, :, lower], got.at[u, :, lower], chunks + u)
    output_swap = swap(send_o, got_o, 2 * chunks)
    others[0].wait()

    def reduce_step(u, carry):
        act_load(u).wait()
        whole = dot_left(wide_left[u], right[0]).reshape(2, 4, unit, width)
        kept, sent = split_cores(core, whole, 0)
        for part in range(4):
            keep[part, u, upper] = kept[0, part]
            send[part, u, upper] = sent[0, part]
        reduce_swap(u).start()
        return carry

    lax.fori_loop(0, chunks, reduce_step, 0)
    others[1].wait()

    def expand_step(u, carry):
        ge_load(u).wait()
        whole = dot_left(left[...], wide_right[u]).reshape(nz, 2, unit, width)
        kept, sent = split_cores(core, whole, 1)
        for n in range(nz):
            keep[u, n, lower] = kept[n, 0]
            send[u, n, lower] = sent[n, 0]
        expand_swap(u).start()
        return carry

    lax.fori_loop(0, chunks, expand_step, 0)
    for c in others[2:]:
        c.wait()
    from_mine, from_theirs = dot_left(narrow[0], right[1]), dot_left(narrow[1], right[1])
    first = jnp.where(core == 0, from_mine, from_theirs)
    second = jnp.where(core == 0, from_theirs, from_mine)
    whole = jnp.concatenate([first, second]).reshape(nz, 2, 4, quarter, width)
    kept, sent = split_cores(core, whole, 1)
    for part in range(4):
        keep_o[part] = kept[:, 0, part]
        send_o[part] = sent[:, 0, part]
    output_swap.start()
    for u in range(chunks):
        reduce_swap(u).wait_recv()
        expand_swap(u).wait_recv()
    for k, out in enumerate((part0, part1, part2, part3)):
        part = r ^ k
        for n in range(nz):
            total = keep[part, n].astype(F32) + got[part, n].astype(F32)
            out[n, : 2 * unit, :] = total.astype(BF16)
    output_swap.wait_recv()
    for k, out in enumerate((part0, part1, part2, part3)):
        part = r ^ k
        total = keep_o[part].astype(F32) + got_o[part].astype(F32)
        out[:, 2 * unit :, :] = total.astype(BF16)
    for u in range(chunks):
        reduce_swap(u).wait_send()
        expand_swap(u).wait_send()
    output_swap.wait_send()


def feed_grads(low, ge, act, gr, mine, theirs, gb):
    rows, width = low.shape
    wide = ge.shape[1]
    chunks = wide // width
    unit = width // UNITS
    quarter = unit // 4
    nz = UNITS // 2
    vmem = lambda *shape: pltpu.VMEM(shape, BF16)
    sems = lambda *shape: pltpu.SemaphoreType.DMA(shape)
    return pl.pallas_call(
        feed_kernel,
        out_shape=[jax.ShapeDtypeStruct((nz, 2 * unit + quarter, width), BF16)] * 4,
        in_specs=[pl.BlockSpec(memory_space=pl.ANY)] * 7,
        out_specs=[pl.BlockSpec(memory_space=pltpu.VMEM)] * 4,
        scratch_shapes=[
            vmem(rows, width),
            vmem(chunks, rows, width),
            vmem(chunks, rows, width),
            vmem(2, rows, width),
            vmem(2, rows, width // 2),
            vmem(4, nz, 2 * unit, width),
            vmem(4, nz, 2 * unit, width),
            vmem(4, nz, 2 * unit, width),
            vmem(4, nz, quarter, width),
            vmem(4, nz, quarter, width),
            vmem(4, nz, quarter, width),
            sems(2 * chunks + 5),
            sems(2 * chunks + 1),
            sems(2 * chunks + 1),
        ],
        compiler_params=params(collective_id=2, has_side_effects=True),
        cost_estimate=pl.CostEstimate(
            flops=2 * rows * width * (2 * wide + width), bytes_accessed=25 << 20, transcendentals=0
        ),
        name="feed_grads",
    )(low, ge, act, gr, mine, theirs, gb)


def finish_kernel(
    own, other, dq, dk, dv, square, residual, feed0, feed1, feed2, feed3, small_keep, small_send,
    dx_out, qkv_out, feed_out, small_out,
    x, d, w, res, keep, send, twin_part, plane_got, plane_part, line_part, line_got, around,
    feed_in, feed_line, feed_got, feed_around, to_twin, from_twin, ready,
    small_got, small_plane, small_line,
    loads, feed_loads, stores, core_s, core_r, dx_s, dx_r, move_s, move_r, moved, plane_s, plane_r, line_s, line_r,
    ring_s, ring_r, feed_s, feed_r, small_s, small_r,
):
    r, s = lax.axis_index("rep"), lax.axis_index("shard")
    z, core = s // 2, s % 2
    half = dq.shape[1]
    rows = own.shape[0]
    block = rows // 2
    unit = w.shape[1]
    quarter = unit // 4
    nz, feed_rows = feed0.shape[:2]
    odd = r % 2
    home = r // 2 == core
    twin = (r, s ^ 1)
    plane = lambda k: (r ^ k, s)
    line = lambda k: (r, s ^ (2 * k))
    barrier = pltpu.get_barrier_semaphore()
    mesh_id = pl.DeviceIdType.MESH
    friends = [twin, (r ^ 2, s ^ 1), (r ^ 3, s ^ 1)] + [plane(k) for k in (1, 2, 3)]
    friends += [line(k) for k in range(1, nz)]
    for device in friends:
        pl.semaphore_signal(barrier, 1, device_id=device, device_id_type=mesh_id)
    pl.semaphore_wait(barrier, len(friends))

    def copy(source, target, sent, got, device):
        return pltpu.make_async_remote_copy(
            source, target, sent, got, device_id=device, device_id_type=mesh_id
        )

    mine, theirs = rows_at(core, rows), rows_at(1 - core, rows)
    local = [
        pltpu.make_async_copy(own, x.at[mine], loads.at[0]),
        pltpu.make_async_copy(other, x.at[theirs], loads.at[1]),
    ]
    for m, source in enumerate((dq, dk, dv)):
        local.append(
            pltpu.make_async_copy(source, d.at[:, pl.ds(m * half, half)], loads.at[2 + m])
        )
    late = [pltpu.make_async_copy(residual, res, loads.at[5])] + [
        pltpu.make_async_copy(
            square.at[:, pl.ds(m * unit, unit), pl.ds(pl.multiple_of(core * half, half), half)],
            w.at[:, :, pl.ds(m * half, half)],
            loads.at[6 + m],
        )
        for m in range(3)
    ]
    feeds = [
        pltpu.make_async_copy(source, feed_in.at[k], feed_loads.at[k])
        for k, source in enumerate((feed0, feed1, feed2, feed3))
    ]
    for c in local + feeds + late:
        c.start()
    small_core = copy(small_send, small_got, small_s.at[0], small_r.at[0], twin)
    small_core.start()
    for c in local:
        c.wait()

    def cross(i):
        return copy(send.at[i], twin_part.at[i], core_s.at[i], core_r.at[i], twin)

    def spread(i, side, stage):
        source = keep if side == 0 else twin_part
        near, far = (1, 2) if side == 0 else (2, 1)
        part = (source.at[i, r ^ near], source.at[i, r ^ 3], plane_part.at[i, side])[stage]
        return copy(
            part,
            plane_got.at[stage, i, side],
            plane_s.at[stage, i, side],
            plane_r.at[stage, i, side],
            plane(far if stage == 2 else near),
        )

    def pass_on(side):
        source = keep if side == 0 else twin_part
        far = 2 if side == 0 else 1
        for i in (0, 1):
            spread(i, side, 1).wait_recv()
            total = source[i, r ^ far].astype(F32) + plane_got[1, i, side].astype(F32)
            plane_part[i, side] = total.astype(BF16)
            spread(i, side, 2).start()

    for i in (0, 1):
        whole = dot_left(x[:, i * half : (i + 1) * half], d[...])
        kept, sent = split_cores(core, whole.reshape(nz // 2, 2, 4, quarter, 3 * half), 1)
        for part in range(4):
            keep[i, part] = kept[:, 0, part]
            send[i, part] = sent[:, 0, part]
        cross(i).start()
        for stage in (1, 0):
            spread(i, 0, stage).start()
    for c in feeds:
        c.wait()
    feed_hops = [
        copy(feed_line.at[z ^ k], feed_got.at[k - 1], feed_s.at[k - 1], feed_r.at[k - 1], line(k))
        for k in range(1, nz)
    ]
    for k in range(nz - 1, -1, -1):
        at = z ^ k
        total = feed_in[0, at].astype(F32)
        for n in (1, 2, 3):
            total = total + feed_in[n, at].astype(F32)
        feed_line[at] = total.astype(BF16)
        if k > 0:
            feed_hops[k - 1].start()
    for i in (0, 1):
        cross(i).wait_recv()
        for stage in (1, 0):
            spread(i, 1, stage).start()

    def share(at):
        return dot_right(d[at, :], w[...].reshape(-1, 3 * half))

    def give(t):
        return copy(to_twin.at[t], from_twin.at[t], dx_s.at[t], dx_r.at[t], twin)

    def away(t, carry):
        at = pl.ds(pl.multiple_of((1 - core) * rows + t * block, block), block)
        to_twin[t] = share(at).astype(BF16)
        give(t).start()
        return carry

    for c in late:
        c.wait()
    lax.fori_loop(0, 2, away, 0)

    def stay(turn):
        return pltpu.make_async_copy(ready.at[odd ^ turn], dx_out.at[odd], moved.at[turn])

    def leave(turn, device):
        return copy(ready.at[odd ^ turn], dx_out.at[odd], move_s.at[turn], move_r.at[turn], device)

    for turn in (0, 1):
        t = odd ^ turn
        at = pl.ds(pl.multiple_of(core * rows + t * block, block), block)
        total = share(at) + res[rows_at(t, block), :]
        give(t).wait_recv()
        ready[t] = (total + from_twin[t].astype(F32)).astype(BF16)
        if turn == 0:

            @pl.when(home)
            def _():
                stay(0).start()

            @pl.when(jnp.logical_not(home))
            def _():
                leave(0, (r ^ 2, s ^ 1)).start()

        else:

            @pl.when(home)
            def _():
                leave(1, (r ^ 1, s)).start()

            @pl.when(jnp.logical_not(home))
            def _():
                leave(1, (r ^ 3, s ^ 1)).start()

    pass_on(0)
    pass_on(1)
    for i in (0, 1):
        for side in (0, 1):
            source = keep if side == 0 else twin_part
            total = source[i, r].astype(F32)
            for stage in (0, 2):
                spread(i, side, stage).wait_recv()
                total = total + plane_got[stage, i, side].astype(F32)
            for n in range(nz // 2):
                line_part[i * (nz // 2) + n, side] = total[n].astype(BF16)
    qkv_line = [
        copy(line_part.at[z ^ k], line_got.at[k - 1], line_s.at[k - 1], line_r.at[k - 1], line(k))
        for k in range(1, nz)
    ]
    for c in qkv_line:
        c.start()
    small_core.wait()
    small_mine = small_keep[...] + small_got[...]
    small_got[...] = small_mine
    small_around = [
        copy(small_got, small_plane.at[k - 1], small_s.at[k], small_r.at[k], plane(k))
        for k in (1, 2, 3)
    ]
    for c in small_around:
        c.start()
    total = feed_line[z].astype(F32)
    for n, c in enumerate(feed_hops):
        c.wait_recv()
        total = total + feed_got[n].astype(F32)
    feed_around[...] = total.astype(BF16)

    def ring(own_part, out, sent, got, number, pieces):
        copies = []
        for n, piece in enumerate(pieces):
            near, far = (1, 2) if n == 0 else (2, 1)
            here, there = own_part.at[piece], out.at[(r,) + piece]
            passed = out.at[(r ^ near,) + piece]
            at = lambda stage: (sent.at[number, n, stage], got.at[number, n, stage])
            copies.append(
                [
                    copy(here, there, *at(0), plane(near)),
                    copy(here, there, *at(1), plane(far)),
                    copy(passed, passed, *at(2), plane(far)),
                ]
            )
        return copies

    def set_out(copies):
        for one in copies:
            one[0].start()
            one[1].start()

    def relay(copies):
        for one in copies:
            one[0].wait_recv()
            one[2].start()

    cut = (feed_rows // 2 + 15) // 16 * 16
    feed_ring = ring(
        feed_around, feed_out, ring_s, ring_r, 0, [(pl.ds(0, cut),), (pl.ds(cut, feed_rows - cut),)]
    )
    qkv_ring = ring(around, qkv_out, ring_s, ring_r, 1, [(0,), (1,)])
    kept = [
        pltpu.make_async_copy(feed_around, feed_out.at[r], stores.at[0]),
        pltpu.make_async_copy(around, qkv_out.at[r], stores.at[1]),
    ]
    set_out(feed_ring)
    kept[0].start()
    small_total = small_mine
    for n, c in enumerate(small_around):
        c.wait()
        small_total = small_total + small_plane[n]
    small_got[...] = small_total
    small_along = [
        copy(small_got.at[z ^ k], small_line.at[k - 1], small_s.at[3 + k], small_r.at[3 + k], line(k))
        for k in range(1, nz)
    ]
    for c in small_along:
        c.start()
    relay(feed_ring)
    total = line_part[z].astype(F32)
    for n, c in enumerate(qkv_line):
        c.wait_recv()
        total = total + line_got[n].astype(F32)
    around[core] = total[0].astype(BF16)
    around[1 - core] = total[1].astype(BF16)
    set_out(qkv_ring)
    kept[1].start()
    total = small_got[z]
    for n, c in enumerate(small_along):
        c.wait()
        total = total + small_line[n]
    small_out[...] = total
    relay(qkv_ring)
    for c in kept:
        c.wait()
    for one in feed_ring + qkv_ring:
        one[0].wait_send()
        one[1].wait()
        one[2].wait()

    @pl.when(home)
    def _():
        stay(0).wait()
        leave(1, (r ^ 1, s)).wait()

    @pl.when(jnp.logical_not(home))
    def _():
        leave(0, (r ^ 2, s ^ 1)).wait()
        leave(1, (r ^ 3, s ^ 1)).wait()

    for c in feed_hops + qkv_line:
        c.wait_send()
    for i in (0, 1):
        cross(i).wait_send()
        for side in (0, 1):
            for stage in range(3):
                spread(i, side, stage).wait_send()
    for t in (0, 1):
        give(t).wait_send()


def finish(own, other, dq, dk, dv, square, residual, feeds, small_keep, small_send):
    rows, width = own.shape
    half = width // 2
    nz, feed_rows = feeds[0].shape[:2]
    unit = width // UNITS
    block = rows // 2
    anywhere = pl.BlockSpec(memory_space=pl.ANY)
    vmem = pl.BlockSpec(memory_space=pltpu.VMEM)
    sems = lambda *shape: pltpu.SemaphoreType.DMA(shape)
    low = lambda *shape: pltpu.VMEM(shape, BF16)
    high = lambda *shape: pltpu.VMEM(shape, F32)
    part = (unit // 4, 3 * half)
    twos = nz // 2
    return pl.pallas_call(
        finish_kernel,
        out_shape=[
            jax.ShapeDtypeStruct((2, block, width), BF16),
            jax.ShapeDtypeStruct((4, 2) + part, BF16),
            jax.ShapeDtypeStruct((4, feed_rows, width), BF16),
            jax.ShapeDtypeStruct(small_keep.shape[1:], F32),
        ],
        in_specs=[anywhere] * 11 + [vmem] * 2,
        out_specs=[anywhere] * 3 + [vmem],
        scratch_shapes=[
            low(2 * rows, width),
            low(2 * rows, 3 * half),
            low(UNITS, unit, 3 * half),
            high(rows, width),
            low(2, 4, twos, *part),
            low(2, 4, twos, *part),
            low(2, 4, twos, *part),
            low(3, 2, 2, twos, *part),
            low(2, 2, twos, *part),
            low(nz, 2, *part),
            low(nz - 1, 2, *part),
            low(2, *part),
            low(4, nz, feed_rows, width),
            low(nz, feed_rows, width),
            low(nz - 1, feed_rows, width),
            low(feed_rows, width),
            low(2, block, width),
            low(2, block, width),
            low(2, block, width),
            high(*small_keep.shape),
            high(3, *small_keep.shape),
            high(nz - 1, *small_keep.shape[1:]),
            sems(9),
            sems(4),
            sems(2),
            sems(2),
            sems(2),
            sems(2),
            sems(2),
            sems(2),
            sems(2),
            sems(2),
            sems(3, 2, 2),
            sems(3, 2, 2),
            sems(nz - 1),
            sems(nz - 1),
            sems(2, 2, 3),
            sems(2, 2, 3),
            sems(nz - 1),
            sems(nz - 1),
            sems(3 + nz),
            sems(3 + nz),
        ],
        compiler_params=params(collective_id=1, has_side_effects=True),
        cost_estimate=pl.CostEstimate(
            flops=2 * 2 * 2 * rows * width * 3 * half, bytes_accessed=150 << 20, transcendentals=0
        ),
        name="finish",
    )(own, other, dq, dk, dv, square, residual, *feeds, small_keep, small_send)


def input_grad_kernel(core, own, other, d_ref, w_ref, dw, sums, dx_own, dx_other):
    part = pl.program_id(0)
    rows = own.shape[0]
    mine = pl.multiple_of(core[0] * rows, rows)
    theirs = pl.multiple_of((1 - core[0]) * rows, rows)
    d_own, d_other = d_ref[0, pl.ds(mine, rows), :], d_ref[0, pl.ds(theirs, rows), :]
    dw[0] = (dot_left(own[...], d_own) + dot_left(other[...], d_other)).astype(dw.dtype)
    sums[0] = jnp.broadcast_to(column_sum(d_own) + column_sum(d_other), sums.shape[1:])
    to_own, to_other = dot_right(d_own, stacked(w_ref)), dot_right(d_other, stacked(w_ref))

    @pl.when(part == 0)
    def _():
        dx_own[...] = to_own
        dx_other[...] = to_other

    @pl.when(part > 0)
    def _():
        dx_own[...] += to_own
        dx_other[...] += to_other


def input_grad(core, own, other, grads, weights, kind):
    rows, width = own.shape
    half = width // 2
    whole = lambda shape: pl.BlockSpec(shape, lambda i, *_: (0,) * len(shape))
    return pl.pallas_call(
        input_grad_kernel,
        out_shape=[
            jax.ShapeDtypeStruct((3, width, half), kind),
            jax.ShapeDtypeStruct((3, 8, half), F32),
            jax.ShapeDtypeStruct((rows, width), F32),
            jax.ShapeDtypeStruct((rows, width), F32),
        ],
        grid_spec=pltpu.PrefetchScalarGridSpec(
            num_scalar_prefetch=1,
            grid=(3,),
            in_specs=[
                whole((rows, width)),
                whole((rows, width)),
                pl.BlockSpec((1, 2 * rows, half), lambda i, core: (i, 0, 0)),
                pl.BlockSpec((UNITS, width // UNITS, half), lambda i, core: (0, i, core[0])),
            ],
            out_specs=[
                pl.BlockSpec((1, width, half), lambda i, core: (i, 0, 0)),
                pl.BlockSpec((1, 8, half), lambda i, core: (i, 0, 0)),
                whole((rows, width)),
                whole((rows, width)),
            ],
        ),
        compiler_params=params(),
        cost_estimate=pl.CostEstimate(
            flops=2 * 2 * 2 * rows * width * 3 * half, bytes_accessed=20 << 20, transcendentals=0
        ),
        name="input_grad",
    )(core, own, other, grads, weights)


def unpack_kernel(feed, qkv, dq, dk, dv, do, de, dr):
    unit, width = dq.shape
    quarter, half = unit // 4, width // 2
    for part in range(4):
        de[:, part * width : (part + 1) * width] = feed[part, :unit, :].astype(F32)
        dr[part * unit : (part + 1) * unit, :] = feed[part, unit : 2 * unit, :].astype(F32)
        rows = slice(part * quarter, (part + 1) * quarter)
        do[rows, :] = feed[part, 2 * unit :, :].astype(F32)
        for m, out in enumerate((dq, dk, dv)):
            for side in (0, 1):
                columns = qkv[part, side, :, m * half : (m + 1) * half]
                out[rows, side * half : (side + 1) * half] = columns.astype(F32)


def unpack(feed, qkv, unit, width):
    shape = lambda *dims: jax.ShapeDtypeStruct(dims, F32)
    return pl.pallas_call(
        unpack_kernel,
        out_shape=[shape(unit, width)] * 4 + [shape(unit, 4 * width), shape(4 * unit, width)],
        in_specs=[pl.BlockSpec(memory_space=pltpu.VMEM)] * 2,
        out_specs=[pl.BlockSpec(memory_space=pltpu.VMEM)] * 6,
        compiler_params=params(),
        name="unpack",
    )(feed, qkv)


def local(tokens, segment_ids, cotangent, *shards):
    rep_size, shard_size = lax.axis_size("rep"), lax.axis_size("shard")
    rep, shard = lax.axis_index("rep"), lax.axis_index("shard")
    core = shard % 2
    core_arg = core.reshape(1).astype(jnp.int32)
    width = tokens.shape[2]
    half = width // 2
    both = ("rep", "shard")

    def flat(r, s):
        return r * shard_size + s

    def route(k, back=False):
        pairs = []
        for r in range(rep_size):
            for s in range(shard_size):
                there = (flat(r, s), flat(2 * (s % 2) + (r + k) % 2, s - s % 2 + r // 2))
                pairs.append(there[::-1] if back else there)
        return pairs

    swap_pairs = [(flat(r, s), flat(r, s ^ 1)) for r in range(rep_size) for s in range(shard_size)]

    def swap(array):
        return lax.ppermute(array, both, swap_pairs)

    odd = rep % 2

    def to_sequences(array):
        a, b = array[0], array[1]
        even_part = lax.ppermute(jnp.where(odd == 0, a, b), both, route(0))
        odd_part = lax.ppermute(jnp.where(odd == 0, b, a), both, route(1))
        return jnp.concatenate(
            [jnp.where(odd == 0, even_part, odd_part), jnp.where(odd == 0, odd_part, even_part)]
        )

    def from_sequences(array):
        rows = array.shape[0] // 2
        a, b = array[:rows], array[rows:]
        even_part = lax.ppermute(jnp.where(odd == 0, a, b), both, route(0, True))
        odd_part = lax.ppermute(jnp.where(odd == 0, b, a), both, route(1, True))
        return jnp.stack(
            [jnp.where(odd == 0, even_part, odd_part), jnp.where(odd == 0, odd_part, even_part)]
        )

    tuned = rep_size == 4 and shard_size == UNITS
    unit = width // UNITS
    chunks = shards[4].shape[1] // width
    short = jnp.stack(shards[6:9] + shards[10:])
    small = jnp.pad(short, ((0, 0), (0, width - short.shape[1])))
    small = small + jnp.pad(shards[9][None], ((0, EXTRA - 1), (half, half - shards[9].shape[0])))
    if tuned:
        square, wide_all, own, other, cot, segments = gather(
            shards[:6], small, tokens, cotangent, segment_ids.reshape(2, -1, 128), shard_size // 2
        )
        segments = segments.reshape(-1)
        small = square[:, 4 * unit :, :]
    else:
        wq, wk, wv, wo, we, wr = [lax.all_gather(m, "shard", axis=0, tiled=True) for m in shards[:6]]
        square = jnp.concatenate(
            [m.reshape(UNITS, unit, width) for m in (wq, wk, wv, wo)]
            + [jnp.zeros((UNITS, EXTRA, width), BF16)],
            axis=1,
        )
        wide_all = jnp.concatenate(
            [
                we.reshape(UNITS, unit, chunks, width).transpose(0, 2, 1, 3),
                wr.reshape(UNITS, chunks, unit, width),
            ],
            axis=2,
        )
        small = lax.all_gather(small[None], "shard", axis=0, tiled=True)
        own = to_sequences(tokens)
        cot = to_sequences(cotangent)
        other = swap(own)
        swapped_ids = swap(segment_ids)
        ids = jnp.where(rep // 2 == core, segment_ids, swapped_ids)
        segments = lax.dynamic_index_in_dim(ids, odd, 0, keepdims=False)
    each = width // shard_size
    table = small[:, :, :each].transpose(1, 0, 2).reshape(8, width).astype(F32)
    be = small[:, 0, half : half + shards[9].shape[0]].reshape(1, -1).astype(F32)

    blocks = segments.reshape(-1, BLOCK)
    begin = jnp.sum((segments[None, :] < blocks[:, :1]).astype(jnp.int32), axis=1)
    end = jnp.sum((segments[None, :] <= blocks[:, -1:]).astype(jnp.int32), axis=1)
    segments = segments[None, :]

    q, k, v = project(core_arg, own, other, square, table)
    attended, lse = attend(begin, end, q, k, v, segments)
    rows = own.shape[0]
    mine = lax.dynamic_slice_in_dim(attended, core * rows, rows)
    theirs = swap(lax.dynamic_slice_in_dim(attended, (1 - core) * rows, rows))
    out, ga_mine, ga_theirs, residual, act, ge, first_low, gr, gb, sums, sum_e = row_local(
        core_arg, own, mine, theirs, cot, square, wide_all, table, be
    )
    ga_other = swap(ga_theirs)
    if not tuned:
        dwr = weight_grad(act, gr, F32)
        dwe = weight_grad(first_low, ge, F32)
        dwo_mine, dwo_theirs = weight_grad(mine, gb, F32), weight_grad(theirs, gb, F32)
        dq, dk, dv, sum_qv = attend_back(
            core_arg, begin, end, q, k, v, attended, ga_mine, ga_other, lse, segments
        )
        dw, sum_qkv, dx_own, dx_other = input_grad(
            core_arg, own, other, jnp.stack([dq, dk, dv]), square, F32
        )
        dx = (residual + dx_own + swap(dx_other.astype(BF16)).astype(F32)).astype(BF16)

        def place(part, dim):
            zero = jnp.zeros_like(part)
            return jnp.where(
                core == 0,
                jnp.concatenate([part, zero], axis=dim),
                jnp.concatenate([zero, part], axis=dim),
            )

        dwo = jnp.where(
            core == 0,
            jnp.concatenate([dwo_mine, dwo_theirs]),
            jnp.concatenate([dwo_theirs, dwo_mine]),
        )
        totals = (
            place(dw[0], 1),
            place(dw[1], 1),
            place(dw[2], 1),
            dwo,
            dwe,
            dwr,
            place(sum_qkv[0, 0], 0),
            place(sum_qkv[2, 0], 0),
            sums[0],
            sum_e[0],
            sums[1],
            sums[2],
            sums[3],
            sums[4],
            sums[5],
        )
        summed = lax.psum_scatter(totals, "shard", scatter_dimension=0, tiled=True)
        final = [part.astype(F32) for part in lax.psum([p.astype(BF16) for p in summed], "rep")]
        return (from_sequences(out), from_sequences(dx)) + tuple(final)

    nz = shard_size // 2

    def plane_send(array, hop):
        pairs = [(flat(r, s), flat(r ^ hop, s)) for r in range(4) for s in range(shard_size)]
        return lax.ppermute(array, both, pairs)

    feeds = feed_grads(first_low, ge, act, gr, mine, theirs, gb)
    feeds, ga_other = lax.optimization_barrier((feeds, ga_other))
    feeds = [feeds[0]] + [plane_send(feeds[hop], hop) for hop in (1, 2, 3)]
    dq, dk, dv, sum_qv = attend_back(
        core_arg, begin, end, q, k, v, attended, ga_mine, ga_other, lse, segments
    )
    wide_unit = sum_e.shape[1] // shard_size

    def place(part):
        zero = jnp.zeros_like(part)
        return jnp.where(
            core == 0, jnp.concatenate([part, zero]), jnp.concatenate([zero, part])
        )

    rows_of = [place(sum_qv[0, 0]), place(sum_qv[1, 0])] + [sums[n] for n in range(6)]
    table = jnp.concatenate(
        [vector.reshape(shard_size, unit) for vector in rows_of]
        + [
            sum_e.reshape(shard_size, wide_unit),
            jnp.zeros((shard_size, 8 * 256 - 8 * unit - wide_unit), F32),
        ],
        axis=1,
    ).reshape(nz, 2, 8, 256)
    small_keep = lax.dynamic_index_in_dim(table, core, 1, keepdims=False)
    small_send = lax.dynamic_index_in_dim(table, 1 - core, 1, keepdims=False)
    dx, dqkv, feed, small = finish(
        own, other, dq, dk, dv, square, residual, feeds, small_keep, small_send
    )
    dwq, dwk, dwv, dwo, dwe, dwr = unpack(feed, dqkv, unit, width)
    small = small.reshape(-1)
    dbq, dbv, dbo, dbr, dg1, ds1, dg2, ds2 = [small[n * unit : (n + 1) * unit] for n in range(8)]
    dbe = small[8 * unit : 8 * unit + wide_unit]
    return (
        from_sequences(out),
        dx,
        dwq,
        dwk,
        dwv,
        dwo,
        dwe,
        dwr,
        dbq,
        dbv,
        dbo,
        dbe,
        dbr,
        dg1,
        ds1,
        dg2,
        ds2,
    )


def solution(mesh):
    row = P("shard", "rep", None)
    in_specs = (row, P("shard", None), row) + (P("shard", None),) * 6 + (P("shard"),) * 9
    out_specs = (row, row) + (P("shard", None),) * 6 + (P("shard"),) * 9
    return jax.shard_map(local, mesh=mesh, in_specs=in_specs, out_specs=out_specs, check_vma=False)
```
